256 devices in a mesh: seq: 16 (over y, x_hi, core), head: 16 (over x_lo, z).
Axes of the slice: x: 4 (x_hi: 2, x_lo: 2; x = x_hi * 2 + x_lo), y: 4, z: 8, core: 2. Of those that a mesh axis runs over, the one named last changes fastest.
Arguments:
- latent_cache: bfloat16 [2, 32768, 576], P(None, 'seq'), may hold values from -8 to 8
- draft_latent: bfloat16 [2, 64, 576], P(None, 'seq'), may hold values from -9 to 9
- query_nope: bfloat16 [2, 64, 128, 128], P(None, None, 'head'), may hold values from -6 to 6
- query_rope: bfloat16 [2, 64, 128, 64], P(None, None, 'head'), may hold values from -8 to 8
- parents: int32 [2, 64], replicated, may hold values from -1 to 62, as said below
- lengths: int32 [2], replicated, may hold values from 16384 to 32768
- key_weight: bfloat16 [128, 128, 512], P('head'), may hold values from -0.25 to 0.25
- value_weight: bfloat16 [128, 512, 128], P('head'), may hold values from -0.25 to 0.25
- out_weight: bfloat16 [16384, 7168], P('head', 'seq'), may hold values from -0.046875 to 0.046875
- residual: bfloat16 [2, 64, 7168], P(None, None, 'seq'), may hold values from -40 to 40
- norm_gain: bfloat16 [7168], P('seq'), may hold values from 0.5 to 1.5
- vocab_weight: bfloat16 [7168, 65536], P('seq', 'head'), may hold values from -0.21875 to 0.21875
Outputs:
- logits: bfloat16 [2, 64, 65536], P(None, None, ('head', 'seq'))
The draws below stay inside these ranges and needn't reach their ends.
Inputs may be any that keep to these rules, and one draw needn't show every extreme that they name: `parents`: token 0 is the root of each tree with parent -1; every other token's parent is an earlier token; the last token's parent is the token just before it.
All inputs are finite; a program needn't handle non-finite values.
Results may differ from the reference program's by a relative error of at most 0.02.
Values may be sent and summed in bfloat16 or wider, within the bound.
A program may use at most 64 MiB of HBM per device.

```python
import math
import jax
import jax.numpy as jnp
from jax import lax

HEADS = 128
NOPE = 128
ROPE = 64
LAT = 512
VH = 128
D = 7168
REQUESTS = 2
DRAFT = 64
CTX = 32768
VOCAB = 65536


def draw_latent_cache(key, part):
    baseline = jnp.clip(jax.random.normal(jax.random.fold_in(key, 1), (REQUESTS, CTX, LAT + ROPE)), -6.0, 6.0)
    return baseline.astype(jnp.bfloat16)


def draw_query_rope(key, part):
    baseline = jnp.clip(jax.random.normal(jax.random.fold_in(key, 2), (REQUESTS, DRAFT, HEADS, ROPE)), -6.0, 6.0)
    return baseline.astype(jnp.bfloat16)


def draw_parents(key, part):
    indices = jnp.arange(DRAFT, dtype=jnp.int32)
    upper = jnp.maximum(indices, 1)[None, :]
    picked = jax.random.randint(jax.random.fold_in(key, 3), (REQUESTS, DRAFT), 0, upper)
    picked = jnp.where(indices[None, :] == DRAFT - 1, DRAFT - 2, picked)
    return jnp.where(indices[None, :] == 0, -1, picked).astype(jnp.int32)


def draw_residual(key, part):
    key_rows, key_cols, key_noise = jax.random.split(jax.random.fold_in(key, 4), 3)
    row_scale = jnp.exp(jax.random.uniform(key_rows, (REQUESTS, DRAFT, 1), minval=math.log(0.03), maxval=math.log(0.3)))
    rising = 3.0 ** (jnp.arange(D, dtype=jnp.float32) / D)
    col_scale = jnp.exp(jax.random.uniform(key_cols, (D,), minval=math.log(0.5), maxval=math.log(5.0))) * rising
    noise = jnp.clip(jax.random.normal(key_noise, (REQUESTS, DRAFT, D)), -4.0, 4.0)
    return (noise * row_scale * col_scale).astype(jnp.bfloat16)


def block_levels(key, extent, cuts, smallest, top_value):
    factor_of = 1.0
    for dim, blocks in cuts:
        heights = jax.random.uniform(jax.random.fold_in(jax.random.fold_in(key, 6), dim), (blocks,), jnp.float32, smallest / len(cuts), top_value / len(cuts))
        factor_of = factor_of * jnp.repeat(jnp.exp(heights), extent[dim] // blocks).reshape((-1,) + (1,) * (len(extent) - 1 - dim))
    return factor_of


def normal_values(key, extent, scale, limit, cuts=(), kind=jnp.bfloat16):
    result = jax.random.normal(key, extent, jnp.float32) * scale
    if len(cuts) > 0:
        result = block_levels(key, extent, cuts, -0.22, 0.18) * result
    return jnp.clip(result, min=-limit, max=limit).astype(kind)


def setup_inputs(seed: int = 0) -> dict:
    key_list = jax.random.split(jax.random.key(seed), 13)
    latent_cache = draw_latent_cache(jax.random.fold_in(key_list[12], 71), 0)
    draft_latent = normal_values(key_list[1], (REQUESTS, DRAFT, LAT + ROPE), 3.0, 9.0, ((1, 16),))
    query_nope = normal_values(key_list[2], (REQUESTS, DRAFT, HEADS, NOPE), 1.0, 6.0, ((2, 16),))
    query_rope = draw_query_rope(jax.random.fold_in(key_list[12], 71), 0)
    parents = draw_parents(jax.random.fold_in(key_list[12], 71), 0)
    lengths = jax.random.randint(key_list[5], (REQUESTS,), CTX // 2, CTX + 1).astype(jnp.int32)
    key_weight = normal_values(key_list[6], (HEADS, NOPE, LAT), LAT ** -0.5, 0.25, ((0, 16),))
    value_weight = normal_values(key_list[7], (HEADS, LAT, VH), LAT ** -0.5, 0.25, ((0, 16),))
    out_weight = normal_values(key_list[8], (HEADS * VH, D), (HEADS * VH) ** -0.5, 0.046875, ((0, 16), (1, 16)))
    residual = draw_residual(jax.random.fold_in(key_list[12], 71), 0)
    norm_gain = jnp.clip(1.0 + 0.1 * jax.random.normal(key_list[10], (D,), jnp.float32), 0.5, 1.5).astype(jnp.bfloat16)
    vocab_weight = normal_values(key_list[11], (D, VOCAB), (D // 9) ** -0.5, 0.21875, ((0, 16), (1, 16)))
    return dict(latent_cache=latent_cache, draft_latent=draft_latent, query_nope=query_nope, query_rope=query_rope, parents=parents, lengths=lengths, key_weight=key_weight, value_weight=value_weight, out_weight=out_weight, residual=residual, norm_gain=norm_gain, vocab_weight=vocab_weight)


NEGATIVE = -1e+30
EPSILON = 1e-06

def ancestry_of(parents):
    token_count = parents.shape[1]
    indices = jnp.arange(token_count, dtype=jnp.int32)
    linked = (parents[:, :, None] == indices[None, None, :]) | (indices[:, None] == indices[None, :])[None]
    reachable = linked.astype(jnp.float32)
    for repeat in range(max(1, (token_count - 1).bit_length())):
        product = jnp.einsum('bij,bjk->bik', reachable, reachable, precision=lax.Precision.HIGHEST)
        reachable = jnp.where(product > 0.5, 1.0, 0.0).astype(jnp.float32)
    return reachable

def reference(latent_cache, draft_latent, query_nope, query_rope, parents, lengths, key_weight, value_weight, out_weight, residual, norm_gain, vocab_weight):
    scaling = 1.0 / math.sqrt(NOPE + ROPE)
    absorbed = jnp.einsum('bthn,hnl->bthl', query_nope.astype(jnp.float32), key_weight.astype(jnp.float32)).astype(jnp.bfloat16)
    queries = jnp.concatenate([absorbed, query_rope], axis=-1)
    ancestry = ancestry_of(parents)
    live = jnp.arange(CTX, dtype=jnp.int32)[None, :] < lengths[:, None]
    cache_keys = latent_cache.astype(jnp.float32)
    draft_keys = draft_latent.astype(jnp.float32)
    cache_values = cache_keys[:, :, :LAT]
    draft_values = draft_keys[:, :, :LAT]

    def one_head(inputs):
        head_query, head_value = inputs
        query_full = head_query.astype(jnp.float32)
        cache_scores = jnp.einsum('btc,bkc->btk', query_full, cache_keys) * scaling
        cache_scores = jnp.where(live[:, None, :], cache_scores, NEGATIVE)
        draft_scores = jnp.einsum('btc,bkc->btk', query_full, draft_keys) * scaling
        draft_scores = jnp.where(ancestry > 0.5, draft_scores, NEGATIVE)
        largest = jnp.maximum(lax.optimization_barrier(jnp.max(cache_scores, -1)), lax.optimization_barrier(jnp.max(draft_scores, -1)))
        cache_weights = jnp.where(live[:, None, :], jnp.exp(cache_scores - largest[..., None]), 0.0)
        draft_weights = jnp.where(ancestry > 0.5, jnp.exp(draft_scores - largest[..., None]), 0.0)
        total = lax.optimization_barrier(jnp.sum(cache_weights, -1)) + lax.optimization_barrier(jnp.sum(draft_weights, -1))
        mixed = jnp.einsum('btk,bkl->btl', cache_weights.astype(jnp.bfloat16).astype(jnp.float32), cache_values)
        mixed = mixed + jnp.einsum('btk,bkl->btl', draft_weights.astype(jnp.bfloat16).astype(jnp.float32), draft_values)
        latent_out = (mixed / total[..., None]).astype(jnp.bfloat16)
        return jnp.einsum('btl,lv->btv', latent_out.astype(jnp.float32), head_value.astype(jnp.float32)).astype(jnp.bfloat16)
    head_out = lax.map(one_head, (jnp.moveaxis(queries, 2, 0), value_weight))
    head_out = jnp.moveaxis(head_out, 0, 2).reshape(REQUESTS * DRAFT, HEADS * VH)
    attention = jnp.dot(head_out, out_weight, preferred_element_type=jnp.float32).reshape(REQUESTS, DRAFT, D)
    hidden = residual.astype(jnp.float32) + attention
    mean_square = lax.optimization_barrier(jnp.mean(hidden * hidden, -1, keepdims=True))
    normed = (hidden * lax.rsqrt(mean_square + EPSILON) * norm_gain.astype(jnp.float32)).astype(jnp.bfloat16)
    logits = jnp.dot(normed.reshape(REQUESTS * DRAFT, D), vocab_weight, preferred_element_type=jnp.float32)
    return logits.reshape(REQUESTS, DRAFT, VOCAB).astype(jnp.bfloat16)
```

```python
import functools
import math

import jax
import jax.numpy as jnp
from jax import lax
from jax.experimental import pallas as pl
from jax.experimental.pallas import tpu as pltpu
from jax.sharding import PartitionSpec as P

MESH = pl.DeviceIdType.MESH
NEGATIVE = -1e30
EPSILON = 1e-06
F32 = jnp.float32
BF16 = jnp.bfloat16

CHIP_STEPS = [(2, 1), (1, 1), (3, 1), (2, 0), (0, 1), (1, 0), (3, 0)]
SEQ_STEPS = [(dy, dx, dk) for dy, dx in CHIP_STEPS for dk in (0, 1)] + [(0, 0, 1)]
REQUESTS, DRAFT, HEADS, LATENT, ROPE, WIDTH = 2, 64, 8, 512, 64, 576
TOKENS = REQUESTS * DRAFT
KEYS, PADDED = 2048, 2176
BLOCK = 256


def nt_dot(a, b):
    return lax.dot_general(a, b, (((1,), (1,)), ((), ())), preferred_element_type=F32)


def dot(a, b):
    return jnp.dot(a, b, preferred_element_type=F32)


def kernel(
    model_width,
    lengths,
    parents_hbm,
    cache_hbm,
    draft_hbm,
    nope_hbm,
    rope_hbm,
    key_hbm,
    value_hbm,
    out_hbm,
    residual_hbm,
    gain_hbm,
    vocab_hbm,
    logits,
    parents,
    kbuf,
    nope,
    rope,
    key_weight,
    value_weight,
    out_weight,
    residual,
    gain,
    vocab,
    nope32,
    rope32,
    qbuf,
    pbuf,
    o_send,
    o_recv,
    ml_send,
    ml_recv,
    g_send,
    g_full,
    a_send,
    a_recv,
    b_send,
    b_full,
    s_send,
    s_recv,
    p_send,
    p_recv,
    l_send,
    l_recv,
    load_sems,
    vocab_sems,
    local_sems,
    o_sems,
    ml_sems,
    g_sems,
    a_sems,
    b_sems,
    s_sems,
    p_sems,
    l_sems,
):
    seat = lax.axis_index("seq")
    mine = lax.axis_index("head")
    y = lax.div(seat, 4)
    xh = lax.rem(lax.div(seat, 2), 2)
    core = lax.rem(seat, 2)
    chip = lax.div(seat, 2)

    def seat_at(dy, dx, dk):
        return lax.rem(y + dy, 4) * 4 + lax.rem(xh + dx, 2) * 2 + lax.rem(core + dk, 2)

    seq_peers = [seat_at(*step) for step in SEQ_STEPS]
    head_peers = [lax.rem(mine + j, 16) for j in range(1, 16)]

    barrier = pltpu.get_barrier_semaphore()
    for peer in seq_peers:
        pl.semaphore_signal(barrier, inc=1, device_id={"seq": peer}, device_id_type=MESH)
    for peer in head_peers:
        pl.semaphore_signal(barrier, inc=1, device_id={"head": peer}, device_id_type=MESH)

    loads = []

    def load(src, dst):
        copy = pltpu.make_async_copy(src, dst, load_sems.at[len(loads)])
        loads.append(copy)
        copy.start()
        return copy

    got_nope = load(nope_hbm, nope)
    got_rope = load(rope_hbm, rope)
    got_key = load(key_hbm, key_weight)
    got_parents = load(parents_hbm, parents)
    got_draft = [load(draft_hbm, kbuf.at[b, pl.ds(KEYS, 16), :]) for b in range(REQUESTS)]
    got_cache = [load(cache_hbm.at[b], kbuf.at[b, pl.ds(0, KEYS), :]) for b in range(REQUESTS)]
    got_value = load(value_hbm, value_weight)
    got_out = load(out_hbm, out_weight)
    got_residual = load(residual_hbm, residual)
    got_gain = load(gain_hbm, gain)

    vocab_order = []
    for half in (1, 0):
        for dy, dx in CHIP_STEPS + [(0, 0)]:
            vocab_order.append(seat_at(dy, dx, half))
    got_vocab = []
    for slot, owner in enumerate(vocab_order):
        columns = pl.ds(pl.multiple_of(owner * 256, 256), 256)
        copy = pltpu.make_async_copy(
            vocab_hbm.at[:, columns], vocab.at[slot], vocab_sems.at[slot]
        )
        copy.start()
        got_vocab.append(copy)

    for b in range(REQUESTS):
        kbuf[b, KEYS + 16 : PADDED, :] = jnp.zeros((PADDED - KEYS - 16, WIDTH), BF16)
    got_parents.wait()
    row = lax.broadcasted_iota(jnp.int32, (TOKENS, TOKENS), 0)
    column = lax.broadcasted_iota(jnp.int32, (TOKENS, TOKENS), 1)
    parent = parents[...]
    first = jnp.where(lax.broadcasted_iota(jnp.int32, (1, TOKENS), 1) >= DRAFT, DRAFT, 0)
    parent = jnp.where(parent < 0, -1, parent + first)
    reach = jnp.where((parent == row) | (row == column), 1.0, 0.0).astype(BF16)
    for _ in range(6):
        reach = jnp.where(dot(reach, reach) > 0.5, 1.0, 0.0).astype(BF16)
    chosen = jnp.where(
        (column < 8)
        & (row == lax.div(column, 4) * DRAFT + seat * 4 + lax.rem(column, 4)),
        1.0,
        0.0,
    )
    reached = dot(reach.astype(F32).T.astype(BF16), chosen.astype(BF16))
    tree_bias = jnp.where(reached > 0.5, 0.0, NEGATIVE)

    got_nope.wait()
    nope32[...] = nope[...].astype(F32)
    got_rope.wait()
    rope32[...] = rope[...].astype(F32)
    got_key.wait()
    for h in range(HEADS):
        picked = nope32[pl.ds(h, TOKENS, stride=HEADS), :].astype(BF16)
        absorbed = dot(picked, key_weight[h]).astype(BF16)
        turned = rope32[pl.ds(h, TOKENS, stride=HEADS), :].astype(BF16)
        for b in range(REQUESTS):
            rows = pl.ds(h * DRAFT, DRAFT)
            qbuf[b, rows, 0:LATENT] = absorbed[b * DRAFT : (b + 1) * DRAFT]
            qbuf[b, rows, LATENT:WIDTH] = turned[b * DRAFT : (b + 1) * DRAFT]

    scale = math.log2(math.e) / math.sqrt(192.0)
    lane = lax.broadcasted_iota(jnp.int32, (DRAFT, 128), 1)
    position = seat * KEYS + lax.broadcasted_iota(jnp.int32, (1, KEYS), 1)
    o_copies, ml_copies, own_copies = [], [], []
    for b in range(REQUESTS):
        got_draft[b].wait()
        got_cache[b].wait()
        if b == 0:
            got_value.wait()
        live_bias = jnp.where(position < lengths[b], 0.0, NEGATIVE)
        tree = tree_bias[b * DRAFT : (b + 1) * DRAFT]
        tops = jnp.zeros((DRAFT, 128), F32)
        totals = jnp.zeros((DRAFT, 128), F32)
        for start in range(0, HEADS * DRAFT, BLOCK):
            rows = pl.ds(start, BLOCK)
            scores = nt_dot(qbuf[b, rows, :], kbuf[b])
            cached = scores[:, :KEYS] + live_bias
            drafted = scores[:, KEYS:] + jnp.concatenate([tree] * (BLOCK // DRAFT), axis=0)
            top = jnp.maximum(
                jnp.max(cached, -1, keepdims=True), jnp.max(drafted, -1, keepdims=True)
            )
            cached = jnp.exp2((cached - top) * scale)
            drafted = jnp.exp2((drafted - top) * scale)
            total = jnp.sum(cached, -1, keepdims=True) + jnp.sum(drafted, -1, keepdims=True)
            pbuf[:, :KEYS] = cached.astype(BF16)
            pbuf[:, KEYS:] = drafted.astype(BF16)
            mixed = dot(pbuf[...], kbuf[b, :, 0:LATENT]).astype(BF16)
            for part in range(BLOCK // DRAFT):
                h = start // DRAFT + part
                sub = slice(part * DRAFT, (part + 1) * DRAFT)
                o_send[b, h] = dot(mixed[sub], value_weight[h]).astype(BF16)
                tops = jnp.where(lane == h, top[sub] * scale, tops)
                totals = jnp.where(lane == h, total[sub], totals)
        turned = jnp.concatenate([tops, totals], axis=0).T
        for h in range(HEADS):
            ml_send[b, h] = turned[h : h + 1]
        if b == 0:
            pl.semaphore_wait(barrier, 30)
        for j, step in enumerate(SEQ_STEPS):
            peer = seq_peers[j]
            there, their_core = lax.div(peer, 2), lax.rem(peer, 2)
            half = pl.ds(pl.multiple_of(their_core * 32, 32), 32)
            copy = pltpu.make_async_remote_copy(
                o_send.at[b, there, half, :],
                o_recv.at[b, j],
                o_sems.at[0, b, j],
                o_sems.at[1, b, j],
                device_id={"seq": peer},
                device_id_type=MESH,
            )
            copy.start()
            o_copies.append(copy)
            copy = pltpu.make_async_remote_copy(
                ml_send.at[b, there],
                ml_recv.at[b, j],
                ml_sems.at[0, b, j],
                ml_sems.at[1, b, j],
                device_id={"seq": peer},
                device_id_type=MESH,
            )
            copy.start()
            ml_copies.append(copy)
        half = pl.ds(pl.multiple_of(core * 32, 32), 32)
        for k, (src, dst) in enumerate(
            ((o_send.at[b, chip, half, :], o_recv.at[b, 15]), (ml_send.at[b, chip], ml_recv.at[b, 15]))
        ):
            copy = pltpu.make_async_copy(src, dst, local_sems.at[b, k])
            copy.start()
            own_copies.append(copy)

    g_copies = []
    for b in range(REQUESTS):
        for copy in ml_copies[b * 15 : (b + 1) * 15]:
            copy.wait_recv()
        for copy in own_copies[b * 2 : (b + 1) * 2]:
            copy.wait()
        gathered = jnp.concatenate(
            [ml_recv[b, j] for j in range(16)] + [jnp.full((112, 128), NEGATIVE, F32)], axis=0
        ).T
        tops, totals = gathered[:DRAFT], gathered[DRAFT:]
        shares = jnp.exp2(tops - jnp.max(tops, -1, keepdims=True))
        shares = shares / jnp.sum(shares * totals, -1, keepdims=True)
        shares = jnp.where(core == 0, shares[:32], shares[32:])
        for copy in o_copies[b * 15 : (b + 1) * 15]:
            copy.wait_recv()
        summed = jnp.zeros((32, 128), F32)
        for j in range(16):
            summed = summed + shares[:, j : j + 1] * o_recv[b, j].astype(F32)
        g_send[b] = summed.astype(BF16)
        place = g_full.at[
            pl.ds(pl.multiple_of(b * DRAFT + core * 32, 32), 32),
            pl.ds(pl.multiple_of(chip * 128, 128), 128),
        ]
        for j, peer in enumerate(seq_peers):
            copy = pltpu.make_async_remote_copy(
                g_send.at[b],
                place,
                g_sems.at[0, b, j],
                g_sems.at[1, b, j],
                device_id={"seq": peer},
                device_id_type=MESH,
            )
            copy.start()
            g_copies.append(copy)
        copy = pltpu.make_async_copy(g_send.at[b], place, local_sems.at[b, 2])
        copy.start()
        own_copies.append(copy)

    got_out.wait()
    for copy in own_copies[4:]:
        copy.wait()
    for copy in g_copies:
        copy.wait_recv()
    attention = dot(g_full[...], out_weight[...]).astype(BF16)
    for i in range(16):
        a_send[i] = attention[i * 8 : (i + 1) * 8]
    a_copies = []
    for j, peer in enumerate(head_peers):
        copy = pltpu.make_async_remote_copy(
            a_send.at[peer],
            a_recv.at[j],
            a_sems.at[0, j],
            a_sems.at[1, j],
            device_id={"head": peer},
            device_id_type=MESH,
        )
        copy.start()
        a_copies.append(copy)
    summed = a_send[mine].astype(F32)
    for j, copy in enumerate(a_copies):
        copy.wait_recv()
        summed = summed + a_recv[j].astype(F32)
    b_send[...] = summed.astype(BF16)
    b_copies = []
    for j, peer in enumerate(head_peers):
        copy = pltpu.make_async_remote_copy(
            b_send,
            b_full.at[mine],
            b_sems.at[0, j],
            b_sems.at[1, j],
            device_id={"head": peer},
            device_id_type=MESH,
        )
        copy.start()
        b_copies.append(copy)
    b_full[mine] = b_send[...]
    got_residual.wait()
    got_gain.wait()
    for copy in b_copies:
        copy.wait_recv()
    attention = jnp.concatenate([b_full[i].astype(F32) for i in range(16)], axis=0)
    hidden = residual[...].astype(F32) + attention

    squares = jnp.sum(hidden * hidden, -1, keepdims=True)
    s_send[...] = jnp.broadcast_to(squares, (TOKENS, 128)).T[0:1]
    s_copies = []
    for j, peer in enumerate(seq_peers):
        copy = pltpu.make_async_remote_copy(
            s_send,
            s_recv.at[j],
            s_sems.at[0, j],
            s_sems.at[1, j],
            device_id={"seq": peer},
            device_id_type=MESH,
        )
        copy.start()
        s_copies.append(copy)
    scaled = (hidden * gain[...].astype(F32)).astype(BF16)

    p_copies = []
    for j in range(8):
        got_vocab[j].wait()
        p_send[j] = dot(scaled, vocab[j]).astype(BF16)
        copy = pltpu.make_async_remote_copy(
            p_send.at[j],
            p_recv.at[j],
            p_sems.at[0, j],
            p_sems.at[1, j],
            device_id={"seq": seq_peers[14]},
            device_id_type=MESH,
        )
        copy.start()
        p_copies.append(copy)
    l_copies = []
    for j in range(8):
        got_vocab[8 + j].wait()
        part = dot(scaled, vocab[8 + j])
        p_copies[j].wait_recv()
        part = part + p_recv[j].astype(F32)
        if j < 7:
            l_send[j] = part.astype(BF16)
            copy = pltpu.make_async_remote_copy(
                l_send.at[j],
                l_recv.at[j],
                l_sems.at[0, j],
                l_sems.at[1, j],
                device_id={"seq": seq_peers[2 * j]},
                device_id_type=MESH,
            )
            copy.start()
            l_copies.append(copy)
    total = s_send[...]
    for j, copy in enumerate(s_copies):
        copy.wait_recv()
        total = total + s_recv[j]
    spread = jnp.broadcast_to(lax.rsqrt(total / model_width + EPSILON), (128, TOKENS)).T
    for j, copy in enumerate(l_copies):
        copy.wait_recv()
        part = part + l_recv[j].astype(F32)
    logits[...] = (part * spread[:, 0:1]).astype(BF16)
    for copy in o_copies + ml_copies + g_copies + a_copies + b_copies + s_copies + p_copies + l_copies:
        copy.wait_send()


def per_device(
    latent_cache,
    draft_latent,
    query_nope,
    query_rope,
    parents,
    lengths,
    key_weight,
    value_weight,
    out_weight,
    residual,
    norm_gain,
    vocab_weight,
):
    local_width = residual.shape[2]
    model_width = local_width * lax.axis_size("seq")
    draft = jnp.pad(draft_latent.reshape(8, WIDTH), ((0, 8), (0, 0)))
    hbm = pl.BlockSpec(memory_space=pl.ANY)
    dma = pltpu.SemaphoreType.DMA
    logits = pl.pallas_call(
        functools.partial(kernel, model_width),
        out_shape=jax.ShapeDtypeStruct((TOKENS, 256), BF16),
        in_specs=[pl.BlockSpec(memory_space=pltpu.SMEM)] + [hbm] * 11,
        out_specs=pl.BlockSpec(memory_space=pltpu.VMEM),
        scratch_shapes=[
            pltpu.VMEM((1, TOKENS), jnp.int32),
            pltpu.VMEM((REQUESTS, PADDED, WIDTH), BF16),
            pltpu.VMEM((TOKENS * HEADS, 128), BF16),
            pltpu.VMEM((TOKENS * HEADS, ROPE), BF16),
            pltpu.VMEM((HEADS, 128, LATENT), BF16),
            pltpu.VMEM((HEADS, LATENT, 128), BF16),
            pltpu.VMEM((1024, local_width), BF16),
            pltpu.VMEM((TOKENS, local_width), BF16),
            pltpu.VMEM((1, local_width), BF16),
            pltpu.VMEM((16, local_width, 256), BF16),
            pltpu.VMEM((TOKENS * HEADS, 128), F32),
            pltpu.VMEM((TOKENS * HEADS, ROPE), F32),
            pltpu.VMEM((REQUESTS, HEADS * DRAFT, WIDTH), BF16),
            pltpu.VMEM((BLOCK, PADDED), BF16),
            pltpu.VMEM((REQUESTS, HEADS, DRAFT, 128), BF16),
            pltpu.VMEM((REQUESTS, 16, 32, 128), BF16),
            pltpu.VMEM((REQUESTS, HEADS, 1, 128), F32),
            pltpu.VMEM((REQUESTS, 16, 1, 128), F32),
            pltpu.VMEM((REQUESTS, 32, 128), BF16),
            pltpu.VMEM((TOKENS, 1024), BF16),
            pltpu.VMEM((16, 8, local_width), BF16),
            pltpu.VMEM((15, 8, local_width), BF16),
            pltpu.VMEM((8, local_width), BF16),
            pltpu.VMEM((16, 8, local_width), BF16),
            pltpu.VMEM((1, TOKENS), F32),
            pltpu.VMEM((15, 1, TOKENS), F32),
            pltpu.VMEM((8, TOKENS, 256), BF16),
            pltpu.VMEM((8, TOKENS, 256), BF16),
            pltpu.VMEM((7, TOKENS, 256), BF16),
            pltpu.VMEM((7, TOKENS, 256), BF16),
            dma((12,)),
            dma((16,)),
            dma((REQUESTS, 3)),
            dma((2, REQUESTS, 15)),
            dma((2, REQUESTS, 15)),
            dma((2, REQUESTS, 15)),
            dma((2, 15)),
            dma((2, 15)),
            dma((2, 15)),
            dma((2, 8)),
            dma((2, 7)),
        ],
        compiler_params=pltpu.CompilerParams(
            collective_id=0, has_side_effects=True, vmem_limit_bytes=60 * 1024 * 1024
        ),
    )(
        lengths,
        parents.reshape(1, TOKENS),
        latent_cache,
        draft,
        query_nope.reshape(TOKENS * HEADS, 128),
        query_rope.reshape(TOKENS * HEADS, ROPE),
        key_weight,
        value_weight,
        out_weight,
        residual.reshape(TOKENS, local_width),
        norm_gain.reshape(1, local_width),
        vocab_weight,
    )
    return logits.reshape(REQUESTS, DRAFT, 256)


def solution(mesh):
    in_specs = (
        P(None, "seq", None),
        P(None, "seq", None),
        P(None, None, "head", None),
        P(None, None, "head", None),
        P(),
        P(),
        P("head", None, None),
        P("head", None, None),
        P("head", "seq"),
        P(None, None, "seq"),
        P("seq"),
        P("seq", "head"),
    )
    out_specs = P(None, None, ("head", "seq"))
    return jax.shard_map(
        per_device, mesh=mesh, in_specs=in_specs, out_specs=out_specs, check_vma=False
    )
```

```python
import functools
import math

import jax
import jax.numpy as jnp
from jax import lax
from jax.experimental import pallas as pl
from jax.experimental.pallas import tpu as pltpu
from jax.sharding import PartitionSpec as P

MESH = pl.DeviceIdType.MESH
NEGATIVE = -1e30
EPSILON = 1e-06
F32 = jnp.float32
BF16 = jnp.bfloat16

CHIP_STEPS = [(2, 1), (1, 1), (3, 1), (2, 0), (0, 1), (1, 0), (3, 0)]
SEQ_STEPS = [(dy, dx, dk) for dy, dx in CHIP_STEPS for dk in (0, 1)] + [(0, 0, 1)]
REQUESTS, DRAFT, HEADS, LATENT, ROPE, WIDTH = 2, 64, 8, 512, 64, 576
TOKENS = REQUESTS * DRAFT
KEYS, EXTRA = 2048, 128
BLOCK = 256


def nt_dot(a, b):
    return lax.dot_general(a, b, (((1,), (1,)), ((), ())), preferred_element_type=F32)


def dot(a, b):
    return jnp.dot(a, b, preferred_element_type=F32)


def kernel(
    model_width,
    lengths,
    parents_hbm,
    cache_hbm,
    draft_hbm,
    nope_hbm,
    rope_hbm,
    key_hbm,
    value_hbm,
    out_hbm,
    residual_hbm,
    gain_hbm,
    vocab_hbm,
    logits,
    parents,
    kbuf,
    draft,
    dbuf,
    nope,
    rope,
    key_weight,
    value_weight,
    out_weight,
    residual,
    gain,
    vocab,
    nope32,
    rope32,
    qbuf,
    o_send,
    o_recv,
    ml_send,
    ml_recv,
    g_send,
    g_full,
    a_send,
    a_recv,
    b_send,
    b_full,
    s_send,
    s_recv,
    p_send,
    p_recv,
    l_send,
    l_recv,
    load_sems,
    vocab_sems,
    local_sems,
    o_sems,
    ml_sems,
    g_sems,
    a_sems,
    b_sems,
    s_sems,
    p_sems,
    l_sems,
):
    seat = lax.axis_index("seq")
    mine = lax.axis_index("head")
    y = lax.div(seat, 4)
    xh = lax.rem(lax.div(seat, 2), 2)
    core = lax.rem(seat, 2)
    chip = lax.div(seat, 2)

    def seat_at(dy, dx, dk):
        return lax.rem(y + dy, 4) * 4 + lax.rem(xh + dx, 2) * 2 + lax.rem(core + dk, 2)

    seq_peers = [seat_at(*step) for step in SEQ_STEPS]
    head_peers = [lax.rem(mine + j, 16) for j in range(1, 16)]

    barrier = pltpu.get_barrier_semaphore()
    for peer in seq_peers:
        pl.semaphore_signal(barrier, inc=1, device_id={"seq": peer}, device_id_type=MESH)
    for peer in head_peers:
        pl.semaphore_signal(barrier, inc=1, device_id={"head": peer}, device_id_type=MESH)

    loads = []

    def load(src, dst):
        copy = pltpu.make_async_copy(src, dst, load_sems.at[len(loads)])
        loads.append(copy)
        copy.start()
        return copy

    got_nope = load(nope_hbm, nope)
    got_rope = load(rope_hbm, rope)
    got_key = load(key_hbm, key_weight)
    got_parents = load(parents_hbm, parents)
    got_draft = load(draft_hbm, draft)
    got_cache = [load(cache_hbm.at[b], kbuf.at[b]) for b in range(REQUESTS)]
    got_value = load(value_hbm, value_weight)
    got_out = load(out_hbm, out_weight)
    got_residual = load(residual_hbm, residual)
    got_gain = load(gain_hbm, gain)

    vocab_order = []
    for half in (1, 0):
        for dy, dx in CHIP_STEPS + [(0, 0)]:
            vocab_order.append(seat_at(dy, dx, half))
    got_vocab = []
    for slot, owner in enumerate(vocab_order):
        columns = pl.ds(pl.multiple_of(owner * 256, 256), 256)
        copy = pltpu.make_async_copy(
            vocab_hbm.at[:, columns], vocab.at[slot], vocab_sems.at[slot]
        )
        copy.start()
        got_vocab.append(copy)

    got_parents.wait()
    row = lax.broadcasted_iota(jnp.int32, (DRAFT, DRAFT), 0)
    column = lax.broadcasted_iota(jnp.int32, (DRAFT, DRAFT), 1)
    reaches = [
        jnp.where((parents[b : b + 1, :] == row) | (row == column), 1.0, 0.0).astype(BF16)
        for b in range(REQUESTS)
    ]
    for _ in range(6):
        reaches = [jnp.where(dot(r, r) > 0.5, 1.0, 0.0).astype(BF16) for r in reaches]
    row = lax.broadcasted_iota(jnp.int32, (DRAFT, EXTRA), 0)
    column = lax.broadcasted_iota(jnp.int32, (DRAFT, EXTRA), 1)
    tree_bias = []
    for b in range(REQUESTS):
        chosen = (column >= 4 * b) & (column < 4 * b + 4) & (row == seat * 4 + column - 4 * b)
        chosen = jnp.where(chosen, 1.0, 0.0).astype(BF16)
        reached = lax.dot_general(
            reaches[b], chosen, (((0,), (0,)), ((), ())), preferred_element_type=F32
        )
        tree_bias.append(jnp.where(reached > 0.5, 0.0, NEGATIVE))
    got_draft.wait()
    dbuf[...] = jnp.zeros((EXTRA, WIDTH), BF16)
    dbuf[0:8, :] = jnp.concatenate([draft[b].astype(F32) for b in range(REQUESTS)], axis=0).astype(BF16)

    got_nope.wait()
    nope32[...] = nope[...].astype(F32)
    got_rope.wait()
    rope32[...] = rope[...].astype(F32)
    got_key.wait()
    for h in range(HEADS):
        picked = nope32[pl.ds(h, TOKENS, stride=HEADS), :].astype(BF16)
        absorbed = dot(picked, key_weight[h]).astype(BF16)
        turned = rope32[pl.ds(h, TOKENS, stride=HEADS), :].astype(BF16)
        for b in range(REQUESTS):
            rows = pl.ds(h * DRAFT, DRAFT)
            qbuf[b, rows, 0:LATENT] = absorbed[b * DRAFT : (b + 1) * DRAFT]
            qbuf[b, rows, LATENT:WIDTH] = turned[b * DRAFT : (b + 1) * DRAFT]

    scale = math.log2(math.e) / math.sqrt(192.0)
    lane = lax.broadcasted_iota(jnp.int32, (DRAFT, 128), 1)
    position = seat * KEYS + lax.broadcasted_iota(jnp.int32, (1, KEYS), 1)
    o_copies, ml_copies, own_copies = [], [], []
    for b in range(REQUESTS):
        got_cache[b].wait()
        if b == 0:
            got_value.wait()
        live_bias = jnp.where(position < lengths[b], 0.0, NEGATIVE)
        tree = jnp.concatenate([tree_bias[b]] * (BLOCK // DRAFT), axis=0)
        tops = jnp.zeros((DRAFT, 128), F32)
        totals = jnp.zeros((DRAFT, 128), F32)
        for start in range(0, HEADS * DRAFT, BLOCK):
            rows = pl.ds(start, BLOCK)
            cached = dot(qbuf[b, rows, :], kbuf[b]) + live_bias
            drafted = nt_dot(qbuf[b, rows, :], dbuf[...]) + tree
            top = jnp.maximum(
                jnp.max(cached, -1, keepdims=True), jnp.max(drafted, -1, keepdims=True)
            )
            cached = jnp.exp2((cached - top) * scale)
            drafted = jnp.exp2((drafted - top) * scale)
            total = jnp.sum(cached, -1, keepdims=True) + jnp.sum(drafted, -1, keepdims=True)
            mixed = nt_dot(cached.astype(BF16), kbuf[b, 0:LATENT, :])
            mixed = (mixed + dot(drafted.astype(BF16), dbuf[:, 0:LATENT])).astype(BF16)
            for part in range(BLOCK // DRAFT):
                h = start // DRAFT + part
                sub = slice(part * DRAFT, (part + 1) * DRAFT)
                o_send[b, h] = dot(mixed[sub], value_weight[h]).astype(BF16)
                tops = jnp.where(lane == h, top[sub] * scale, tops)
                totals = jnp.where(lane == h, total[sub], totals)
        turned = jnp.concatenate([tops, totals], axis=0).T
        for h in range(HEADS):
            ml_send[b, h] = turned[h : h + 1]
        if b == 0:
            pl.semaphore_wait(barrier, 30)
        for j, step in enumerate(SEQ_STEPS):
            peer = seq_peers[j]
            there, their_core = lax.div(peer, 2), lax.rem(peer, 2)
            half = pl.ds(pl.multiple_of(their_core * 32, 32), 32)
            copy = pltpu.make_async_remote_copy(
                o_send.at[b, there, half, :],
                o_recv.at[b, j],
                o_sems.at[0, b, j],
                o_sems.at[1, b, j],
                device_id={"seq": peer},
                device_id_type=MESH,
            )
            copy.start()
            o_copies.append(copy)
            copy = pltpu.make_async_remote_copy(
                ml_send.at[b, there],
                ml_recv.at[b, j],
                ml_sems.at[0, b, j],
                ml_sems.at[1, b, j],
                device_id={"seq": peer},
                device_id_type=MESH,
            )
            copy.start()
            ml_copies.append(copy)
        half = pl.ds(pl.multiple_of(core * 32, 32), 32)
        for k, (src, dst) in enumerate(
            ((o_send.at[b, chip, half, :], o_recv.at[b, 15]), (ml_send.at[b, chip], ml_recv.at[b, 15]))
        ):
            copy = pltpu.make_async_copy(src, dst, local_sems.at[b, k])
            copy.start()
            own_copies.append(copy)

    g_copies = []
    for b in range(REQUESTS):
        for copy in ml_copies[b * 15 : (b + 1) * 15]:
            copy.wait_recv()
        for copy in own_copies[b * 2 : (b + 1) * 2]:
            copy.wait()
        gathered = jnp.concatenate(
            [ml_recv[b, j] for j in range(16)] + [jnp.full((112, 128), NEGATIVE, F32)], axis=0
        ).T
        tops, totals = gathered[:DRAFT], gathered[DRAFT:]
        shares = jnp.exp2(tops - jnp.max(tops, -1, keepdims=True))
        shares = shares / jnp.sum(shares * totals, -1, keepdims=True)
        shares = jnp.where(core == 0, shares[:32], shares[32:])
        for copy in o_copies[b * 15 : (b + 1) * 15]:
            copy.wait_recv()
        summed = jnp.zeros((32, 128), F32)
        for j in range(16):
            summed = summed + shares[:, j : j + 1] * o_recv[b, j].astype(F32)
        g_send[b] = summed.astype(BF16)
        place = g_full.at[
            pl.ds(pl.multiple_of(b * DRAFT + core * 32, 32), 32),
            pl.ds(pl.multiple_of(chip * 128, 128), 128),
        ]
        for j, peer in enumerate(seq_peers):
            copy = pltpu.make_async_remote_copy(
                g_send.at[b],
                place,
                g_sems.at[0, b, j],
                g_sems.at[1, b, j],
                device_id={"seq": peer},
                device_id_type=MESH,
            )
            copy.start()
            g_copies.append(copy)
        copy = pltpu.make_async_copy(g_send.at[b], place, local_sems.at[b, 2])
        copy.start()
        own_copies.append(copy)

    got_out.wait()
    for copy in own_copies[4:]:
        copy.wait()
    for copy in g_copies:
        copy.wait_recv()
    attention = nt_dot(g_full[...], out_weight[...]).astype(BF16)
    for i in range(16):
        a_send[i] = attention[i * 8 : (i + 1) * 8]
    a_copies = []
    for j, peer in enumerate(head_peers):
        copy = pltpu.make_async_remote_copy(
            a_send.at[peer],
            a_recv.at[j],
            a_sems.at[0, j],
            a_sems.at[1, j],
            device_id={"head": peer},
            device_id_type=MESH,
        )
        copy.start()
        a_copies.append(copy)
    summed = a_send[mine].astype(F32)
    for j, copy in enumerate(a_copies):
        copy.wait_recv()
        summed = summed + a_recv[j].astype(F32)
    b_send[...] = summed.astype(BF16)
    b_copies = []
    for j, peer in enumerate(head_peers):
        copy = pltpu.make_async_remote_copy(
            b_send,
            b_full.at[mine],
            b_sems.at[0, j],
            b_sems.at[1, j],
            device_id={"head": peer},
            device_id_type=MESH,
        )
        copy.start()
        b_copies.append(copy)
    b_full[mine] = b_send[...]
    got_residual.wait()
    got_gain.wait()
    for copy in b_copies:
        copy.wait_recv()
    attention = jnp.concatenate([b_full[i].astype(F32) for i in range(16)], axis=0)
    hidden = residual[...].astype(F32) + attention

    squares = jnp.sum(hidden * hidden, -1, keepdims=True)
    s_send[...] = jnp.broadcast_to(squares, (TOKENS, 128)).T[0:1]
    s_copies = []
    for j, peer in enumerate(seq_peers):
        copy = pltpu.make_async_remote_copy(
            s_send,
            s_recv.at[j],
            s_sems.at[0, j],
            s_sems.at[1, j],
            device_id={"seq": peer},
            device_id_type=MESH,
        )
        copy.start()
        s_copies.append(copy)
    scaled = (hidden * gain[...].astype(F32)[None, :]).astype(BF16)

    p_copies = []
    for j in range(8):
        got_vocab[j].wait()
        p_send[j] = dot(scaled, vocab[j]).astype(BF16)
        copy = pltpu.make_async_remote_copy(
            p_send.at[j],
            p_recv.at[j],
            p_sems.at[0, j],
            p_sems.at[1, j],
            device_id={"seq": seq_peers[14]},
            device_id_type=MESH,
        )
        copy.start()
        p_copies.append(copy)
    l_copies = []
    for j in range(8):
        got_vocab[8 + j].wait()
        part = dot(scaled, vocab[8 + j])
        p_copies[j].wait_recv()
        part = part + p_recv[j].astype(F32)
        if j < 7:
            l_send[j] = part.astype(BF16)
            copy = pltpu.make_async_remote_copy(
                l_send.at[j],
                l_recv.at[j],
                l_sems.at[0, j],
                l_sems.at[1, j],
                device_id={"seq": seq_peers[2 * j]},
                device_id_type=MESH,
            )
            copy.start()
            l_copies.append(copy)
    total = s_send[...]
    for j, copy in enumerate(s_copies):
        copy.wait_recv()
        total = total + s_recv[j]
    spread = jnp.broadcast_to(lax.rsqrt(total / model_width + EPSILON), (128, TOKENS)).T
    for j, copy in enumerate(l_copies):
        copy.wait_recv()
        part = part + l_recv[j].astype(F32)
    logits[...] = (part * spread[:, 0:1]).astype(BF16)
    for copy in o_copies + ml_copies + g_copies + a_copies + b_copies + s_copies + p_copies + l_copies:
        copy.wait_send()


def per_device(
    latent_cache,
    draft_latent,
    query_nope,
    query_rope,
    parents,
    lengths,
    key_weight,
    value_weight,
    out_weight,
    residual,
    norm_gain,
    vocab_weight,
):
    local_width = residual.shape[2]
    model_width = local_width * lax.axis_size("seq")
    hbm = pl.BlockSpec(memory_space=pl.ANY)
    dma = pltpu.SemaphoreType.DMA
    logits = pl.pallas_call(
        functools.partial(kernel, model_width),
        out_shape=jax.ShapeDtypeStruct((TOKENS, 256), BF16),
        in_specs=[pl.BlockSpec(memory_space=pltpu.SMEM)] + [hbm] * 11,
        out_specs=pl.BlockSpec(memory_space=pltpu.VMEM),
        scratch_shapes=[
            pltpu.VMEM((REQUESTS, DRAFT), jnp.int32),
            pltpu.VMEM((REQUESTS, WIDTH, KEYS), BF16),
            pltpu.VMEM((REQUESTS, 4, WIDTH), BF16),
            pltpu.VMEM((EXTRA, WIDTH), BF16),
            pltpu.VMEM((TOKENS * HEADS, 128), BF16),
            pltpu.VMEM((TOKENS * HEADS, ROPE), BF16),
            pltpu.VMEM((HEADS, 128, LATENT), BF16),
            pltpu.VMEM((HEADS, LATENT, 128), BF16),
            pltpu.VMEM((local_width, 1024), BF16),
            pltpu.VMEM((TOKENS, local_width), BF16),
            pltpu.VMEM((local_width,), BF16),
            pltpu.VMEM((16, local_width, 256), BF16),
            pltpu.VMEM((TOKENS * HEADS, 128), F32),
            pltpu.VMEM((TOKENS * HEADS, ROPE), F32),
            pltpu.VMEM((REQUESTS, HEADS * DRAFT, WIDTH), BF16),
            pltpu.VMEM((REQUESTS, HEADS, DRAFT, 128), BF16),
            pltpu.VMEM((REQUESTS, 16, 32, 128), BF16),
            pltpu.VMEM((REQUESTS, HEADS, 1, 128), F32),
            pltpu.VMEM((REQUESTS, 16, 1, 128), F32),
            pltpu.VMEM((REQUESTS, 32, 128), BF16),
            pltpu.VMEM((TOKENS, 1024), BF16),
            pltpu.VMEM((16, 8, local_width), BF16),
            pltpu.VMEM((15, 8, local_width), BF16),
            pltpu.VMEM((8, local_width), BF16),
            pltpu.VMEM((16, 8, local_width), BF16),
            pltpu.VMEM((1, TOKENS), F32),
            pltpu.VMEM((15, 1, TOKENS), F32),
            pltpu.VMEM((8, TOKENS, 256), BF16),
            pltpu.VMEM((8, TOKENS, 256), BF16),
            pltpu.VMEM((7, TOKENS, 256), BF16),
            pltpu.VMEM((7, TOKENS, 256), BF16),
            dma((12,)),
            dma((16,)),
            dma((REQUESTS, 3)),
            dma((2, REQUESTS, 15)),
            dma((2, REQUESTS, 15)),
            dma((2, REQUESTS, 15)),
            dma((2, 15)),
            dma((2, 15)),
            dma((2, 15)),
            dma((2, 8)),
            dma((2, 7)),
        ],
        compiler_params=pltpu.CompilerParams(
            collective_id=0, has_side_effects=True, vmem_limit_bytes=60 * 1024 * 1024
        ),
    )(
        lengths,
        parents,
        jnp.swapaxes(latent_cache, 1, 2),
        draft_latent,
        query_nope.reshape(TOKENS * HEADS, 128),
        query_rope.reshape(TOKENS * HEADS, ROPE),
        key_weight,
        value_weight,
        out_weight.T,
        residual.reshape(TOKENS, local_width),
        norm_gain,
        vocab_weight,
    )
    return logits.reshape(REQUESTS, DRAFT, 256)


def solution(mesh):
    in_specs = (
        P(None, "seq", None),
        P(None, "seq", None),
        P(None, None, "head", None),
        P(None, None, "head", None),
        P(),
        P(),
        P("head", None, None),
        P("head", None, None),
        P("head", "seq"),
        P(None, None, "seq"),
        P("seq"),
        P("seq", "head"),
    )
    out_specs = P(None, None, ("head", "seq"))
    return jax.shard_map(
        per_device, mesh=mesh, in_specs=in_specs, out_specs=out_specs, check_vma=False
    )
```

```python
import functools
import math

import jax
import jax.numpy as jnp
from jax import lax
from jax.experimental import pallas as pl
from jax.experimental.pallas import tpu as pltpu
from jax.sharding import PartitionSpec as P

MESH = pl.DeviceIdType.MESH
NEGATIVE = -1e30
EPSILON = 1e-06
F32 = jnp.float32
BF16 = jnp.bfloat16

CHIP_STEPS = [(2, 1), (1, 1), (3, 1), (2, 0), (0, 1), (1, 0), (3, 0)]
SEQ_STEPS = [(dy, dx, dk) for dy, dx in CHIP_STEPS for dk in (0, 1)] + [(0, 0, 1)]
REQUESTS, DRAFT, HEADS, LATENT, ROPE, WIDTH = 2, 64, 8, 512, 64, 576
TOKENS = REQUESTS * DRAFT
KEYS, EXTRA = 2048, 128
HALF = DRAFT // 2
BLOCK = 512


def nt_dot(a, b):
    return lax.dot_general(a, b, (((1,), (1,)), ((), ())), preferred_element_type=F32)


def dot(a, b):
    return jnp.dot(a, b, preferred_element_type=F32)


def kernel(
    model_width,
    lengths,
    parents_hbm,
    cache_hbm,
    draft_hbm,
    nope_hbm,
    rope_hbm,
    key_hbm,
    value_hbm,
    out_hbm,
    residual_hbm,
    gain_hbm,
    vocab_hbm,
    logits,
    parents,
    kbuf,
    draft,
    dbuf,
    nope,
    rope,
    key_weight,
    value_weight,
    out_weight,
    residual,
    gain,
    gain_rows,
    vocab,
    nope32,
    rope32,
    qbuf,
    o_send,
    o_recv,
    ml_send,
    ml_recv,
    g_send,
    g_full,
    a_send,
    a_recv,
    b_send,
    b_full,
    s_send,
    s_recv,
    l_send,
    l_recv,
    load_sems,
    vocab_sems,
    local_sems,
    o_sems,
    ml_sems,
    g_sems,
    a_sems,
    b_sems,
    s_sems,
    swap_sems,
    l_sems,
):
    seat = lax.axis_index("seq")
    mine = lax.axis_index("head")
    y = lax.div(seat, 4)
    xh = lax.rem(lax.div(seat, 2), 2)
    core = lax.rem(seat, 2)
    chip = lax.div(seat, 2)

    def seat_at(dy, dx, dk):
        return lax.rem(y + dy, 4) * 4 + lax.rem(xh + dx, 2) * 2 + lax.rem(core + dk, 2)

    seq_peers = [seat_at(*step) for step in SEQ_STEPS]
    chip_peers = seq_peers[0:14:2]
    head_peers = [lax.rem(mine + j, 16) for j in range(1, 16)]

    barrier = pltpu.get_barrier_semaphore()
    for peer in seq_peers:
        pl.semaphore_signal(barrier, inc=1, device_id={"seq": peer}, device_id_type=MESH)
    for peer in head_peers:
        pl.semaphore_signal(barrier, inc=1, device_id={"head": peer}, device_id_type=MESH)

    loads = []

    def load(src, dst):
        copy = pltpu.make_async_copy(src, dst, load_sems.at[len(loads)])
        loads.append(copy)
        copy.start()
        return copy

    got_nope = load(nope_hbm, nope)
    got_rope = load(rope_hbm, rope)
    got_key = load(key_hbm, key_weight)
    got_parents = load(parents_hbm, parents)
    got_draft = load(draft_hbm, draft)
    got_cache = [load(cache_hbm.at[b], kbuf.at[b]) for b in range(REQUESTS)]
    got_value = load(value_hbm, value_weight)
    got_out = load(out_hbm, out_weight.at[core])
    got_residual = [
        load(
            residual_hbm.at[pl.ds(pl.multiple_of(b * DRAFT + core * HALF, HALF), HALF), :],
            residual.at[core, pl.ds(b * HALF, HALF), :],
        )
        for b in range(REQUESTS)
    ]
    got_gain = load(gain_hbm, gain)

    got_vocab = []
    for slot, (dy, dx) in enumerate(CHIP_STEPS + [(0, 0)]):
        owner = lax.div(seat_at(dy, dx, 0), 2)
        columns = pl.ds(pl.multiple_of(owner * 512, 512), 512)
        copy = pltpu.make_async_copy(
            vocab_hbm.at[:, columns], vocab.at[core, slot], vocab_sems.at[slot]
        )
        copy.start()
        got_vocab.append(copy)

    got_parents.wait()
    row = lax.broadcasted_iota(jnp.int32, (DRAFT, DRAFT), 0)
    column = lax.broadcasted_iota(jnp.int32, (DRAFT, DRAFT), 1)
    reaches = [
        jnp.where((parents[b : b + 1, :] == row) | (row == column), 1.0, 0.0).astype(BF16)
        for b in range(REQUESTS)
    ]
    for _ in range(6):
        reaches = [jnp.where(dot(r, r) > 0.5, 1.0, 0.0).astype(BF16) for r in reaches]
    row = lax.broadcasted_iota(jnp.int32, (DRAFT, EXTRA), 0)
    column = lax.broadcasted_iota(jnp.int32, (DRAFT, EXTRA), 1)
    tree_bias = []
    for b in range(REQUESTS):
        chosen = (column >= 4 * b) & (column < 4 * b + 4) & (row == seat * 4 + column - 4 * b)
        chosen = jnp.where(chosen, 1.0, 0.0).astype(BF16)
        reached = lax.dot_general(
            reaches[b], chosen, (((0,), (0,)), ((), ())), preferred_element_type=F32
        )
        tree_bias.append(jnp.where(reached > 0.5, 0.0, NEGATIVE))
    got_draft.wait()
    dbuf[...] = jnp.zeros((EXTRA, WIDTH), BF16)
    dbuf[0:8, :] = jnp.concatenate([draft[b].astype(F32) for b in range(REQUESTS)], axis=0).astype(BF16)

    got_nope.wait()
    nope32[...] = nope[...].astype(F32)
    got_rope.wait()
    rope32[...] = rope[...].astype(F32)
    got_key.wait()
    for h in range(HEADS):
        picked = nope32[pl.ds(h, TOKENS, stride=HEADS), :].astype(BF16)
        absorbed = dot(picked, key_weight[h]).astype(BF16)
        turned = rope32[pl.ds(h, TOKENS, stride=HEADS), :].astype(BF16)
        for b in range(REQUESTS):
            rows = pl.ds(h * DRAFT, DRAFT)
            qbuf[b, rows, 0:LATENT] = absorbed[b * DRAFT : (b + 1) * DRAFT]
            qbuf[b, rows, LATENT:WIDTH] = turned[b * DRAFT : (b + 1) * DRAFT]

    scale = math.log2(math.e) / math.sqrt(192.0)
    lane = lax.broadcasted_iota(jnp.int32, (DRAFT, 128), 1)
    position = seat * KEYS + lax.broadcasted_iota(jnp.int32, (1, KEYS), 1)
    o_copies, ml_copies, own_copies, swap_copies = [], [], [], []
    partner = seq_peers[14]
    for b in range(REQUESTS):
        got_cache[b].wait()
        if b == 0:
            got_value.wait()
        live_bias = jnp.where(position < lengths[b], 0.0, NEGATIVE)
        tree = jnp.concatenate([tree_bias[b]] * (BLOCK // DRAFT), axis=0)
        tops = jnp.zeros((DRAFT, 128), F32)
        totals = jnp.zeros((DRAFT, 128), F32)
        for start in range(0, HEADS * DRAFT, BLOCK):
            rows = pl.ds(start, BLOCK)
            cached = dot(qbuf[b, rows, :], kbuf[b]) + live_bias
            drafted = nt_dot(qbuf[b, rows, :], dbuf[...]) + tree
            top = jnp.maximum(
                jnp.max(cached, -1, keepdims=True), jnp.max(drafted, -1, keepdims=True)
            )
            cached = jnp.exp2((cached - top) * scale)
            drafted = jnp.exp2((drafted - top) * scale)
            total = jnp.sum(cached, -1, keepdims=True) + jnp.sum(drafted, -1, keepdims=True)
            mixed = nt_dot(cached.astype(BF16), kbuf[b, 0:LATENT, :])
            mixed = (mixed + dot(drafted.astype(BF16), dbuf[:, 0:LATENT])).astype(BF16)
            for part in range(BLOCK // DRAFT):
                h = start // DRAFT + part
                sub = slice(part * DRAFT, (part + 1) * DRAFT)
                o_send[b, h] = dot(mixed[sub], value_weight[h]).astype(BF16)
                tops = jnp.where(lane == h, top[sub] * scale, tops)
                totals = jnp.where(lane == h, total[sub], totals)
        turned = jnp.concatenate([tops, totals], axis=0).T
        for h in range(HEADS):
            ml_send[b, h] = turned[h : h + 1]
        if b == 0:
            pl.semaphore_wait(barrier, 30)
        for j, step in enumerate(SEQ_STEPS):
            peer = seq_peers[j]
            there, their_core = lax.div(peer, 2), lax.rem(peer, 2)
            half = pl.ds(pl.multiple_of(their_core * 32, 32), 32)
            copy = pltpu.make_async_remote_copy(
                o_send.at[b, there, half, :],
                o_recv.at[b, j],
                o_sems.at[0, b, j],
                o_sems.at[1, b, j],
                device_id={"seq": peer},
                device_id_type=MESH,
            )
            copy.start()
            o_copies.append(copy)
            copy = pltpu.make_async_remote_copy(
                ml_send.at[b, there],
                ml_recv.at[b, j],
                ml_sems.at[0, b, j],
                ml_sems.at[1, b, j],
                device_id={"seq": peer},
                device_id_type=MESH,
            )
            copy.start()
            ml_copies.append(copy)
        swaps = []
        if b == 0:
            got_out.wait()
            got_gain.wait()
            gain_rows[core] = gain[...].astype(F32)[None, :]
            swaps.append((out_weight.at[core], out_weight.at[core], 0))
            swaps.append((gain_rows.at[core], gain_rows.at[core], 1))
            for request in range(REQUESTS):
                other_rows = pl.multiple_of(request * DRAFT + (1 - core) * HALF, HALF)
                swaps.append(
                    (
                        residual_hbm.at[pl.ds(other_rows, HALF), :],
                        residual.at[core, pl.ds(request * HALF, HALF), :],
                        2 + request,
                    )
                )
        else:
            for slot in range(8):
                got_vocab[slot].wait()
                swaps.append((vocab.at[core, slot], vocab.at[core, slot], 4 + slot))
        for src, dst, k in swaps:
            copy = pltpu.make_async_remote_copy(
                src,
                dst,
                swap_sems.at[0, k],
                swap_sems.at[1, k],
                device_id={"seq": partner},
                device_id_type=MESH,
            )
            copy.start()
            swap_copies.append(copy)
        half = pl.ds(pl.multiple_of(core * 32, 32), 32)
        for k, (src, dst) in enumerate(
            ((o_send.at[b, chip, half, :], o_recv.at[b, 15]), (ml_send.at[b, chip], ml_recv.at[b, 15]))
        ):
            copy = pltpu.make_async_copy(src, dst, local_sems.at[b, k])
            copy.start()
            own_copies.append(copy)

    g_copies = []
    for b in range(REQUESTS):
        for copy in ml_copies[b * 15 : (b + 1) * 15]:
            copy.wait_recv()
        for copy in own_copies[b * 2 : (b + 1) * 2]:
            copy.wait()
        gathered = jnp.concatenate(
            [ml_recv[b, j] for j in range(16)] + [jnp.full((112, 128), NEGATIVE, F32)], axis=0
        ).T
        tops, totals = gathered[:DRAFT], gathered[DRAFT:]
        shares = jnp.exp2(tops - jnp.max(tops, -1, keepdims=True))
        shares = shares / jnp.sum(shares * totals, -1, keepdims=True)
        shares = jnp.where(core == 0, shares[:32], shares[32:])
        for copy in o_copies[b * 15 : (b + 1) * 15]:
            copy.wait_recv()
        summed = jnp.zeros((32, 128), F32)
        for j in range(16):
            summed = summed + shares[:, j : j + 1] * o_recv[b, j].astype(F32)
        g_send[b] = summed.astype(BF16)
        place = g_full.at[
            pl.ds(b * HALF, HALF),
            pl.ds(pl.multiple_of(chip * 128, 128), 128),
        ]
        for j, peer in enumerate(chip_peers):
            copy = pltpu.make_async_remote_copy(
                g_send.at[b],
                place,
                g_sems.at[0, b, j],
                g_sems.at[1, b, j],
                device_id={"seq": peer},
                device_id_type=MESH,
            )
            copy.start()
            g_copies.append(copy)
        copy = pltpu.make_async_copy(g_send.at[b], place, local_sems.at[b, 2])
        copy.start()
        own_copies.append(copy)

    for copy in own_copies[4:]:
        copy.wait()
    swap_copies[0].wait_recv()
    for copy in g_copies:
        copy.wait_recv()
    for side in range(2):
        attention = nt_dot(g_full[...], out_weight[side]).astype(BF16)
        for i in range(8):
            a_send[2 * i + side] = attention[i * 8 : (i + 1) * 8]
    a_copies = []
    for j, peer in enumerate(head_peers):
        copy = pltpu.make_async_remote_copy(
            a_send.at[peer],
            a_recv.at[j],
            a_sems.at[0, j],
            a_sems.at[1, j],
            device_id={"head": peer},
            device_id_type=MESH,
        )
        copy.start()
        a_copies.append(copy)
    summed = a_send[mine].astype(F32)
    for j, copy in enumerate(a_copies):
        copy.wait_recv()
        summed = summed + a_recv[j].astype(F32)
    b_send[...] = summed.astype(BF16)
    b_copies = []
    for j, peer in enumerate(head_peers):
        copy = pltpu.make_async_remote_copy(
            b_send,
            b_full.at[mine],
            b_sems.at[0, j],
            b_sems.at[1, j],
            device_id={"head": peer},
            device_id_type=MESH,
        )
        copy.start()
        b_copies.append(copy)
    b_full[mine] = b_send[...]
    for copy in got_residual:
        copy.wait()
    for copy in swap_copies[1:4]:
        copy.wait_recv()
    for copy in b_copies:
        copy.wait_recv()
    squares = jnp.zeros((2 * HALF, 1), F32)
    scaled = []
    for side in range(2):
        attention = jnp.concatenate(
            [b_full[2 * i + side].astype(F32) for i in range(8)], axis=0
        )
        hidden = residual[side].astype(F32) + attention
        squares = squares + jnp.sum(hidden * hidden, -1, keepdims=True)
        scaled.append((hidden * gain_rows[side]).astype(BF16))

    s_send[...] = jnp.broadcast_to(jnp.concatenate([squares] * 2, axis=0), (TOKENS, 128)).T[0:1]
    s_copies = []
    for j, peer in enumerate(seq_peers):
        copy = pltpu.make_async_remote_copy(
            s_send,
            s_recv.at[j],
            s_sems.at[0, j],
            s_sems.at[1, j],
            device_id={"seq": peer},
            device_id_type=MESH,
        )
        copy.start()
        s_copies.append(copy)
    l_copies = []
    for slot in range(8):
        swap_copies[4 + slot].wait_recv()
        part = dot(scaled[0], vocab[0, slot]) + dot(scaled[1], vocab[1, slot])
        for side in range(2):
            l_send[slot, side] = part[:, side * 256 : (side + 1) * 256].astype(BF16)
        for dk in range(2):
            j = 2 * slot + dk
            if slot == 7:
                if dk == 0:
                    continue
                j = 14
            copy = pltpu.make_async_remote_copy(
                l_send.at[slot, lax.rem(core + dk, 2)],
                l_recv.at[j],
                l_sems.at[0, j],
                l_sems.at[1, j],
                device_id={"seq": seq_peers[j]},
                device_id_type=MESH,
            )
            copy.start()
            l_copies.append(copy)
    sums = [l_send[7, core].astype(F32), jnp.zeros((2 * HALF, 256), F32)]
    squares = [s_send[...], jnp.zeros((1, TOKENS), F32)]
    for j, (_, _, dk) in enumerate(SEQ_STEPS):
        s_copies[j].wait_recv()
        squares[dk] = squares[dk] + s_recv[j]
    for j, (_, _, dk) in enumerate(SEQ_STEPS):
        l_copies[j].wait_recv()
        sums[dk] = sums[dk] + l_recv[j].astype(F32)
    for dk in range(2):
        scales = jnp.broadcast_to(
            lax.rsqrt(squares[dk] / model_width + EPSILON), (128, TOKENS)
        ).T
        done = (sums[dk] * scales[: 2 * HALF, 0:1]).astype(BF16)
        owner = lax.rem(core + dk, 2)
        for b in range(REQUESTS):
            rows = pl.ds(pl.multiple_of(b * DRAFT + owner * HALF, HALF), HALF)
            logits[rows, :] = done[b * HALF : (b + 1) * HALF]
    for copy in o_copies + ml_copies + swap_copies + g_copies + a_copies + b_copies + s_copies + l_copies:
        copy.wait_send()


def per_device(
    latent_cache,
    draft_latent,
    query_nope,
    query_rope,
    parents,
    lengths,
    key_weight,
    value_weight,
    out_weight,
    residual,
    norm_gain,
    vocab_weight,
):
    local_width = residual.shape[2]
    model_width = local_width * lax.axis_size("seq")
    hbm = pl.BlockSpec(memory_space=pl.ANY)
    dma = pltpu.SemaphoreType.DMA
    logits = pl.pallas_call(
        functools.partial(kernel, model_width),
        out_shape=jax.ShapeDtypeStruct((TOKENS, 256), BF16),
        in_specs=[pl.BlockSpec(memory_space=pltpu.SMEM)] + [hbm] * 11,
        out_specs=pl.BlockSpec(memory_space=pltpu.VMEM),
        scratch_shapes=[
            pltpu.VMEM((REQUESTS, DRAFT), jnp.int32),
            pltpu.VMEM((REQUESTS, WIDTH, KEYS), BF16),
            pltpu.VMEM((REQUESTS, 4, WIDTH), BF16),
            pltpu.VMEM((EXTRA, WIDTH), BF16),
            pltpu.VMEM((TOKENS * HEADS, 128), BF16),
            pltpu.VMEM((TOKENS * HEADS, ROPE), BF16),
            pltpu.VMEM((HEADS, 128, LATENT), BF16),
            pltpu.VMEM((HEADS, LATENT, 128), BF16),
            pltpu.VMEM((2, local_width, 1024), BF16),
            pltpu.VMEM((2, 2 * HALF, local_width), BF16),
            pltpu.VMEM((local_width,), BF16),
            pltpu.VMEM((2, 1, local_width), F32),
            pltpu.VMEM((2, 8, local_width, 512), BF16),
            pltpu.VMEM((TOKENS * HEADS, 128), F32),
            pltpu.VMEM((TOKENS * HEADS, ROPE), F32),
            pltpu.VMEM((REQUESTS, HEADS * DRAFT, WIDTH), BF16),
            pltpu.VMEM((REQUESTS, HEADS, DRAFT, 128), BF16),
            pltpu.VMEM((REQUESTS, 16, 32, 128), BF16),
            pltpu.VMEM((REQUESTS, HEADS, 1, 128), F32),
            pltpu.VMEM((REQUESTS, 16, 1, 128), F32),
            pltpu.VMEM((REQUESTS, 32, 128), BF16),
            pltpu.VMEM((2 * HALF, 1024), BF16),
            pltpu.VMEM((16, 8, local_width), BF16),
            pltpu.VMEM((15, 8, local_width), BF16),
            pltpu.VMEM((8, local_width), BF16),
            pltpu.VMEM((16, 8, local_width), BF16),
            pltpu.VMEM((1, TOKENS), F32),
            pltpu.VMEM((15, 1, TOKENS), F32),
            pltpu.VMEM((8, 2, 2 * HALF, 256), BF16),
            pltpu.VMEM((15, 2 * HALF, 256), BF16),
            dma((12,)),
            dma((8,)),
            dma((REQUESTS, 3)),
            dma((2, REQUESTS, 15)),
            dma((2, REQUESTS, 15)),
            dma((2, REQUESTS, 7)),
            dma((2, 15)),
            dma((2, 15)),
            dma((2, 15)),
            dma((2, 12)),
            dma((2, 15)),
        ],
        compiler_params=pltpu.CompilerParams(
            collective_id=0, has_side_effects=True, vmem_limit_bytes=60 * 1024 * 1024
        ),
    )(
        lengths,
        parents,
        jnp.swapaxes(latent_cache, 1, 2),
        draft_latent,
        query_nope.reshape(TOKENS * HEADS, 128),
        query_rope.reshape(TOKENS * HEADS, ROPE),
        key_weight,
        value_weight,
        out_weight.T,
        residual.reshape(TOKENS, local_width),
        norm_gain,
        vocab_weight,
    )
    return logits.reshape(REQUESTS, DRAFT, 256)


def solution(mesh):
    in_specs = (
        P(None, "seq", None),
        P(None, "seq", None),
        P(None, None, "head", None),
        P(None, None, "head", None),
        P(),
        P(),
        P("head", None, None),
        P("head", None, None),
        P("head", "seq"),
        P(None, None, "seq"),
        P("seq"),
        P("seq", "head"),
    )
    out_specs = P(None, None, ("head", "seq"))
    return jax.shard_map(
        per_device, mesh=mesh, in_specs=in_specs, out_specs=out_specs, check_vma=False
    )
```

```python
import functools
import math

import jax
import jax.numpy as jnp
from jax import lax
from jax.experimental import pallas as pl
from jax.experimental.pallas import tpu as pltpu
from jax.sharding import PartitionSpec as P

MESH = pl.DeviceIdType.MESH
NEGATIVE = -1e30
EPSILON = 1e-06
F32 = jnp.float32
BF16 = jnp.bfloat16

CHIP_STEPS = [(2, 1), (1, 1), (3, 1), (2, 0), (0, 1), (1, 0), (3, 0)]
SEQ_STEPS = [(dy, dx, dk) for dy, dx in CHIP_STEPS for dk in (0, 1)] + [(0, 0, 1)]
REQUESTS, DRAFT, HEADS, LATENT, ROPE, WIDTH = 2, 64, 8, 512, 64, 576
TOKENS = REQUESTS * DRAFT
KEYS, EXTRA = 2048, 128
HALF = DRAFT // 2


def nt_dot(a, b):
    return lax.dot_general(a, b, (((1,), (1,)), ((), ())), preferred_element_type=F32)


def dot(a, b):
    return jnp.dot(a, b, preferred_element_type=F32)


def kernel(
    model_width,
    lengths_hbm,
    parents_hbm,
    cache_hbm,
    draft_hbm,
    nope_hbm,
    rope_hbm,
    key_hbm,
    value_hbm,
    out_hbm,
    residual_hbm,
    gain_hbm,
    vocab_hbm,
    logits,
    lengths,
    parents,
    kbuf,
    draft,
    dbuf,
    nope,
    rope,
    key_weight,
    value_weight,
    out_weight,
    residual,
    gain,
    gain_rows,
    vocab,
    nope32,
    rope32,
    qbuf,
    o_send,
    o_recv,
    ml_send,
    ml_recv,
    g_send,
    g_full,
    a_send,
    a_recv,
    b_send,
    b_full,
    s_send,
    s_recv,
    l_send,
    l_recv,
    load_sems,
    vocab_sems,
    local_sems,
    o_sems,
    ml_sems,
    g_sems,
    a_sems,
    b_sems,
    s_sems,
    swap_sems,
    l_sems,
):
    seat = lax.axis_index("seq")
    mine = lax.axis_index("head")
    y = lax.div(seat, 4)
    xh = lax.rem(lax.div(seat, 2), 2)
    core = lax.rem(seat, 2)
    chip = lax.div(seat, 2)

    def seat_at(dy, dx, dk):
        return lax.rem(y + dy, 4) * 4 + lax.rem(xh + dx, 2) * 2 + lax.rem(core + dk, 2)

    seq_peers = [seat_at(*step) for step in SEQ_STEPS]
    chip_peers = seq_peers[0:14:2]
    head_peers = [lax.rem(mine + j, 16) for j in range(1, 16)]

    barrier = pltpu.get_barrier_semaphore()
    for peer in seq_peers:
        pl.semaphore_signal(barrier, inc=1, device_id={"seq": peer}, device_id_type=MESH)
    for peer in head_peers:
        pl.semaphore_signal(barrier, inc=1, device_id={"head": peer}, device_id_type=MESH)

    loads = []

    def load(src, dst):
        copy = pltpu.make_async_copy(src, dst, load_sems.at[len(loads)])
        loads.append(copy)
        copy.start()
        return copy

    got_lengths = load(lengths_hbm, lengths)
    got_nope = load(nope_hbm, nope)
    got_rope = load(rope_hbm, rope)
    got_key = load(key_hbm, key_weight)
    got_parents = load(parents_hbm, parents)
    got_draft = load(draft_hbm, draft)
    got_cache = [load(cache_hbm.at[b], kbuf.at[b]) for b in range(REQUESTS)]
    got_value = load(value_hbm, value_weight)
    got_out = load(out_hbm, out_weight.at[core])
    got_residual = [
        load(
            residual_hbm.at[pl.ds(pl.multiple_of(b * DRAFT + core * HALF, HALF), HALF), :],
            residual.at[core, pl.ds(b * HALF, HALF), :],
        )
        for b in range(REQUESTS)
    ]
    got_gain = load(gain_hbm, gain)

    got_vocab = []
    for slot, (dy, dx) in enumerate(CHIP_STEPS + [(0, 0)]):
        owner = lax.div(seat_at(dy, dx, 0), 2)
        columns = pl.ds(pl.multiple_of(owner * 512, 512), 512)
        copy = pltpu.make_async_copy(
            vocab_hbm.at[:, columns], vocab.at[core, slot], vocab_sems.at[slot]
        )
        copy.start()
        got_vocab.append(copy)

    got_parents.wait()
    row = lax.broadcasted_iota(jnp.int32, (DRAFT, DRAFT), 0)
    column = lax.broadcasted_iota(jnp.int32, (DRAFT, DRAFT), 1)
    reaches = [
        jnp.where((parents[b : b + 1, :] == row) | (row == column), 1.0, 0.0).astype(BF16)
        for b in range(REQUESTS)
    ]
    for _ in range(6):
        reaches = [jnp.where(dot(r, r) > 0.5, 1.0, 0.0).astype(BF16) for r in reaches]
    row = lax.broadcasted_iota(jnp.int32, (DRAFT, EXTRA), 0)
    column = lax.broadcasted_iota(jnp.int32, (DRAFT, EXTRA), 1)
    tree_bias = []
    for b in range(REQUESTS):
        chosen = (column >= 4 * b) & (column < 4 * b + 4) & (row == seat * 4 + column - 4 * b)
        chosen = jnp.where(chosen, 1.0, 0.0).astype(BF16)
        reached = lax.dot_general(
            reaches[b], chosen, (((0,), (0,)), ((), ())), preferred_element_type=F32
        )
        tree_bias.append(jnp.where(reached > 0.5, 0.0, NEGATIVE))
    got_draft.wait()
    dbuf[...] = jnp.zeros((EXTRA, WIDTH), BF16)
    dbuf[0:8, :] = jnp.concatenate([draft[b].astype(F32) for b in range(REQUESTS)], axis=0).astype(BF16)

    got_nope.wait()
    nope32[...] = nope[...].astype(F32)
    got_rope.wait()
    rope32[...] = rope[...].astype(F32)
    got_key.wait()
    for h in range(HEADS):
        picked = nope32[pl.ds(h, TOKENS, stride=HEADS), :].astype(BF16)
        absorbed = dot(picked, key_weight[h]).astype(BF16)
        turned = rope32[pl.ds(h, TOKENS, stride=HEADS), :].astype(BF16)
        for b in range(REQUESTS):
            rows = pl.ds(h * DRAFT, DRAFT)
            qbuf[b, rows, 0:LATENT] = absorbed[b * DRAFT : (b + 1) * DRAFT]
            qbuf[b, rows, LATENT:WIDTH] = turned[b * DRAFT : (b + 1) * DRAFT]

    scale = math.log2(math.e) / math.sqrt(192.0)
    lane = lax.broadcasted_iota(jnp.int32, (DRAFT, 128), 1)
    position = seat * KEYS + lax.broadcasted_iota(jnp.int32, (1, KEYS), 1)
    o_copies, ml_copies, own_copies, swap_copies = [], [], [], []
    partner = seq_peers[14]

    def score(b):
        got_cache[b].wait()
        live_bias = jnp.where(position < lengths[b], 0.0, NEGATIVE)
        tree = jnp.concatenate([tree_bias[b]] * HEADS, axis=0)
        return dot(qbuf[b], kbuf[b]) + live_bias, nt_dot(qbuf[b], dbuf[...]) + tree

    got_lengths.wait()
    got_value.wait()
    scores = [score(0), score(1)]
    for b in range(REQUESTS):
        tops = jnp.zeros((DRAFT, 128), F32)
        totals = jnp.zeros((DRAFT, 128), F32)
        cached, drafted = scores[b]
        top = jnp.maximum(
            jnp.max(cached, -1, keepdims=True), jnp.max(drafted, -1, keepdims=True)
        )
        cached = jnp.exp2((cached - top) * scale)
        drafted = jnp.exp2((drafted - top) * scale)
        total = jnp.sum(cached, -1, keepdims=True) + jnp.sum(drafted, -1, keepdims=True)
        mixed = nt_dot(cached.astype(BF16), kbuf[b, 0:LATENT, :])
        mixed = (mixed + dot(drafted.astype(BF16), dbuf[:, 0:LATENT])).astype(BF16)
        for h in range(HEADS):
            sub = slice(h * DRAFT, (h + 1) * DRAFT)
            o_send[b, h] = dot(mixed[sub], value_weight[h]).astype(BF16)
            tops = jnp.where(lane == h, top[sub] * scale, tops)
            totals = jnp.where(lane == h, total[sub], totals)
        turned = jnp.concatenate([tops, totals], axis=0).T
        for h in range(HEADS):
            ml_send[b, h] = turned[h : h + 1]
        if b == 0:
            pl.semaphore_wait(barrier, 30)
        for j, step in enumerate(SEQ_STEPS):
            peer = seq_peers[j]
            there, their_core = lax.div(peer, 2), lax.rem(peer, 2)
            half = pl.ds(pl.multiple_of(their_core * 32, 32), 32)
            copy = pltpu.make_async_remote_copy(
                o_send.at[b, there, half, :],
                o_recv.at[b, j],
                o_sems.at[0, b, j],
                o_sems.at[1, b, j],
                device_id={"seq": peer},
                device_id_type=MESH,
            )
            copy.start()
            o_copies.append(copy)
            copy = pltpu.make_async_remote_copy(
                ml_send.at[b, there],
                ml_recv.at[b, j],
                ml_sems.at[0, b, j],
                ml_sems.at[1, b, j],
                device_id={"seq": peer},
                device_id_type=MESH,
            )
            copy.start()
            ml_copies.append(copy)
        swaps = []
        if b == 0:
            got_out.wait()
            got_gain.wait()
            gain_rows[core] = gain[...].astype(F32)[None, :]
            swaps.append((out_weight.at[core], out_weight.at[core], 0))
            swaps.append((gain_rows.at[core], gain_rows.at[core], 1))
            for request in range(REQUESTS):
                other_rows = pl.multiple_of(request * DRAFT + (1 - core) * HALF, HALF)
                swaps.append(
                    (
                        residual_hbm.at[pl.ds(other_rows, HALF), :],
                        residual.at[core, pl.ds(request * HALF, HALF), :],
                        2 + request,
                    )
                )
        else:
            for slot in range(8):
                got_vocab[slot].wait()
                swaps.append((vocab.at[core, slot], vocab.at[core, slot], 4 + slot))
        for src, dst, k in swaps:
            copy = pltpu.make_async_remote_copy(
                src,
                dst,
                swap_sems.at[0, k],
                swap_sems.at[1, k],
                device_id={"seq": partner},
                device_id_type=MESH,
            )
            copy.start()
            swap_copies.append(copy)
        half = pl.ds(pl.multiple_of(core * 32, 32), 32)
        for k, (src, dst) in enumerate(
            ((o_send.at[b, chip, half, :], o_recv.at[b, 15]), (ml_send.at[b, chip], ml_recv.at[b, 15]))
        ):
            copy = pltpu.make_async_copy(src, dst, local_sems.at[b, k])
            copy.start()
            own_copies.append(copy)

    g_copies = []
    for b in range(REQUESTS):
        for copy in ml_copies[b * 15 : (b + 1) * 15]:
            copy.wait_recv()
        for copy in own_copies[b * 2 : (b + 1) * 2]:
            copy.wait()
        gathered = jnp.concatenate(
            [ml_recv[b, j] for j in range(16)] + [jnp.full((112, 128), NEGATIVE, F32)], axis=0
        ).T
        tops, totals = gathered[:DRAFT], gathered[DRAFT:]
        shares = jnp.exp2(tops - jnp.max(tops, -1, keepdims=True))
        shares = shares / jnp.sum(shares * totals, -1, keepdims=True)
        shares = jnp.where(core == 0, shares[:32], shares[32:])
        for copy in o_copies[b * 15 : (b + 1) * 15]:
            copy.wait_recv()
        summed = jnp.zeros((32, 128), F32)
        for j in range(16):
            summed = summed + shares[:, j : j + 1] * o_recv[b, j].astype(F32)
        g_send[b] = summed.astype(BF16)
        place = g_full.at[
            pl.ds(b * HALF, HALF),
            pl.ds(pl.multiple_of(chip * 128, 128), 128),
        ]
        for j, peer in enumerate(chip_peers):
            copy = pltpu.make_async_remote_copy(
                g_send.at[b],
                place,
                g_sems.at[0, b, j],
                g_sems.at[1, b, j],
                device_id={"seq": peer},
                device_id_type=MESH,
            )
            copy.start()
            g_copies.append(copy)
        copy = pltpu.make_async_copy(g_send.at[b], place, local_sems.at[b, 2])
        copy.start()
        own_copies.append(copy)

    for copy in own_copies[4:]:
        copy.wait()
    swap_copies[0].wait_recv()
    for copy in g_copies:
        copy.wait_recv()
    for side in range(2):
        attention = nt_dot(g_full[...], out_weight[side]).astype(BF16)
        for i in range(8):
            a_send[2 * i + side] = attention[i * 8 : (i + 1) * 8]
    a_copies = []
    for j, peer in enumerate(head_peers):
        copy = pltpu.make_async_remote_copy(
            a_send.at[peer],
            a_recv.at[j],
            a_sems.at[0, j],
            a_sems.at[1, j],
            device_id={"head": peer},
            device_id_type=MESH,
        )
        copy.start()
        a_copies.append(copy)
    summed = a_send[mine].astype(F32)
    for j, copy in enumerate(a_copies):
        copy.wait_recv()
        summed = summed + a_recv[j].astype(F32)
    b_send[...] = summed.astype(BF16)
    b_copies = []
    for j, peer in enumerate(head_peers):
        copy = pltpu.make_async_remote_copy(
            b_send,
            b_full.at[mine],
            b_sems.at[0, j],
            b_sems.at[1, j],
            device_id={"head": peer},
            device_id_type=MESH,
        )
        copy.start()
        b_copies.append(copy)
    b_full[mine] = b_send[...]
    for copy in got_residual:
        copy.wait()
    for copy in swap_copies[1:4]:
        copy.wait_recv()
    for copy in b_copies:
        copy.wait_recv()
    squares = jnp.zeros((2 * HALF, 1), F32)
    scaled = []
    for side in range(2):
        attention = jnp.concatenate(
            [b_full[2 * i + side].astype(F32) for i in range(8)], axis=0
        )
        hidden = residual[side].astype(F32) + attention
        squares = squares + jnp.sum(hidden * hidden, -1, keepdims=True)
        scaled.append((hidden * gain_rows[side]).astype(BF16))

    s_send[...] = jnp.broadcast_to(jnp.concatenate([squares] * 2, axis=0), (TOKENS, 128)).T[0:1]
    s_copies = []
    for j, peer in enumerate(seq_peers):
        copy = pltpu.make_async_remote_copy(
            s_send,
            s_recv.at[j],
            s_sems.at[0, j],
            s_sems.at[1, j],
            device_id={"seq": peer},
            device_id_type=MESH,
        )
        copy.start()
        s_copies.append(copy)
    l_copies = []
    for slot in range(8):
        swap_copies[4 + slot].wait_recv()
        part = dot(scaled[0], vocab[0, slot]) + dot(scaled[1], vocab[1, slot])
        for side in range(2):
            l_send[slot, side] = part[:, side * 256 : (side + 1) * 256].astype(BF16)
        for dk in range(2):
            j = 2 * slot + dk
            if slot == 7:
                if dk == 0:
                    continue
                j = 14
            copy = pltpu.make_async_remote_copy(
                l_send.at[slot, lax.rem(core + dk, 2)],
                l_recv.at[j],
                l_sems.at[0, j],
                l_sems.at[1, j],
                device_id={"seq": seq_peers[j]},
                device_id_type=MESH,
            )
            copy.start()
            l_copies.append(copy)
    sums = [l_send[7, core].astype(F32), jnp.zeros((2 * HALF, 256), F32)]
    squares = [s_send[...], jnp.zeros((1, TOKENS), F32)]
    for j, (_, _, dk) in enumerate(SEQ_STEPS):
        s_copies[j].wait_recv()
        squares[dk] = squares[dk] + s_recv[j]
    for j, (_, _, dk) in enumerate(SEQ_STEPS):
        l_copies[j].wait_recv()
        sums[dk] = sums[dk] + l_recv[j].astype(F32)
    for dk in range(2):
        scales = jnp.broadcast_to(
            lax.rsqrt(squares[dk] / model_width + EPSILON), (128, TOKENS)
        ).T
        done = (sums[dk] * scales[: 2 * HALF, 0:1]).astype(BF16)
        owner = lax.rem(core + dk, 2)
        for b in range(REQUESTS):
            rows = pl.ds(pl.multiple_of(b * DRAFT + owner * HALF, HALF), HALF)
            logits[rows, :] = done[b * HALF : (b + 1) * HALF]
    for copy in o_copies + ml_copies + swap_copies + g_copies + a_copies + b_copies + s_copies + l_copies:
        copy.wait_send()


def per_device(
    latent_cache,
    draft_latent,
    query_nope,
    query_rope,
    parents,
    lengths,
    key_weight,
    value_weight,
    out_weight,
    residual,
    norm_gain,
    vocab_weight,
):
    local_width = residual.shape[2]
    model_width = local_width * lax.axis_size("seq")
    operands = [
        lengths,
        parents,
        jnp.swapaxes(latent_cache, 1, 2),
        draft_latent,
        query_nope.reshape(TOKENS * HEADS, 128),
        query_rope.reshape(TOKENS * HEADS, ROPE),
        key_weight,
        value_weight,
        out_weight.T,
        residual.reshape(TOKENS, local_width),
        norm_gain,
        vocab_weight,
    ]
    hbm = pl.BlockSpec(memory_space=pltpu.HBM)
    dma = pltpu.SemaphoreType.DMA
    logits = pl.pallas_call(
        functools.partial(kernel, model_width),
        out_shape=jax.ShapeDtypeStruct((TOKENS, 256), BF16),
        in_specs=[hbm] * 12,
        out_specs=pl.BlockSpec(memory_space=pltpu.VMEM),
        scratch_shapes=[
            pltpu.SMEM((REQUESTS,), jnp.int32),
            pltpu.VMEM((REQUESTS, DRAFT), jnp.int32),
            pltpu.VMEM((REQUESTS, WIDTH, KEYS), BF16),
            pltpu.VMEM((REQUESTS, 4, WIDTH), BF16),
            pltpu.VMEM((EXTRA, WIDTH), BF16),
            pltpu.VMEM((TOKENS * HEADS, 128), BF16),
            pltpu.VMEM((TOKENS * HEADS, ROPE), BF16),
            pltpu.VMEM((HEADS, 128, LATENT), BF16),
            pltpu.VMEM((HEADS, LATENT, 128), BF16),
            pltpu.VMEM((2, local_width, 1024), BF16),
            pltpu.VMEM((2, 2 * HALF, local_width), BF16),
            pltpu.VMEM((local_width,), BF16),
            pltpu.VMEM((2, 1, local_width), F32),
            pltpu.VMEM((2, 8, local_width, 512), BF16),
            pltpu.VMEM((TOKENS * HEADS, 128), F32),
            pltpu.VMEM((TOKENS * HEADS, ROPE), F32),
            pltpu.VMEM((REQUESTS, HEADS * DRAFT, WIDTH), BF16),
            pltpu.VMEM((REQUESTS, HEADS, DRAFT, 128), BF16),
            pltpu.VMEM((REQUESTS, 16, 32, 128), BF16),
            pltpu.VMEM((REQUESTS, HEADS, 1, 128), F32),
            pltpu.VMEM((REQUESTS, 16, 1, 128), F32),
            pltpu.VMEM((REQUESTS, 32, 128), BF16),
            pltpu.VMEM((2 * HALF, 1024), BF16),
            pltpu.VMEM((16, 8, local_width), BF16),
            pltpu.VMEM((15, 8, local_width), BF16),
            pltpu.VMEM((8, local_width), BF16),
            pltpu.VMEM((16, 8, local_width), BF16),
            pltpu.VMEM((1, TOKENS), F32),
            pltpu.VMEM((15, 1, TOKENS), F32),
            pltpu.VMEM((8, 2, 2 * HALF, 256), BF16),
            pltpu.VMEM((15, 2 * HALF, 256), BF16),
            dma((16,)),
            dma((8,)),
            dma((REQUESTS, 3)),
            dma((2, REQUESTS, 15)),
            dma((2, REQUESTS, 15)),
            dma((2, REQUESTS, 7)),
            dma((2, 15)),
            dma((2, 15)),
            dma((2, 15)),
            dma((2, 12)),
            dma((2, 15)),
        ],
        compiler_params=pltpu.CompilerParams(
            collective_id=0, has_side_effects=True, vmem_limit_bytes=48 * 1024 * 1024
        ),
    )(
        *[pltpu.with_memory_space_constraint(a, pltpu.HBM) for a in operands],
    )
    return logits.reshape(REQUESTS, DRAFT, 256)


def solution(mesh):
    in_specs = (
        P(None, "seq", None),
        P(None, "seq", None),
        P(None, None, "head", None),
        P(None, None, "head", None),
        P(),
        P(),
        P("head", None, None),
        P("head", None, None),
        P("head", "seq"),
        P(None, None, "seq"),
        P("seq"),
        P("seq", "head"),
    )
    out_specs = P(None, None, ("head", "seq"))
    return jax.shard_map(
        per_device, mesh=mesh, in_specs=in_specs, out_specs=out_specs, check_vma=False
    )
```

```python
import functools
import math

import jax
import jax.numpy as jnp
from jax import lax
from jax.experimental import pallas as pl
from jax.experimental.pallas import tpu as pltpu
from jax.sharding import PartitionSpec as P

MESH = pl.DeviceIdType.MESH
NEGATIVE = -1e30
EPSILON = 1e-06
F32 = jnp.float32
BF16 = jnp.bfloat16

CHIP_STEPS = [(2, 1), (1, 1), (3, 1), (2, 0), (0, 1), (1, 0), (3, 0)]
SEQ_STEPS = [(dy, dx, dk) for dy, dx in CHIP_STEPS for dk in (0, 1)] + [(0, 0, 1)]
REQUESTS, DRAFT, HEADS, LATENT, ROPE, WIDTH = 2, 64, 8, 512, 64, 576
TOKENS = REQUESTS * DRAFT
KEYS, EXTRA = 2048, 128
HALF = DRAFT // 2


def nt_dot(a, b):
    return lax.dot_general(a, b, (((1,), (1,)), ((), ())), preferred_element_type=F32)


def dot(a, b):
    return jnp.dot(a, b, preferred_element_type=F32)


def kernel(
    model_width,
    lengths_hbm,
    parents_hbm,
    cache_hbm,
    draft_hbm,
    nope_hbm,
    rope_hbm,
    key_hbm,
    value_hbm,
    out_hbm,
    residual_hbm,
    gain_hbm,
    vocab_hbm,
    logits,
    lengths,
    parents,
    kbuf,
    draft,
    dbuf,
    nope,
    rope,
    key_weight,
    value_weight,
    out_weight,
    residual,
    gain,
    gain_rows,
    vocab,
    nope32,
    rope32,
    qbuf,
    o_send,
    o_recv,
    ml_send,
    ml_recv,
    g_send,
    g_full,
    a_send,
    a_recv,
    b_send,
    b_full,
    s_send,
    s_recv,
    l_send,
    l_recv,
    load_sems,
    vocab_sems,
    local_sems,
    o_sems,
    ml_sems,
    g_sems,
    a_sems,
    b_sems,
    s_sems,
    swap_sems,
    l_sems,
):
    seat = lax.axis_index("seq")
    mine = lax.axis_index("head")
    y = lax.div(seat, 4)
    xh = lax.rem(lax.div(seat, 2), 2)
    core = lax.rem(seat, 2)
    chip = lax.div(seat, 2)

    def seat_at(dy, dx, dk):
        return lax.rem(y + dy, 4) * 4 + lax.rem(xh + dx, 2) * 2 + lax.rem(core + dk, 2)

    seq_peers = [seat_at(*step) for step in SEQ_STEPS]
    chip_peers = seq_peers[0:14:2]
    head_peers = [lax.rem(mine + j, 16) for j in range(1, 16)]

    barrier = pltpu.get_barrier_semaphore()
    for peer in seq_peers:
        pl.semaphore_signal(barrier, inc=1, device_id={"seq": peer}, device_id_type=MESH)
    for peer in head_peers:
        pl.semaphore_signal(barrier, inc=1, device_id={"head": peer}, device_id_type=MESH)

    loads = []

    def load(src, dst):
        copy = pltpu.make_async_copy(src, dst, load_sems.at[len(loads)])
        loads.append(copy)
        copy.start()
        return copy

    got_lengths = load(lengths_hbm, lengths)
    got_nope = load(nope_hbm, nope)
    got_rope = load(rope_hbm, rope)
    got_key = load(key_hbm, key_weight)
    got_parents = load(parents_hbm, parents)
    got_draft = load(draft_hbm, draft)
    got_cache = [load(cache_hbm.at[b], kbuf.at[b]) for b in range(REQUESTS)]
    got_value = load(value_hbm, value_weight)
    got_out = load(out_hbm, out_weight.at[core])
    got_residual = [
        load(
            residual_hbm.at[pl.ds(pl.multiple_of(b * DRAFT + core * HALF, HALF), HALF), :],
            residual.at[core, pl.ds(b * HALF, HALF), :],
        )
        for b in range(REQUESTS)
    ]
    got_gain = load(gain_hbm, gain)

    got_vocab = []
    for slot, (dy, dx) in enumerate(CHIP_STEPS + [(0, 0)]):
        owner = lax.div(seat_at(dy, dx, 0), 2)
        columns = pl.ds(pl.multiple_of(owner * 512, 512), 512)
        copy = pltpu.make_async_copy(
            vocab_hbm.at[:, columns], vocab.at[core, slot], vocab_sems.at[slot]
        )
        copy.start()
        got_vocab.append(copy)

    got_parents.wait()
    row = lax.broadcasted_iota(jnp.int32, (DRAFT, DRAFT), 0)
    column = lax.broadcasted_iota(jnp.int32, (DRAFT, DRAFT), 1)
    reaches = [
        jnp.where((parents[b : b + 1, :] == row) | (row == column), 1.0, 0.0).astype(BF16)
        for b in range(REQUESTS)
    ]
    for _ in range(6):
        reaches = [jnp.where(dot(r, r) > 0.5, 1.0, 0.0).astype(BF16) for r in reaches]
    row = lax.broadcasted_iota(jnp.int32, (DRAFT, EXTRA), 0)
    column = lax.broadcasted_iota(jnp.int32, (DRAFT, EXTRA), 1)
    tree_bias = []
    for b in range(REQUESTS):
        chosen = (column >= 4 * b) & (column < 4 * b + 4) & (row == seat * 4 + column - 4 * b)
        chosen = jnp.where(chosen, 1.0, 0.0).astype(BF16)
        reached = lax.dot_general(
            reaches[b], chosen, (((0,), (0,)), ((), ())), preferred_element_type=F32
        )
        tree_bias.append(jnp.where(reached > 0.5, 0.0, NEGATIVE))
    got_draft.wait()
    dbuf[...] = jnp.zeros((EXTRA, WIDTH), BF16)
    dbuf[0:8, :] = jnp.concatenate([draft[b].astype(F32) for b in range(REQUESTS)], axis=0).astype(BF16)

    got_nope.wait()
    nope32[...] = nope[...].astype(F32)
    got_rope.wait()
    rope32[...] = rope[...].astype(F32)
    got_key.wait()
    for h in range(HEADS):
        picked = nope32[pl.ds(h, TOKENS, stride=HEADS), :].astype(BF16)
        absorbed = dot(picked, key_weight[h]).astype(BF16)
        turned = rope32[pl.ds(h, TOKENS, stride=HEADS), :].astype(BF16)
        for b in range(REQUESTS):
            rows = pl.ds(h * DRAFT, DRAFT)
            qbuf[b, rows, 0:LATENT] = absorbed[b * DRAFT : (b + 1) * DRAFT]
            qbuf[b, rows, LATENT:WIDTH] = turned[b * DRAFT : (b + 1) * DRAFT]

    scale = math.log2(math.e) / math.sqrt(192.0)
    lane = lax.broadcasted_iota(jnp.int32, (DRAFT, 128), 1)
    position = seat * KEYS + lax.broadcasted_iota(jnp.int32, (1, KEYS), 1)
    o_copies, ml_copies, own_copies, swap_copies = [], [], [], []
    partner = seq_peers[14]

    def score(b):
        got_cache[b].wait()
        live_bias = jnp.where(position < lengths[b], 0.0, NEGATIVE)
        tree = jnp.concatenate([tree_bias[b]] * HEADS, axis=0)
        return dot(qbuf[b], kbuf[b]) + live_bias, nt_dot(qbuf[b], dbuf[...]) + tree

    got_lengths.wait()
    got_value.wait()
    scores = [score(0), score(1)]
    for b in range(REQUESTS):
        tops = jnp.zeros((DRAFT, 128), F32)
        totals = jnp.zeros((DRAFT, 128), F32)
        cached, drafted = scores[b]
        top = jnp.maximum(
            jnp.max(cached, -1, keepdims=True), jnp.max(drafted, -1, keepdims=True)
        )
        cached = jnp.exp2((cached - top) * scale)
        drafted = jnp.exp2((drafted - top) * scale)
        total = jnp.sum(cached, -1, keepdims=True) + jnp.sum(drafted, -1, keepdims=True)
        mixed = nt_dot(cached.astype(BF16), kbuf[b, 0:LATENT, :])
        mixed = (mixed + dot(drafted.astype(BF16), dbuf[:, 0:LATENT])).astype(BF16)
        for h in range(HEADS):
            sub = slice(h * DRAFT, (h + 1) * DRAFT)
            o_send[b, h] = dot(mixed[sub], value_weight[h]).astype(BF16)
            tops = jnp.where(lane == h, top[sub] * scale, tops)
            totals = jnp.where(lane == h, total[sub], totals)
        turned = jnp.concatenate([tops, totals], axis=0).T
        for h in range(HEADS):
            ml_send[b, h] = turned[h : h + 1]
        if b == 0:
            pl.semaphore_wait(barrier, 30)
        for j, step in enumerate(SEQ_STEPS):
            peer = seq_peers[j]
            there, their_core = lax.div(peer, 2), lax.rem(peer, 2)
            half = pl.ds(pl.multiple_of(their_core * 32, 32), 32)
            copy = pltpu.make_async_remote_copy(
                o_send.at[b, there, half, :],
                o_recv.at[b, j],
                o_sems.at[0, b, j],
                o_sems.at[1, b, j],
                device_id={"seq": peer},
                device_id_type=MESH,
            )
            copy.start()
            o_copies.append(copy)
            copy = pltpu.make_async_remote_copy(
                ml_send.at[b, there],
                ml_recv.at[b, j],
                ml_sems.at[0, b, j],
                ml_sems.at[1, b, j],
                device_id={"seq": peer},
                device_id_type=MESH,
            )
            copy.start()
            ml_copies.append(copy)
        swaps = []
        if b == 0:
            got_out.wait()
            got_gain.wait()
            gain_rows[core] = gain[...].astype(F32)[None, :]
            swaps.append((out_weight.at[core], out_weight.at[core], 0))
            swaps.append((gain_rows.at[core], gain_rows.at[core], 1))
            for request in range(REQUESTS):
                other_rows = pl.multiple_of(request * DRAFT + (1 - core) * HALF, HALF)
                swaps.append(
                    (
                        residual_hbm.at[pl.ds(other_rows, HALF), :],
                        residual.at[core, pl.ds(request * HALF, HALF), :],
                        2 + request,
                    )
                )
        else:
            for slot in range(8):
                got_vocab[slot].wait()
                swaps.append((vocab.at[core, slot], vocab.at[core, slot], 4 + slot))
        for src, dst, k in swaps:
            copy = pltpu.make_async_remote_copy(
                src,
                dst,
                swap_sems.at[0, k],
                swap_sems.at[1, k],
                device_id={"seq": partner},
                device_id_type=MESH,
            )
            copy.start()
            swap_copies.append(copy)
        half = pl.ds(pl.multiple_of(core * 32, 32), 32)
        for k, (src, dst) in enumerate(
            ((o_send.at[b, chip, half, :], o_recv.at[b, 15]), (ml_send.at[b, chip], ml_recv.at[b, 15]))
        ):
            copy = pltpu.make_async_copy(src, dst, local_sems.at[b, k])
            copy.start()
            own_copies.append(copy)

    g_copies = []
    for b in range(REQUESTS):
        for copy in ml_copies[b * 15 : (b + 1) * 15]:
            copy.wait_recv()
        for copy in own_copies[b * 2 : (b + 1) * 2]:
            copy.wait()
        gathered = jnp.concatenate(
            [ml_recv[b, j] for j in range(16)] + [jnp.full((112, 128), NEGATIVE, F32)], axis=0
        ).T
        tops, totals = gathered[:DRAFT], gathered[DRAFT:]
        shares = jnp.exp2(tops - jnp.max(tops, -1, keepdims=True))
        shares = shares / jnp.sum(shares * totals, -1, keepdims=True)
        shares = jnp.where(core == 0, shares[:32], shares[32:])
        for copy in o_copies[b * 15 : (b + 1) * 15]:
            copy.wait_recv()
        summed = jnp.zeros((32, 128), F32)
        for j in range(16):
            summed = summed + shares[:, j : j + 1] * o_recv[b, j].astype(F32)
        g_send[b] = summed.astype(BF16)
        place = g_full.at[b, :, pl.ds(pl.multiple_of(chip * 128, 128), 128)]
        for j, peer in enumerate(chip_peers):
            copy = pltpu.make_async_remote_copy(
                g_send.at[b],
                place,
                g_sems.at[0, b, j],
                g_sems.at[1, b, j],
                device_id={"seq": peer},
                device_id_type=MESH,
            )
            copy.start()
            g_copies.append(copy)
        copy = pltpu.make_async_copy(g_send.at[b], place, local_sems.at[b, 2])
        copy.start()
        own_copies.append(copy)

    a_copies, b_copies = [], []
    for b in range(REQUESTS):
        own_copies[4 + b].wait()
        if b == 0:
            swap_copies[0].wait_recv()
        for copy in g_copies[b * 7 : (b + 1) * 7]:
            copy.wait_recv()
        for side in range(2):
            attention = nt_dot(g_full[b], out_weight[side])
            for i in range(8):
                a_send[b, 2 * i + side] = attention[i * 4 : (i + 1) * 4].astype(BF16)
        for j, peer in enumerate(head_peers):
            copy = pltpu.make_async_remote_copy(
                a_send.at[b, peer],
                a_recv.at[b, j],
                a_sems.at[0, b, j],
                a_sems.at[1, b, j],
                device_id={"head": peer},
                device_id_type=MESH,
            )
            copy.start()
            a_copies.append(copy)
    for b in range(REQUESTS):
        summed = a_send[b, mine].astype(F32)
        for j in range(15):
            a_copies[b * 15 + j].wait_recv()
            summed = summed + a_recv[b, j].astype(F32)
        b_send[b] = summed.astype(BF16)
        for j, peer in enumerate(head_peers):
            copy = pltpu.make_async_remote_copy(
                b_send.at[b],
                b_full.at[b, mine],
                b_sems.at[0, b, j],
                b_sems.at[1, b, j],
                device_id={"head": peer},
                device_id_type=MESH,
            )
            copy.start()
            b_copies.append(copy)
        b_full[b, mine] = b_send[b]

    for copy in got_residual:
        copy.wait()
    for copy in swap_copies[1:4]:
        copy.wait_recv()
    square_parts, l_copies = [], []
    for b in range(REQUESTS):
        for copy in b_copies[b * 15 : (b + 1) * 15]:
            copy.wait_recv()
        squares = jnp.zeros((HALF, 1), F32)
        scaled = []
        for side in range(2):
            attention = jnp.concatenate(
                [b_full[b, 2 * i + side].astype(F32) for i in range(8)], axis=0
            )
            hidden = residual[side, b * HALF : (b + 1) * HALF].astype(F32) + attention
            squares = squares + jnp.sum(hidden * hidden, -1, keepdims=True)
            scaled.append((hidden * gain_rows[side]).astype(BF16))
        square_parts.append(squares)
        if b == 1:
            squares = jnp.concatenate(square_parts * 2, axis=0)
            s_send[...] = jnp.broadcast_to(squares, (TOKENS, 128)).T[0:1]
            s_copies = []
            for j, peer in enumerate(seq_peers):
                copy = pltpu.make_async_remote_copy(
                    s_send,
                    s_recv.at[j],
                    s_sems.at[0, j],
                    s_sems.at[1, j],
                    device_id={"seq": peer},
                    device_id_type=MESH,
                )
                copy.start()
                s_copies.append(copy)
        for slot in range(8):
            if b == 0:
                swap_copies[4 + slot].wait_recv()
            part = dot(scaled[0], vocab[0, slot]) + dot(scaled[1], vocab[1, slot])
            for side in range(2):
                l_send[b, slot, side] = part[:, side * 256 : (side + 1) * 256].astype(BF16)
            for dk in range(2):
                j = 2 * slot + dk
                if slot == 7:
                    if dk == 0:
                        continue
                    j = 14
                copy = pltpu.make_async_remote_copy(
                    l_send.at[b, slot, lax.rem(core + dk, 2)],
                    l_recv.at[b, j],
                    l_sems.at[0, b, j],
                    l_sems.at[1, b, j],
                    device_id={"seq": seq_peers[j]},
                    device_id_type=MESH,
                )
                copy.start()
                l_copies.append(copy)
    squares = [s_send[...], jnp.zeros((1, TOKENS), F32)]
    for j, (_, _, dk) in enumerate(SEQ_STEPS):
        s_copies[j].wait_recv()
        squares[dk] = squares[dk] + s_recv[j]
    scales = [
        jnp.broadcast_to(lax.rsqrt(total / model_width + EPSILON), (128, TOKENS)).T
        for total in squares
    ]
    for b in range(REQUESTS):
        sums = [l_send[b, 7, core].astype(F32), jnp.zeros((HALF, 256), F32)]
        for j, (_, _, dk) in enumerate(SEQ_STEPS):
            l_copies[b * 15 + j].wait_recv()
            sums[dk] = sums[dk] + l_recv[b, j].astype(F32)
        for dk in range(2):
            owner = lax.rem(core + dk, 2)
            rows = pl.ds(pl.multiple_of(b * DRAFT + owner * HALF, HALF), HALF)
            logits[rows, :] = (sums[dk] * scales[dk][b * HALF : (b + 1) * HALF, 0:1]).astype(BF16)
    for copy in o_copies + ml_copies + swap_copies + g_copies + a_copies + b_copies + s_copies + l_copies:
        copy.wait_send()


def per_device(
    latent_cache,
    draft_latent,
    query_nope,
    query_rope,
    parents,
    lengths,
    key_weight,
    value_weight,
    out_weight,
    residual,
    norm_gain,
    vocab_weight,
):
    local_width = residual.shape[2]
    model_width = local_width * lax.axis_size("seq")
    operands = [
        lengths,
        parents,
        jnp.swapaxes(latent_cache, 1, 2),
        draft_latent,
        query_nope.reshape(TOKENS * HEADS, 128),
        query_rope.reshape(TOKENS * HEADS, ROPE),
        key_weight,
        value_weight,
        out_weight.T,
        residual.reshape(TOKENS, local_width),
        norm_gain,
        vocab_weight,
    ]
    hbm = pl.BlockSpec(memory_space=pltpu.HBM)
    dma = pltpu.SemaphoreType.DMA
    logits = pl.pallas_call(
        functools.partial(kernel, model_width),
        out_shape=jax.ShapeDtypeStruct((TOKENS, 256), BF16),
        in_specs=[hbm] * 12,
        out_specs=pl.BlockSpec(memory_space=pltpu.VMEM),
        scratch_shapes=[
            pltpu.SMEM((REQUESTS,), jnp.int32),
            pltpu.VMEM((REQUESTS, DRAFT), jnp.int32),
            pltpu.VMEM((REQUESTS, WIDTH, KEYS), BF16),
            pltpu.VMEM((REQUESTS, 4, WIDTH), BF16),
            pltpu.VMEM((EXTRA, WIDTH), BF16),
            pltpu.VMEM((TOKENS * HEADS, 128), BF16),
            pltpu.VMEM((TOKENS * HEADS, ROPE), BF16),
            pltpu.VMEM((HEADS, 128, LATENT), BF16),
            pltpu.VMEM((HEADS, LATENT, 128), BF16),
            pltpu.VMEM((2, local_width, 1024), BF16),
            pltpu.VMEM((2, 2 * HALF, local_width), BF16),
            pltpu.VMEM((local_width,), BF16),
            pltpu.VMEM((2, 1, local_width), F32),
            pltpu.VMEM((2, 8, local_width, 512), BF16),
            pltpu.VMEM((TOKENS * HEADS, 128), F32),
            pltpu.VMEM((TOKENS * HEADS, ROPE), F32),
            pltpu.VMEM((REQUESTS, HEADS * DRAFT, WIDTH), BF16),
            pltpu.VMEM((REQUESTS, HEADS, DRAFT, 128), BF16),
            pltpu.VMEM((REQUESTS, 16, 32, 128), BF16),
            pltpu.VMEM((REQUESTS, HEADS, 1, 128), F32),
            pltpu.VMEM((REQUESTS, 16, 1, 128), F32),
            pltpu.VMEM((REQUESTS, 32, 128), BF16),
            pltpu.VMEM((REQUESTS, HALF, 1024), BF16),
            pltpu.VMEM((REQUESTS, 16, 4, local_width), BF16),
            pltpu.VMEM((REQUESTS, 15, 4, local_width), BF16),
            pltpu.VMEM((REQUESTS, 4, local_width), BF16),
            pltpu.VMEM((REQUESTS, 16, 4, local_width), BF16),
            pltpu.VMEM((1, TOKENS), F32),
            pltpu.VMEM((15, 1, TOKENS), F32),
            pltpu.VMEM((REQUESTS, 8, 2, HALF, 256), BF16),
            pltpu.VMEM((REQUESTS, 15, HALF, 256), BF16),
            dma((16,)),
            dma((8,)),
            dma((REQUESTS, 3)),
            dma((2, REQUESTS, 15)),
            dma((2, REQUESTS, 15)),
            dma((2, REQUESTS, 7)),
            dma((2, REQUESTS, 15)),
            dma((2, REQUESTS, 15)),
            dma((2, 15)),
            dma((2, 12)),
            dma((2, REQUESTS, 15)),
        ],
        compiler_params=pltpu.CompilerParams(
            collective_id=0, has_side_effects=True, vmem_limit_bytes=48 * 1024 * 1024
        ),
    )(
        *[pltpu.with_memory_space_constraint(a, pltpu.HBM) for a in operands],
    )
    return logits.reshape(REQUESTS, DRAFT, 256)


def solution(mesh):
    in_specs = (
        P(None, "seq", None),
        P(None, "seq", None),
        P(None, None, "head", None),
        P(None, None, "head", None),
        P(),
        P(),
        P("head", None, None),
        P("head", None, None),
        P("head", "seq"),
        P(None, None, "seq"),
        P("seq"),
        P("seq", "head"),
    )
    out_specs = P(None, None, ("head", "seq"))
    return jax.shard_map(
        per_device, mesh=mesh, in_specs=in_specs, out_specs=out_specs, check_vma=False
    )
```

```python
import functools
import math

import jax
import jax.numpy as jnp
from jax import lax
from jax.experimental import pallas as pl
from jax.experimental.pallas import tpu as pltpu
from jax.sharding import PartitionSpec as P

MESH = pl.DeviceIdType.MESH
NEGATIVE = -1e30
EPSILON = 1e-06
F32 = jnp.float32
BF16 = jnp.bfloat16

CHIP_STEPS = [(2, 1), (1, 1), (3, 1), (2, 0), (0, 1), (1, 0), (3, 0)]
SEQ_STEPS = [(dy, dx, dk) for dy, dx in CHIP_STEPS for dk in (0, 1)] + [(0, 0, 1)]
REQUESTS, DRAFT, HEADS, LATENT, ROPE, WIDTH = 2, 64, 8, 512, 64, 576
TOKENS = REQUESTS * DRAFT
KEYS, EXTRA = 2048, 128
HALF = DRAFT // 2


def nt_dot(a, b):
    return lax.dot_general(a, b, (((1,), (1,)), ((), ())), preferred_element_type=F32)


def dot(a, b):
    return jnp.dot(a, b, preferred_element_type=F32)


def kernel(
    model_width,
    lengths_hbm,
    parents_hbm,
    cache_hbm,
    draft_hbm,
    nope_hbm,
    rope_hbm,
    key_hbm,
    value_hbm,
    out_hbm,
    residual_hbm,
    gain_hbm,
    vocab_hbm,
    logits,
    lengths,
    parents,
    kbuf,
    draft,
    dbuf,
    nope,
    rope,
    key_weight,
    value_weight,
    out_weight,
    residual,
    gain,
    gain_rows,
    vocab,
    nope32,
    rope32,
    qbuf,
    o_send,
    o_recv,
    ml_send,
    ml_recv,
    g_send,
    g_full,
    a_send,
    a_recv,
    b_send,
    b_full,
    s_send,
    s_recv,
    l_send,
    l_recv,
    load_sems,
    vocab_sems,
    local_sems,
    o_sems,
    ml_sems,
    g_sems,
    a_sems,
    b_sems,
    s_sems,
    swap_sems,
    l_sems,
):
    seat = lax.axis_index("seq")
    mine = lax.axis_index("head")
    y = lax.div(seat, 4)
    xh = lax.rem(lax.div(seat, 2), 2)
    core = lax.rem(seat, 2)
    chip = lax.div(seat, 2)

    def seat_at(dy, dx, dk):
        return lax.rem(y + dy, 4) * 4 + lax.rem(xh + dx, 2) * 2 + lax.rem(core + dk, 2)

    seq_peers = [seat_at(*step) for step in SEQ_STEPS]
    chip_peers = seq_peers[0:14:2]
    head_peers = [lax.rem(mine + j, 16) for j in range(1, 16)]

    loads = []

    def load(src, dst):
        copy = pltpu.make_async_copy(src, dst, load_sems.at[len(loads)])
        loads.append(copy)
        copy.start()
        return copy

    got_parents = load(parents_hbm, parents)
    got_nope = load(nope_hbm, nope)
    got_key = load(key_hbm, key_weight)
    got_rope = load(rope_hbm, rope)
    got_draft = load(draft_hbm, draft)
    got_lengths = load(lengths_hbm, lengths)
    got_cache = []
    for b in range(REQUESTS):
        parts = [pl.ds(start, WIDTH // 4) for start in range(0, WIDTH, WIDTH // 4)]
        got_cache.append([load(cache_hbm.at[b, part, :], kbuf.at[b, part, :]) for part in parts])
    got_value = load(value_hbm, value_weight)
    got_out = load(out_hbm, out_weight.at[core])
    got_residual = [
        load(
            residual_hbm.at[pl.ds(pl.multiple_of(b * DRAFT + core * HALF, HALF), HALF), :],
            residual.at[core, pl.ds(b * HALF, HALF), :],
        )
        for b in range(REQUESTS)
    ]
    got_gain = load(gain_hbm, gain)

    got_vocab = []
    for slot, (dy, dx) in enumerate(CHIP_STEPS + [(0, 0)]):
        owner = lax.div(seat_at(dy, dx, 0), 2)
        columns = pl.ds(pl.multiple_of(owner * 512, 512), 512)
        copy = pltpu.make_async_copy(
            vocab_hbm.at[:, columns], vocab.at[core, :, pl.ds(slot * 512, 512)], vocab_sems.at[slot]
        )
        copy.start()
        got_vocab.append(copy)

    barrier = pltpu.get_barrier_semaphore()
    for peer in seq_peers:
        pl.semaphore_signal(barrier, inc=1, device_id={"seq": peer}, device_id_type=MESH)
    for peer in head_peers:
        pl.semaphore_signal(barrier, inc=1, device_id={"head": peer}, device_id_type=MESH)

    for copy in (got_parents, got_draft, got_nope, got_rope, got_key):
        copy.wait()
    row = lax.broadcasted_iota(jnp.int32, (DRAFT, DRAFT), 0)
    column = lax.broadcasted_iota(jnp.int32, (DRAFT, DRAFT), 1)
    reaches = [
        jnp.where((parents[b : b + 1, :] == row) | (row == column), 1.0, 0.0).astype(BF16)
        for b in range(REQUESTS)
    ]
    for _ in range(6):
        reaches = [jnp.where(dot(r, r) > 0.5, 1.0, 0.0).astype(BF16) for r in reaches]
    row = lax.broadcasted_iota(jnp.int32, (DRAFT, EXTRA), 0)
    column = lax.broadcasted_iota(jnp.int32, (DRAFT, EXTRA), 1)
    tree_bias = []
    for b in range(REQUESTS):
        chosen = (column >= 4 * b) & (column < 4 * b + 4) & (row == seat * 4 + column - 4 * b)
        chosen = jnp.where(chosen, 1.0, 0.0).astype(BF16)
        reached = lax.dot_general(
            reaches[b], chosen, (((0,), (0,)), ((), ())), preferred_element_type=F32
        )
        tree_bias.append(jnp.where(reached > 0.5, 0.0, NEGATIVE))
    dbuf[...] = jnp.zeros((EXTRA, WIDTH), BF16)
    dbuf[0:8, :] = jnp.concatenate([draft[b].astype(F32) for b in range(REQUESTS)], axis=0).astype(BF16)

    nope32[...] = nope[...].astype(F32)
    rope32[...] = rope[...].astype(F32)
    for h in range(HEADS):
        picked = nope32[pl.ds(h, TOKENS, stride=HEADS), :].astype(BF16)
        absorbed = dot(picked, key_weight[h]).astype(BF16)
        turned = rope32[pl.ds(h, TOKENS, stride=HEADS), :].astype(BF16)
        for b in range(REQUESTS):
            rows = pl.ds(h * DRAFT, DRAFT)
            qbuf[b, rows, 0:LATENT] = absorbed[b * DRAFT : (b + 1) * DRAFT]
            qbuf[b, rows, LATENT:WIDTH] = turned[b * DRAFT : (b + 1) * DRAFT]

    scale = math.log2(math.e) / math.sqrt(192.0)
    lane = lax.broadcasted_iota(jnp.int32, (DRAFT, 128), 1)
    position = seat * KEYS + lax.broadcasted_iota(jnp.int32, (1, KEYS), 1)
    o_copies, ml_copies, own_copies, swap_copies = [], [], [], []
    partner = seq_peers[14]

    def score(b):
        for copy in got_cache[b]:
            copy.wait()
        live_bias = jnp.where(position < lengths[b], 0.0, NEGATIVE)
        tree = jnp.concatenate([tree_bias[b]] * HEADS, axis=0)
        return dot(qbuf[b], kbuf[b]) + live_bias, nt_dot(qbuf[b], dbuf[...]) + tree

    got_lengths.wait()
    got_value.wait()
    scores = [score(0), score(1)]
    for b in range(REQUESTS):
        tops = jnp.zeros((DRAFT, 128), F32)
        totals = jnp.zeros((DRAFT, 128), F32)
        cached, drafted = scores[b]
        top = jnp.maximum(
            jnp.max(cached, -1, keepdims=True), jnp.max(drafted, -1, keepdims=True)
        )
        cached = jnp.exp2((cached - top) * scale)
        drafted = jnp.exp2((drafted - top) * scale)
        total = jnp.sum(cached, -1, keepdims=True) + jnp.sum(drafted, -1, keepdims=True)
        mixed = nt_dot(cached.astype(BF16), kbuf[b, 0:LATENT, :])
        mixed = (mixed + dot(drafted.astype(BF16), dbuf[:, 0:LATENT])).astype(BF16)
        for h in range(HEADS):
            sub = slice(h * DRAFT, (h + 1) * DRAFT)
            o_send[b, h] = dot(mixed[sub], value_weight[h]).astype(BF16)
            tops = jnp.where(lane == h, top[sub] * scale, tops)
            totals = jnp.where(lane == h, total[sub], totals)
        turned = jnp.concatenate([tops, totals], axis=0).T
        for h in range(HEADS):
            ml_send[b, h] = turned[h : h + 1]
        if b == 0:
            pl.semaphore_wait(barrier, 30)
        for j, step in enumerate(SEQ_STEPS):
            peer = seq_peers[j]
            there, their_core = lax.div(peer, 2), lax.rem(peer, 2)
            half = pl.ds(pl.multiple_of(their_core * 32, 32), 32)
            copy = pltpu.make_async_remote_copy(
                o_send.at[b, there, half, :],
                o_recv.at[b, j],
                o_sems.at[0, b, j],
                o_sems.at[1, b, j],
                device_id={"seq": peer},
                device_id_type=MESH,
            )
            copy.start()
            o_copies.append(copy)
            copy = pltpu.make_async_remote_copy(
                ml_send.at[b, there],
                ml_recv.at[b, j],
                ml_sems.at[0, b, j],
                ml_sems.at[1, b, j],
                device_id={"seq": peer},
                device_id_type=MESH,
            )
            copy.start()
            ml_copies.append(copy)
        swaps = []
        if b == 0:
            got_out.wait()
            got_gain.wait()
            gain_rows[core] = gain[...].astype(F32)[None, :]
            swaps.append((out_weight.at[core], out_weight.at[core], 0))
            swaps.append((gain_rows.at[core], gain_rows.at[core], 1))
            for request in range(REQUESTS):
                other_rows = pl.multiple_of(request * DRAFT + (1 - core) * HALF, HALF)
                swaps.append(
                    (
                        residual_hbm.at[pl.ds(other_rows, HALF), :],
                        residual.at[core, pl.ds(request * HALF, HALF), :],
                        2 + request,
                    )
                )
        else:
            for slot in range(8):
                got_vocab[slot].wait()
                place = vocab.at[core, :, pl.ds(slot * 512, 512)]
                swaps.append((place, place, 4 + slot))
        for src, dst, k in swaps:
            copy = pltpu.make_async_remote_copy(
                src,
                dst,
                swap_sems.at[0, k],
                swap_sems.at[1, k],
                device_id={"seq": partner},
                device_id_type=MESH,
            )
            copy.start()
            swap_copies.append(copy)
        half = pl.ds(pl.multiple_of(core * 32, 32), 32)
        for k, (src, dst) in enumerate(
            ((o_send.at[b, chip, half, :], o_recv.at[b, 15]), (ml_send.at[b, chip], ml_recv.at[b, 15]))
        ):
            copy = pltpu.make_async_copy(src, dst, local_sems.at[b, k])
            copy.start()
            own_copies.append(copy)

    g_copies = []
    for b in range(REQUESTS):
        for copy in ml_copies[b * 15 : (b + 1) * 15]:
            copy.wait_recv()
        for copy in own_copies[b * 2 : (b + 1) * 2]:
            copy.wait()
        gathered = jnp.concatenate(
            [ml_recv[b, j] for j in range(16)] + [jnp.full((112, 128), NEGATIVE, F32)], axis=0
        ).T
        tops, totals = gathered[:DRAFT], gathered[DRAFT:]
        shares = jnp.exp2(tops - jnp.max(tops, -1, keepdims=True))
        shares = shares / jnp.sum(shares * totals, -1, keepdims=True)
        shares = jnp.where(core == 0, shares[:32], shares[32:])
        for copy in o_copies[b * 15 : (b + 1) * 15]:
            copy.wait_recv()
        summed = jnp.zeros((32, 128), F32)
        for j in range(16):
            summed = summed + shares[:, j : j + 1] * o_recv[b, j].astype(F32)
        g_send[b] = summed.astype(BF16)
        place = g_full.at[b, :, pl.ds(pl.multiple_of(chip * 128, 128), 128)]
        for j, peer in enumerate(chip_peers):
            copy = pltpu.make_async_remote_copy(
                g_send.at[b],
                place,
                g_sems.at[0, b, j],
                g_sems.at[1, b, j],
                device_id={"seq": peer},
                device_id_type=MESH,
            )
            copy.start()
            g_copies.append(copy)
        copy = pltpu.make_async_copy(g_send.at[b], place, local_sems.at[b, 2])
        copy.start()
        own_copies.append(copy)

    a_copies, b_copies = [], []
    for b in range(REQUESTS):
        own_copies[4 + b].wait()
        if b == 0:
            swap_copies[0].wait_recv()
        for copy in g_copies[b * 7 : (b + 1) * 7]:
            copy.wait_recv()
        for side in range(2):
            attention = nt_dot(g_full[b], out_weight[side])
            for i in range(8):
                a_send[b, 2 * i + side] = attention[i * 4 : (i + 1) * 4].astype(BF16)
        for j, peer in enumerate(head_peers):
            copy = pltpu.make_async_remote_copy(
                a_send.at[b, peer],
                a_recv.at[b, j],
                a_sems.at[0, b, j],
                a_sems.at[1, b, j],
                device_id={"head": peer},
                device_id_type=MESH,
            )
            copy.start()
            a_copies.append(copy)
    for b in range(REQUESTS):
        summed = a_send[b, mine].astype(F32)
        for j in range(15):
            a_copies[b * 15 + j].wait_recv()
            summed = summed + a_recv[b, j].astype(F32)
        b_send[b] = summed.astype(BF16)
        for j, peer in enumerate(head_peers):
            copy = pltpu.make_async_remote_copy(
                b_send.at[b],
                b_full.at[b, mine],
                b_sems.at[0, b, j],
                b_sems.at[1, b, j],
                device_id={"head": peer},
                device_id_type=MESH,
            )
            copy.start()
            b_copies.append(copy)
        b_full[b, mine] = b_send[b]

    for copy in got_residual:
        copy.wait()
    for copy in swap_copies[1:4]:
        copy.wait_recv()
    square_parts, l_copies = [], []
    for b in range(REQUESTS):
        for copy in b_copies[b * 15 : (b + 1) * 15]:
            copy.wait_recv()
        squares = jnp.zeros((HALF, 1), F32)
        scaled = []
        for side in range(2):
            attention = jnp.concatenate(
                [b_full[b, 2 * i + side].astype(F32) for i in range(8)], axis=0
            )
            hidden = residual[side, b * HALF : (b + 1) * HALF].astype(F32) + attention
            squares = squares + jnp.sum(hidden * hidden, -1, keepdims=True)
            scaled.append((hidden * gain_rows[side]).astype(BF16))
        square_parts.append(squares)
        if b == 1:
            squares = jnp.concatenate(square_parts * 2, axis=0)
            s_send[...] = jnp.broadcast_to(squares, (TOKENS, 128)).T[0:1]
            s_copies = []
            for j, peer in enumerate(seq_peers):
                copy = pltpu.make_async_remote_copy(
                    s_send,
                    s_recv.at[j],
                    s_sems.at[0, j],
                    s_sems.at[1, j],
                    device_id={"seq": peer},
                    device_id_type=MESH,
                )
                copy.start()
                s_copies.append(copy)
        chips = 4 if b == 0 else 2
        for slot in range(8):
            if b == 0:
                swap_copies[4 + slot].wait_recv()
        for group in range(0, 8, chips):
            columns = slice(group * 512, (group + chips) * 512)
            part = dot(scaled[0], vocab[0, :, columns]) + dot(scaled[1], vocab[1, :, columns])
            part = part.astype(BF16)
            for k in range(2 * chips):
                l_send[b, group + k // 2, k % 2] = part[:, k * 256 : (k + 1) * 256]
            for j in range(2 * group, min(2 * (group + chips), 15)):
                slot, dk = (7, 1) if j == 14 else (j // 2, j % 2)
                copy = pltpu.make_async_remote_copy(
                    l_send.at[b, slot, lax.rem(core + dk, 2)],
                    l_recv.at[b, j],
                    l_sems.at[0, b, j],
                    l_sems.at[1, b, j],
                    device_id={"seq": seq_peers[j]},
                    device_id_type=MESH,
                )
                copy.start()
                l_copies.append(copy)
    squares = [s_send[...], jnp.zeros((1, TOKENS), F32)]
    for j, (_, _, dk) in enumerate(SEQ_STEPS):
        s_copies[j].wait_recv()
        squares[dk] = squares[dk] + s_recv[j]
    scales = [
        jnp.broadcast_to(lax.rsqrt(total / model_width + EPSILON), (128, TOKENS)).T
        for total in squares
    ]
    for b in range(REQUESTS):
        sums = [l_send[b, 7, core].astype(F32), jnp.zeros((HALF, 256), F32)]
        for j, (_, _, dk) in enumerate(SEQ_STEPS):
            l_copies[b * 15 + j].wait_recv()
            sums[dk] = sums[dk] + l_recv[b, j].astype(F32)
        for dk in range(2):
            owner = lax.rem(core + dk, 2)
            rows = pl.ds(pl.multiple_of(b * DRAFT + owner * HALF, HALF), HALF)
            logits[rows, :] = (sums[dk] * scales[dk][b * HALF : (b + 1) * HALF, 0:1]).astype(BF16)
    for copy in o_copies + ml_copies + swap_copies + g_copies + a_copies + b_copies + s_copies + l_copies:
        copy.wait_send()


def per_device(
    latent_cache,
    draft_latent,
    query_nope,
    query_rope,
    parents,
    lengths,
    key_weight,
    value_weight,
    out_weight,
    residual,
    norm_gain,
    vocab_weight,
):
    local_width = residual.shape[2]
    model_width = local_width * lax.axis_size("seq")
    operands = [
        lengths,
        parents,
        jnp.swapaxes(latent_cache, 1, 2),
        draft_latent,
        query_nope.reshape(TOKENS * HEADS, 128),
        query_rope.reshape(TOKENS * HEADS, ROPE),
        key_weight,
        value_weight,
        out_weight.T,
        residual.reshape(TOKENS, local_width),
        norm_gain,
        vocab_weight,
    ]
    hbm = pl.BlockSpec(memory_space=pltpu.HBM)
    dma = pltpu.SemaphoreType.DMA
    logits = pl.pallas_call(
        functools.partial(kernel, model_width),
        out_shape=jax.ShapeDtypeStruct((TOKENS, 256), BF16),
        in_specs=[hbm] * 12,
        out_specs=pl.BlockSpec(memory_space=pltpu.VMEM),
        scratch_shapes=[
            pltpu.SMEM((REQUESTS,), jnp.int32),
            pltpu.VMEM((REQUESTS, DRAFT), jnp.int32),
            pltpu.VMEM((REQUESTS, WIDTH, KEYS), BF16),
            pltpu.VMEM((REQUESTS, 4, WIDTH), BF16),
            pltpu.VMEM((EXTRA, WIDTH), BF16),
            pltpu.VMEM((TOKENS * HEADS, 128), BF16),
            pltpu.VMEM((TOKENS * HEADS, ROPE), BF16),
            pltpu.VMEM((HEADS, 128, LATENT), BF16),
            pltpu.VMEM((HEADS, LATENT, 128), BF16),
            pltpu.VMEM((2, local_width, 1024), BF16),
            pltpu.VMEM((2, 2 * HALF, local_width), BF16),
            pltpu.VMEM((local_width,), BF16),
            pltpu.VMEM((2, 1, local_width), F32),
            pltpu.VMEM((2, local_width, 4096), BF16),
            pltpu.VMEM((TOKENS * HEADS, 128), F32),
            pltpu.VMEM((TOKENS * HEADS, ROPE), F32),
            pltpu.VMEM((REQUESTS, HEADS * DRAFT, WIDTH), BF16),
            pltpu.VMEM((REQUESTS, HEADS, DRAFT, 128), BF16),
            pltpu.VMEM((REQUESTS, 16, 32, 128), BF16),
            pltpu.VMEM((REQUESTS, HEADS, 1, 128), F32),
            pltpu.VMEM((REQUESTS, 16, 1, 128), F32),
            pltpu.VMEM((REQUESTS, 32, 128), BF16),
            pltpu.VMEM((REQUESTS, HALF, 1024), BF16),
            pltpu.VMEM((REQUESTS, 16, 4, local_width), BF16),
            pltpu.VMEM((REQUESTS, 15, 4, local_width), BF16),
            pltpu.VMEM((REQUESTS, 4, local_width), BF16),
            pltpu.VMEM((REQUESTS, 16, 4, local_width), BF16),
            pltpu.VMEM((1, TOKENS), F32),
            pltpu.VMEM((15, 1, TOKENS), F32),
            pltpu.VMEM((REQUESTS, 8, 2, HALF, 256), BF16),
            pltpu.VMEM((REQUESTS, 15, HALF, 256), BF16),
            dma((20,)),
            dma((8,)),
            dma((REQUESTS, 3)),
            dma((2, REQUESTS, 15)),
            dma((2, REQUESTS, 15)),
            dma((2, REQUESTS, 7)),
            dma((2, REQUESTS, 15)),
            dma((2, REQUESTS, 15)),
            dma((2, 15)),
            dma((2, 12)),
            dma((2, REQUESTS, 15)),
        ],
        compiler_params=pltpu.CompilerParams(
            collective_id=0, has_side_effects=True, vmem_limit_bytes=48 * 1024 * 1024
        ),
    )(
        *[pltpu.with_memory_space_constraint(a, pltpu.HBM) for a in operands],
    )
    return logits.reshape(REQUESTS, DRAFT, 256)


def solution(mesh):
    in_specs = (
        P(None, "seq", None),
        P(None, "seq", None),
        P(None, None, "head", None),
        P(None, None, "head", None),
        P(),
        P(),
        P("head", None, None),
        P("head", None, None),
        P("head", "seq"),
        P(None, None, "seq"),
        P("seq"),
        P("seq", "head"),
    )
    out_specs = P(None, None, ("head", "seq"))
    return jax.shard_map(
        per_device, mesh=mesh, in_specs=in_specs, out_specs=out_specs, check_vma=False
    )
```

```python
import functools
import math

import jax
import jax.numpy as jnp
from jax import lax
from jax.experimental import pallas as pl
from jax.experimental.pallas import tpu as pltpu
from jax.sharding import PartitionSpec as P

MESH = pl.DeviceIdType.MESH
NEGATIVE = -1e30
EPSILON = 1e-06
F32 = jnp.float32
BF16 = jnp.bfloat16

CHIP_STEPS = [(2, 1), (1, 1), (3, 1), (2, 0), (0, 1), (1, 0), (3, 0)]
SEQ_STEPS = [(dy, dx, dk) for dy, dx in CHIP_STEPS for dk in (0, 1)] + [(0, 0, 1)]
REQUESTS, DRAFT, HEADS, LATENT, ROPE, WIDTH = 2, 64, 8, 512, 64, 576
TOKENS = REQUESTS * DRAFT
KEYS, EXTRA = 2048, 128
KEY_PARTS = [slice(0, KEYS // 2), slice(KEYS // 2, KEYS)]
HALF = DRAFT // 2


def nt_dot(a, b):
    return lax.dot_general(a, b, (((1,), (1,)), ((), ())), preferred_element_type=F32)


def dot(a, b):
    return jnp.dot(a, b, preferred_element_type=F32)


def kernel(
    model_width,
    lengths_hbm,
    parents_hbm,
    cache_hbm,
    draft_hbm,
    nope_hbm,
    rope_hbm,
    key_hbm,
    value_hbm,
    out_hbm,
    residual_hbm,
    gain_hbm,
    vocab_hbm,
    logits,
    lengths,
    parents,
    kbuf,
    draft,
    dbuf,
    nope,
    rope,
    key_weight,
    value_weight,
    out_weight,
    residual,
    gain,
    gain_rows,
    vocab,
    nope32,
    rope32,
    qbuf,
    o_send,
    o_recv,
    ml_send,
    ml_recv,
    g_send,
    g_full,
    a_send,
    a_recv,
    b_send,
    b_full,
    s_send,
    s_recv,
    l_send,
    l_recv,
    load_sems,
    vocab_sems,
    local_sems,
    o_sems,
    ml_sems,
    g_sems,
    a_sems,
    b_sems,
    s_sems,
    swap_sems,
    l_sems,
):
    seat = lax.axis_index("seq")
    mine = lax.axis_index("head")
    y = lax.div(seat, 4)
    xh = lax.rem(lax.div(seat, 2), 2)
    core = lax.rem(seat, 2)
    chip = lax.div(seat, 2)

    def seat_at(dy, dx, dk):
        return lax.rem(y + dy, 4) * 4 + lax.rem(xh + dx, 2) * 2 + lax.rem(core + dk, 2)

    seq_peers = [seat_at(*step) for step in SEQ_STEPS]
    chip_peers = seq_peers[0:14:2]
    head_peers = [lax.rem(mine + j, 16) for j in range(1, 16)]

    loads = []

    def load(src, dst):
        copy = pltpu.make_async_copy(src, dst, load_sems.at[len(loads)])
        loads.append(copy)
        copy.start()
        return copy

    got_parents = load(parents_hbm, parents)
    got_nope = load(nope_hbm, nope)
    got_key = load(key_hbm, key_weight)
    got_rope = load(rope_hbm, rope)
    got_draft = load(draft_hbm, draft)
    got_lengths = load(lengths_hbm, lengths)
    def load_cache(b):
        parts = [pl.ds(start, WIDTH // 4) for start in range(0, WIDTH, WIDTH // 4)]
        return [load(cache_hbm.at[b, part, :], kbuf.at[b, part, :]) for part in parts]

    got_cache = [load_cache(0)]

    barrier = pltpu.get_barrier_semaphore()
    for peer in seq_peers:
        pl.semaphore_signal(barrier, inc=1, device_id={"seq": peer}, device_id_type=MESH)
    for peer in head_peers:
        pl.semaphore_signal(barrier, inc=1, device_id={"head": peer}, device_id_type=MESH)

    for copy in (got_parents, got_draft, got_nope, got_rope, got_key):
        copy.wait()
    got_value = load(value_hbm, value_weight)
    row = lax.broadcasted_iota(jnp.int32, (DRAFT, DRAFT), 0)
    column = lax.broadcasted_iota(jnp.int32, (DRAFT, DRAFT), 1)
    reaches = [
        jnp.where((parents[b : b + 1, :] == row) | (row == column), 1.0, 0.0).astype(BF16)
        for b in range(REQUESTS)
    ]
    for _ in range(6):
        reaches = [jnp.where(dot(r, r) > 0.5, 1.0, 0.0).astype(BF16) for r in reaches]
    row = lax.broadcasted_iota(jnp.int32, (DRAFT, EXTRA), 0)
    column = lax.broadcasted_iota(jnp.int32, (DRAFT, EXTRA), 1)
    tree_bias = []
    for b in range(REQUESTS):
        chosen = (column >= 4 * b) & (column < 4 * b + 4) & (row == seat * 4 + column - 4 * b)
        chosen = jnp.where(chosen, 1.0, 0.0).astype(BF16)
        reached = lax.dot_general(
            reaches[b], chosen, (((0,), (0,)), ((), ())), preferred_element_type=F32
        )
        tree_bias.append(jnp.where(reached > 0.5, 0.0, NEGATIVE))
    dbuf[...] = jnp.zeros((EXTRA, WIDTH), BF16)
    dbuf[0:8, :] = jnp.concatenate([draft[b].astype(F32) for b in range(REQUESTS)], axis=0).astype(BF16)

    nope32[...] = nope[...].astype(F32)
    rope32[...] = rope[...].astype(F32)
    for h in range(HEADS):
        picked = nope32[pl.ds(h, TOKENS, stride=HEADS), :].astype(BF16)
        absorbed = dot(picked, key_weight[h]).astype(BF16)
        turned = rope32[pl.ds(h, TOKENS, stride=HEADS), :].astype(BF16)
        for b in range(REQUESTS):
            rows = pl.ds(h * DRAFT, DRAFT)
            qbuf[b, rows, 0:LATENT] = absorbed[b * DRAFT : (b + 1) * DRAFT]
            qbuf[b, rows, LATENT:WIDTH] = turned[b * DRAFT : (b + 1) * DRAFT]

    scale = math.log2(math.e) / math.sqrt(192.0)
    lane = lax.broadcasted_iota(jnp.int32, (DRAFT, 128), 1)
    position = seat * KEYS + lax.broadcasted_iota(jnp.int32, (1, KEYS), 1)
    o_copies, ml_copies, own_copies, swap_copies = [], [], [], []
    partner = seq_peers[14]

    for copy in got_cache[0] + [got_lengths, got_value]:
        copy.wait()

    got_cache.append(load_cache(1))
    got_out = load(out_hbm, out_weight.at[core])
    got_residual = [
        load(
            residual_hbm.at[pl.ds(pl.multiple_of(b * DRAFT + core * HALF, HALF), HALF), :],
            residual.at[core, pl.ds(b * HALF, HALF), :],
        )
        for b in range(REQUESTS)
    ]
    got_gain = load(gain_hbm, gain)

    got_vocab = []
    for slot, (dy, dx) in enumerate(CHIP_STEPS + [(0, 0)]):
        owner = lax.div(seat_at(dy, dx, 0), 2)
        columns = pl.ds(pl.multiple_of(owner * 512, 512), 512)
        copy = pltpu.make_async_copy(
            vocab_hbm.at[:, columns], vocab.at[core, :, pl.ds(slot * 512, 512)], vocab_sems.at[slot]
        )
        copy.start()
        got_vocab.append(copy)

    for b in range(REQUESTS):
        if b == 1:
            for copy in got_cache[1]:
                copy.wait()
        tree = jnp.concatenate([tree_bias[b]] * HEADS, axis=0)
        drafted = nt_dot(qbuf[b], dbuf[...]) + tree
        top = jnp.max(drafted, -1, keepdims=True)
        scores = []
        for columns in KEY_PARTS:
            live_bias = jnp.where(position[:, columns] < lengths[b], 0.0, NEGATIVE)
            scores.append(dot(qbuf[b], kbuf[b, :, columns]) + live_bias)
            top = jnp.maximum(top, jnp.max(scores[-1], -1, keepdims=True))
        drafted = jnp.exp2((drafted - top) * scale)
        total = jnp.sum(drafted, -1, keepdims=True)
        mixed = dot(drafted.astype(BF16), dbuf[:, 0:LATENT])
        for columns, cached in zip(KEY_PARTS, scores):
            cached = jnp.exp2((cached - top) * scale)
            total = total + jnp.sum(cached, -1, keepdims=True)
            mixed = mixed + nt_dot(cached.astype(BF16), kbuf[b, 0:LATENT, columns])
        mixed = mixed.astype(BF16)
        tops = jnp.zeros((DRAFT, 128), F32)
        totals = jnp.zeros((DRAFT, 128), F32)
        for h in range(HEADS):
            sub = slice(h * DRAFT, (h + 1) * DRAFT)
            o_send[b, h] = dot(mixed[sub], value_weight[h]).astype(BF16)
            tops = jnp.where(lane == h, top[sub] * scale, tops)
            totals = jnp.where(lane == h, total[sub], totals)
        turned = jnp.concatenate([tops, totals], axis=0).T
        for h in range(HEADS):
            ml_send[b, h] = turned[h : h + 1]
        if b == 0:
            pl.semaphore_wait(barrier, 30)
        for j, step in enumerate(SEQ_STEPS):
            peer = seq_peers[j]
            there, their_core = lax.div(peer, 2), lax.rem(peer, 2)
            half = pl.ds(pl.multiple_of(their_core * 32, 32), 32)
            copy = pltpu.make_async_remote_copy(
                o_send.at[b, there, half, :],
                o_recv.at[b, j],
                o_sems.at[0, b, j],
                o_sems.at[1, b, j],
                device_id={"seq": peer},
                device_id_type=MESH,
            )
            copy.start()
            o_copies.append(copy)
            copy = pltpu.make_async_remote_copy(
                ml_send.at[b, there],
                ml_recv.at[b, j],
                ml_sems.at[0, b, j],
                ml_sems.at[1, b, j],
                device_id={"seq": peer},
                device_id_type=MESH,
            )
            copy.start()
            ml_copies.append(copy)
        swaps = []
        if b == 0:
            got_out.wait()
            got_gain.wait()
            gain_rows[core] = gain[...].astype(F32)[None, :]
            swaps.append((out_weight.at[core], out_weight.at[core], 0))
            swaps.append((gain_rows.at[core], gain_rows.at[core], 1))
            for request in range(REQUESTS):
                other_rows = pl.multiple_of(request * DRAFT + (1 - core) * HALF, HALF)
                swaps.append(
                    (
                        residual_hbm.at[pl.ds(other_rows, HALF), :],
                        residual.at[core, pl.ds(request * HALF, HALF), :],
                        2 + request,
                    )
                )
            for slot in range(8):
                got_vocab[slot].wait()
                place = vocab.at[core, :, pl.ds(slot * 512, 512)]
                swaps.append((place, place, 4 + slot))
        for src, dst, k in swaps:
            copy = pltpu.make_async_remote_copy(
                src,
                dst,
                swap_sems.at[0, k],
                swap_sems.at[1, k],
                device_id={"seq": partner},
                device_id_type=MESH,
            )
            copy.start()
            swap_copies.append(copy)
        half = pl.ds(pl.multiple_of(core * 32, 32), 32)
        for k, (src, dst) in enumerate(
            ((o_send.at[b, chip, half, :], o_recv.at[b, 15]), (ml_send.at[b, chip], ml_recv.at[b, 15]))
        ):
            copy = pltpu.make_async_copy(src, dst, local_sems.at[b, k])
            copy.start()
            own_copies.append(copy)

    g_copies = []
    for b in range(REQUESTS):
        for copy in ml_copies[b * 15 : (b + 1) * 15]:
            copy.wait_recv()
        for copy in own_copies[b * 2 : (b + 1) * 2]:
            copy.wait()
        gathered = jnp.concatenate(
            [ml_recv[b, j] for j in range(16)] + [jnp.full((112, 128), NEGATIVE, F32)], axis=0
        ).T
        tops, totals = gathered[:DRAFT], gathered[DRAFT:]
        shares = jnp.exp2(tops - jnp.max(tops, -1, keepdims=True))
        shares = shares / jnp.sum(shares * totals, -1, keepdims=True)
        shares = jnp.where(core == 0, shares[:32], shares[32:])
        for copy in o_copies[b * 15 : (b + 1) * 15]:
            copy.wait_recv()
        summed = jnp.zeros((32, 128), F32)
        for j in range(16):
            summed = summed + shares[:, j : j + 1] * o_recv[b, j].astype(F32)
        g_send[b] = summed.astype(BF16)
        place = g_full.at[b, :, pl.ds(pl.multiple_of(chip * 128, 128), 128)]
        for j, peer in enumerate(chip_peers):
            copy = pltpu.make_async_remote_copy(
                g_send.at[b],
                place,
                g_sems.at[0, b, j],
                g_sems.at[1, b, j],
                device_id={"seq": peer},
                device_id_type=MESH,
            )
            copy.start()
            g_copies.append(copy)
        copy = pltpu.make_async_copy(g_send.at[b], place, local_sems.at[b, 2])
        copy.start()
        own_copies.append(copy)

    a_copies, b_copies = [], []
    for b in range(REQUESTS):
        own_copies[4 + b].wait()
        if b == 0:
            swap_copies[0].wait_recv()
        for copy in g_copies[b * 7 : (b + 1) * 7]:
            copy.wait_recv()
        for side in range(2):
            attention = nt_dot(g_full[b], out_weight[side])
            for i in range(8):
                a_send[b, 2 * i + side] = attention[i * 4 : (i + 1) * 4].astype(BF16)
        for j, peer in enumerate(head_peers):
            copy = pltpu.make_async_remote_copy(
                a_send.at[b, peer],
                a_recv.at[b, j],
                a_sems.at[0, b, j],
                a_sems.at[1, b, j],
                device_id={"head": peer},
                device_id_type=MESH,
            )
            copy.start()
            a_copies.append(copy)
    for b in range(REQUESTS):
        summed = a_send[b, mine].astype(F32)
        for j in range(15):
            a_copies[b * 15 + j].wait_recv()
            summed = summed + a_recv[b, j].astype(F32)
        b_send[b] = summed.astype(BF16)
        for j, peer in enumerate(head_peers):
            copy = pltpu.make_async_remote_copy(
                b_send.at[b],
                b_full.at[b, mine],
                b_sems.at[0, b, j],
                b_sems.at[1, b, j],
                device_id={"head": peer},
                device_id_type=MESH,
            )
            copy.start()
            b_copies.append(copy)
        b_full[b, mine] = b_send[b]

    for copy in got_residual:
        copy.wait()
    for copy in swap_copies[1:4]:
        copy.wait_recv()
    square_parts, l_copies = [], []
    for b in range(REQUESTS):
        for copy in b_copies[b * 15 : (b + 1) * 15]:
            copy.wait_recv()
        squares = jnp.zeros((HALF, 1), F32)
        scaled = []
        for side in range(2):
            attention = jnp.concatenate(
                [b_full[b, 2 * i + side].astype(F32) for i in range(8)], axis=0
            )
            hidden = residual[side, b * HALF : (b + 1) * HALF].astype(F32) + attention
            squares = squares + jnp.sum(hidden * hidden, -1, keepdims=True)
            scaled.append((hidden * gain_rows[side]).astype(BF16))
        square_parts.append(squares)
        if b == 1:
            squares = jnp.concatenate(square_parts * 2, axis=0)
            s_send[...] = jnp.broadcast_to(squares, (TOKENS, 128)).T[0:1]
            s_copies = []
            for j, peer in enumerate(seq_peers):
                copy = pltpu.make_async_remote_copy(
                    s_send,
                    s_recv.at[j],
                    s_sems.at[0, j],
                    s_sems.at[1, j],
                    device_id={"seq": peer},
                    device_id_type=MESH,
                )
                copy.start()
                s_copies.append(copy)
        chips = 4 if b == 0 else 2
        for slot in range(8):
            if b == 0:
                swap_copies[4 + slot].wait_recv()
        for group in range(0, 8, chips):
            columns = slice(group * 512, (group + chips) * 512)
            part = dot(scaled[0], vocab[0, :, columns]) + dot(scaled[1], vocab[1, :, columns])
            part = part.astype(BF16)
            for k in range(2 * chips):
                l_send[b, group + k // 2, k % 2] = part[:, k * 256 : (k + 1) * 256]
            for j in range(2 * group, min(2 * (group + chips), 15)):
                slot, dk = (7, 1) if j == 14 else (j // 2, j % 2)
                copy = pltpu.make_async_remote_copy(
                    l_send.at[b, slot, lax.rem(core + dk, 2)],
                    l_recv.at[b, j],
                    l_sems.at[0, b, j],
                    l_sems.at[1, b, j],
                    device_id={"seq": seq_peers[j]},
                    device_id_type=MESH,
                )
                copy.start()
                l_copies.append(copy)
    squares = [s_send[...], jnp.zeros((1, TOKENS), F32)]
    for j, (_, _, dk) in enumerate(SEQ_STEPS):
        s_copies[j].wait_recv()
        squares[dk] = squares[dk] + s_recv[j]
    scales = [
        jnp.broadcast_to(lax.rsqrt(total / model_width + EPSILON), (128, TOKENS)).T
        for total in squares
    ]
    for b in range(REQUESTS):
        sums = [l_send[b, 7, core].astype(F32), jnp.zeros((HALF, 256), F32)]
        for j, (_, _, dk) in enumerate(SEQ_STEPS):
            l_copies[b * 15 + j].wait_recv()
            sums[dk] = sums[dk] + l_recv[b, j].astype(F32)
        for dk in range(2):
            owner = lax.rem(core + dk, 2)
            rows = pl.ds(pl.multiple_of(b * DRAFT + owner * HALF, HALF), HALF)
            logits[rows, :] = (sums[dk] * scales[dk][b * HALF : (b + 1) * HALF, 0:1]).astype(BF16)
    for copy in o_copies + ml_copies + swap_copies + g_copies + a_copies + b_copies + s_copies + l_copies:
        copy.wait_send()


def per_device(
    latent_cache,
    draft_latent,
    query_nope,
    query_rope,
    parents,
    lengths,
    key_weight,
    value_weight,
    out_weight,
    residual,
    norm_gain,
    vocab_weight,
):
    local_width = residual.shape[2]
    model_width = local_width * lax.axis_size("seq")
    operands = [
        lengths,
        parents,
        jnp.swapaxes(latent_cache, 1, 2),
        draft_latent,
        query_nope.reshape(TOKENS * HEADS, 128),
        query_rope.reshape(TOKENS * HEADS, ROPE),
        key_weight,
        value_weight,
        out_weight.T,
        residual.reshape(TOKENS, local_width),
        norm_gain,
        vocab_weight,
    ]
    hbm = pl.BlockSpec(memory_space=pltpu.HBM)
    dma = pltpu.SemaphoreType.DMA
    logits = pl.pallas_call(
        functools.partial(kernel, model_width),
        out_shape=jax.ShapeDtypeStruct((TOKENS, 256), BF16),
        in_specs=[hbm] * 12,
        out_specs=pl.BlockSpec(memory_space=pltpu.VMEM),
        scratch_shapes=[
            pltpu.SMEM((REQUESTS,), jnp.int32),
            pltpu.VMEM((REQUESTS, DRAFT), jnp.int32),
            pltpu.VMEM((REQUESTS, WIDTH, KEYS), BF16),
            pltpu.VMEM((REQUESTS, 4, WIDTH), BF16),
            pltpu.VMEM((EXTRA, WIDTH), BF16),
            pltpu.VMEM((TOKENS * HEADS, 128), BF16),
            pltpu.VMEM((TOKENS * HEADS, ROPE), BF16),
            pltpu.VMEM((HEADS, 128, LATENT), BF16),
            pltpu.VMEM((HEADS, LATENT, 128), BF16),
            pltpu.VMEM((2, local_width, 1024), BF16),
            pltpu.VMEM((2, 2 * HALF, local_width), BF16),
            pltpu.VMEM((local_width,), BF16),
            pltpu.VMEM((2, 1, local_width), F32),
            pltpu.VMEM((2, local_width, 4096), BF16),
            pltpu.VMEM((TOKENS * HEADS, 128), F32),
            pltpu.VMEM((TOKENS * HEADS, ROPE), F32),
            pltpu.VMEM((REQUESTS, HEADS * DRAFT, WIDTH), BF16),
            pltpu.VMEM((REQUESTS, HEADS, DRAFT, 128), BF16),
            pltpu.VMEM((REQUESTS, 16, 32, 128), BF16),
            pltpu.VMEM((REQUESTS, HEADS, 1, 128), F32),
            pltpu.VMEM((REQUESTS, 16, 1, 128), F32),
            pltpu.VMEM((REQUESTS, 32, 128), BF16),
            pltpu.VMEM((REQUESTS, HALF, 1024), BF16),
            pltpu.VMEM((REQUESTS, 16, 4, local_width), BF16),
            pltpu.VMEM((REQUESTS, 15, 4, local_width), BF16),
            pltpu.VMEM((REQUESTS, 4, local_width), BF16),
            pltpu.VMEM((REQUESTS, 16, 4, local_width), BF16),
            pltpu.VMEM((1, TOKENS), F32),
            pltpu.VMEM((15, 1, TOKENS), F32),
            pltpu.VMEM((REQUESTS, 8, 2, HALF, 256), BF16),
            pltpu.VMEM((REQUESTS, 15, HALF, 256), BF16),
            dma((20,)),
            dma((8,)),
            dma((REQUESTS, 3)),
            dma((2, REQUESTS, 15)),
            dma((2, REQUESTS, 15)),
            dma((2, REQUESTS, 7)),
            dma((2, REQUESTS, 15)),
            dma((2, REQUESTS, 15)),
            dma((2, 15)),
            dma((2, 12)),
            dma((2, REQUESTS, 15)),
        ],
        compiler_params=pltpu.CompilerParams(
            collective_id=0, has_side_effects=True, vmem_limit_bytes=48 * 1024 * 1024
        ),
    )(
        *[pltpu.with_memory_space_constraint(a, pltpu.HBM) for a in operands],
    )
    return logits.reshape(REQUESTS, DRAFT, 256)


def solution(mesh):
    in_specs = (
        P(None, "seq", None),
        P(None, "seq", None),
        P(None, None, "head", None),
        P(None, None, "head", None),
        P(),
        P(),
        P("head", None, None),
        P("head", None, None),
        P("head", "seq"),
        P(None, None, "seq"),
        P("seq"),
        P("seq", "head"),
    )
    out_specs = P(None, None, ("head", "seq"))
    return jax.shard_map(
        per_device, mesh=mesh, in_specs=in_specs, out_specs=out_specs, check_vma=False
    )
```

```python
import functools
import math

import jax
import jax.numpy as jnp
from jax import lax
from jax.experimental import pallas as pl
from jax.experimental.pallas import tpu as pltpu
from jax.sharding import PartitionSpec as P

MESH = pl.DeviceIdType.MESH
NEGATIVE = -1e30
EPSILON = 1e-06
F32 = jnp.float32
BF16 = jnp.bfloat16

CHIP_STEPS = [(2, 1), (1, 1), (3, 1), (2, 0), (0, 1), (1, 0), (3, 0)]
SEQ_STEPS = [(dy, dx, dk) for dy, dx in CHIP_STEPS for dk in (0, 1)] + [(0, 0, 1)]
REQUESTS, DRAFT, HEADS, LATENT, ROPE, WIDTH = 2, 64, 8, 512, 64, 576
TOKENS = REQUESTS * DRAFT
KEYS, EXTRA = 2048, 128
KEY_PARTS = [slice(0, KEYS // 2), slice(KEYS // 2, KEYS)]
HALF = DRAFT // 2


def nt_dot(a, b):
    return lax.dot_general(a, b, (((1,), (1,)), ((), ())), preferred_element_type=F32)


def dot(a, b):
    return jnp.dot(a, b, preferred_element_type=F32)


def kernel(
    model_width,
    lengths_hbm,
    parents_hbm,
    cache_hbm,
    draft_hbm,
    nope_hbm,
    rope_hbm,
    key_hbm,
    value_hbm,
    out_hbm,
    residual_hbm,
    gain_hbm,
    vocab_hbm,
    logits,
    lengths,
    parents,
    kbuf,
    draft,
    dbuf,
    tree_bias,
    nope,
    rope,
    key_weight,
    value_weight,
    out_weight,
    residual,
    gain,
    gain_rows,
    vocab,
    nope32,
    rope32,
    qbuf,
    o_send,
    o_recv,
    ml_send,
    ml_recv,
    g_send,
    g_full,
    a_send,
    a_recv,
    b_send,
    b_full,
    s_send,
    s_recv,
    l_send,
    l_recv,
    load_sems,
    vocab_sems,
    local_sems,
    o_sems,
    ml_sems,
    g_sems,
    a_sems,
    b_sems,
    s_sems,
    swap_sems,
    l_sems,
):
    seat = lax.axis_index("seq")
    mine = lax.axis_index("head")
    y = lax.div(seat, 4)
    xh = lax.rem(lax.div(seat, 2), 2)
    core = lax.rem(seat, 2)
    chip = lax.div(seat, 2)

    def seat_at(dy, dx, dk):
        return lax.rem(y + dy, 4) * 4 + lax.rem(xh + dx, 2) * 2 + lax.rem(core + dk, 2)

    seq_peers = [seat_at(*step) for step in SEQ_STEPS]
    chip_peers = seq_peers[0:14:2]
    head_peers = [lax.rem(mine + j, 16) for j in range(1, 16)]

    loads = []

    def load(src, dst):
        copy = pltpu.make_async_copy(src, dst, load_sems.at[len(loads)])
        loads.append(copy)
        copy.start()
        return copy

    got_parents = load(parents_hbm, parents)
    got_nope = load(nope_hbm, nope)
    got_key = load(key_hbm, key_weight)
    got_rope = load(rope_hbm, rope)
    got_draft = load(draft_hbm, draft)
    got_lengths = load(lengths_hbm, lengths)
    def load_cache(b):
        parts = [pl.ds(start, WIDTH // 4) for start in range(0, WIDTH, WIDTH // 4)]
        return [load(cache_hbm.at[b, part, :], kbuf.at[b, part, :]) for part in parts]

    got_cache = [load_cache(0)]

    barrier = pltpu.get_barrier_semaphore()
    for peer in seq_peers:
        pl.semaphore_signal(barrier, inc=1, device_id={"seq": peer}, device_id_type=MESH)
    for peer in head_peers:
        pl.semaphore_signal(barrier, inc=1, device_id={"head": peer}, device_id_type=MESH)

    for copy in (got_parents, got_draft, got_nope, got_rope, got_key):
        copy.wait()
    got_value = load(value_hbm, value_weight)
    row = lax.broadcasted_iota(jnp.int32, (DRAFT, DRAFT), 0)
    column = lax.broadcasted_iota(jnp.int32, (DRAFT, DRAFT), 1)
    reaches = [
        jnp.where((parents[b : b + 1, :] == row) | (row == column), 1.0, 0.0).astype(BF16)
        for b in range(REQUESTS)
    ]
    for _ in range(6):
        reaches = [jnp.where(dot(r, r) > 0.5, 1.0, 0.0).astype(BF16) for r in reaches]
    row = lax.broadcasted_iota(jnp.int32, (DRAFT, EXTRA), 0)
    column = lax.broadcasted_iota(jnp.int32, (DRAFT, EXTRA), 1)
    for b in range(REQUESTS):
        chosen = (column >= 4 * b) & (column < 4 * b + 4) & (row == seat * 4 + column - 4 * b)
        chosen = jnp.where(chosen, 1.0, 0.0).astype(BF16)
        reached = lax.dot_general(
            reaches[b], chosen, (((0,), (0,)), ((), ())), preferred_element_type=F32
        )
        tree_bias[b] = jnp.where(reached > 0.5, 0.0, NEGATIVE)
    dbuf[...] = jnp.zeros((EXTRA, WIDTH), BF16)
    dbuf[0:8, :] = jnp.concatenate([draft[b].astype(F32) for b in range(REQUESTS)], axis=0).astype(BF16)

    nope32[...] = nope[...].astype(F32)
    rope32[...] = rope[...].astype(F32)
    for h in range(HEADS):
        picked = nope32[pl.ds(h, TOKENS, stride=HEADS), :].astype(BF16)
        absorbed = dot(picked, key_weight[h]).astype(BF16)
        turned = rope32[pl.ds(h, TOKENS, stride=HEADS), :].astype(BF16)
        for b in range(REQUESTS):
            rows = pl.ds(h * DRAFT, DRAFT)
            qbuf[b, rows, 0:LATENT] = absorbed[b * DRAFT : (b + 1) * DRAFT]
            qbuf[b, rows, LATENT:WIDTH] = turned[b * DRAFT : (b + 1) * DRAFT]

    scale = math.log2(math.e) / math.sqrt(192.0)
    lane = lax.broadcasted_iota(jnp.int32, (DRAFT, 128), 1)
    position = seat * KEYS + lax.broadcasted_iota(jnp.int32, (1, KEYS), 1)
    partner = seq_peers[14]

    for copy in got_cache[0] + [got_lengths, got_value]:
        copy.wait()

    got_cache.append(load_cache(1))
    got_out = load(out_hbm, out_weight.at[core])
    got_residual = [
        load(
            residual_hbm.at[pl.ds(pl.multiple_of(b * DRAFT + core * HALF, HALF), HALF), :],
            residual.at[core, pl.ds(b * HALF, HALF), :],
        )
        for b in range(REQUESTS)
    ]
    got_gain = load(gain_hbm, gain)

    got_vocab = []
    for slot, (dy, dx) in enumerate(CHIP_STEPS + [(0, 0)]):
        owner = lax.div(seat_at(dy, dx, 0), 2)
        columns = pl.ds(pl.multiple_of(owner * 512, 512), 512)
        copy = pltpu.make_async_copy(
            vocab_hbm.at[:, columns], vocab.at[core, :, pl.ds(slot * 512, 512)], vocab_sems.at[slot]
        )
        copy.start()
        got_vocab.append(copy)

    def o_copy(b, j):
        peer = seq_peers[j]
        half = pl.ds(pl.multiple_of(lax.rem(peer, 2) * HALF, HALF), HALF)
        return pltpu.make_async_remote_copy(
            o_send.at[b, lax.div(peer, 2), half, :],
            o_recv.at[b, j],
            o_sems.at[0, b, j],
            o_sems.at[1, b, j],
            device_id={"seq": peer},
            device_id_type=MESH,
        )

    def ml_copy(b, j):
        peer = seq_peers[j]
        return pltpu.make_async_remote_copy(
            ml_send.at[b, lax.div(peer, 2)],
            ml_recv.at[b, j],
            ml_sems.at[0, b, j],
            ml_sems.at[1, b, j],
            device_id={"seq": peer},
            device_id_type=MESH,
        )

    def own_copy(b, k):
        half = pl.ds(pl.multiple_of(core * HALF, HALF), HALF)
        src, dst = (
            (o_send.at[b, chip, half, :], o_recv.at[b, 15]),
            (ml_send.at[b, chip], ml_recv.at[b, 15]),
        )[k]
        return pltpu.make_async_copy(src, dst, local_sems.at[b, k])

    swaps = [
        (out_weight.at[core], out_weight.at[core]),
        (gain_rows.at[core], gain_rows.at[core]),
    ]
    for request in range(REQUESTS):
        other_rows = pl.multiple_of(request * DRAFT + (1 - core) * HALF, HALF)
        swaps.append(
            (
                residual_hbm.at[pl.ds(other_rows, HALF), :],
                residual.at[core, pl.ds(request * HALF, HALF), :],
            )
        )
    for slot in range(8):
        place = vocab.at[core, :, pl.ds(slot * 512, 512)]
        swaps.append((place, place))
    swap_copies = [
        pltpu.make_async_remote_copy(
            src,
            dst,
            swap_sems.at[0, k],
            swap_sems.at[1, k],
            device_id={"seq": partner},
            device_id_type=MESH,
        )
        for k, (src, dst) in enumerate(swaps)
    ]

    @pl.loop(0, REQUESTS)
    def _(b):
        @pl.when(b == 1)
        def _():
            for copy in got_cache[1]:
                copy.wait()

        tree = jnp.concatenate([tree_bias[b]] * HEADS, axis=0)
        drafted = nt_dot(qbuf[b], dbuf[...]) + tree
        top = jnp.max(drafted, -1, keepdims=True)
        scores = []
        for columns in KEY_PARTS:
            live_bias = jnp.where(position[:, columns] < lengths[b], 0.0, NEGATIVE)
            scores.append(dot(qbuf[b], kbuf[b, :, columns]) + live_bias)
            top = jnp.maximum(top, jnp.max(scores[-1], -1, keepdims=True))
        drafted = jnp.exp2((drafted - top) * scale)
        total = jnp.sum(drafted, -1, keepdims=True)
        mixed = dot(drafted.astype(BF16), dbuf[:, 0:LATENT])
        for columns, cached in zip(KEY_PARTS, scores):
            cached = jnp.exp2((cached - top) * scale)
            total = total + jnp.sum(cached, -1, keepdims=True)
            mixed = mixed + nt_dot(cached.astype(BF16), kbuf[b, 0:LATENT, columns])
        mixed = mixed.astype(BF16)
        tops = jnp.zeros((DRAFT, 128), F32)
        totals = jnp.zeros((DRAFT, 128), F32)
        for h in range(HEADS):
            sub = slice(h * DRAFT, (h + 1) * DRAFT)
            o_send[b, h] = dot(mixed[sub], value_weight[h]).astype(BF16)
            tops = jnp.where(lane == h, top[sub] * scale, tops)
            totals = jnp.where(lane == h, total[sub], totals)
        turned = jnp.concatenate([tops, totals], axis=0).T
        for h in range(HEADS):
            ml_send[b, h] = turned[h : h + 1]

        @pl.when(b == 0)
        def _():
            pl.semaphore_wait(barrier, 30)

        for j in range(15):
            o_copy(b, j).start()
            ml_copy(b, j).start()
        for k in range(2):
            own_copy(b, k).start()

        @pl.when(b == 0)
        def _():
            got_out.wait()
            got_gain.wait()
            gain_rows[core] = gain[...].astype(F32)[None, :]
            for copy in got_vocab:
                copy.wait()
            for copy in swap_copies:
                copy.start()

    o_copies = [o_copy(b, j) for b in range(REQUESTS) for j in range(15)]
    ml_copies = [ml_copy(b, j) for b in range(REQUESTS) for j in range(15)]
    own_copies = [own_copy(b, k) for b in range(REQUESTS) for k in range(2)]

    g_copies = []
    for b in range(REQUESTS):
        for copy in ml_copies[b * 15 : (b + 1) * 15]:
            copy.wait_recv()
        for copy in own_copies[b * 2 : (b + 1) * 2]:
            copy.wait()
        gathered = jnp.concatenate(
            [ml_recv[b, j] for j in range(16)] + [jnp.full((112, 128), NEGATIVE, F32)], axis=0
        ).T
        tops, totals = gathered[:DRAFT], gathered[DRAFT:]
        shares = jnp.exp2(tops - jnp.max(tops, -1, keepdims=True))
        shares = shares / jnp.sum(shares * totals, -1, keepdims=True)
        shares = jnp.where(core == 0, shares[:32], shares[32:])
        for copy in o_copies[b * 15 : (b + 1) * 15]:
            copy.wait_recv()
        summed = jnp.zeros((32, 128), F32)
        for j in range(16):
            summed = summed + shares[:, j : j + 1] * o_recv[b, j].astype(F32)
        g_send[b] = summed.astype(BF16)
        place = g_full.at[b, :, pl.ds(pl.multiple_of(chip * 128, 128), 128)]
        for j, peer in enumerate(chip_peers):
            copy = pltpu.make_async_remote_copy(
                g_send.at[b],
                place,
                g_sems.at[0, b, j],
                g_sems.at[1, b, j],
                device_id={"seq": peer},
                device_id_type=MESH,
            )
            copy.start()
            g_copies.append(copy)
        copy = pltpu.make_async_copy(g_send.at[b], place, local_sems.at[b, 2])
        copy.start()
        own_copies.append(copy)

    a_copies, b_copies = [], []
    for b in range(REQUESTS):
        own_copies[4 + b].wait()
        if b == 0:
            swap_copies[0].wait_recv()
        for copy in g_copies[b * 7 : (b + 1) * 7]:
            copy.wait_recv()
        for side in range(2):
            attention = nt_dot(g_full[b], out_weight[side])
            for i in range(8):
                a_send[b, 2 * i + side] = attention[i * 4 : (i + 1) * 4].astype(BF16)
        for j, peer in enumerate(head_peers):
            copy = pltpu.make_async_remote_copy(
                a_send.at[b, peer],
                a_recv.at[b, j],
                a_sems.at[0, b, j],
                a_sems.at[1, b, j],
                device_id={"head": peer},
                device_id_type=MESH,
            )
            copy.start()
            a_copies.append(copy)
    for b in range(REQUESTS):
        summed = a_send[b, mine].astype(F32)
        for j in range(15):
            a_copies[b * 15 + j].wait_recv()
            summed = summed + a_recv[b, j].astype(F32)
        b_send[b] = summed.astype(BF16)
        for j, peer in enumerate(head_peers):
            copy = pltpu.make_async_remote_copy(
                b_send.at[b],
                b_full.at[b, mine],
                b_sems.at[0, b, j],
                b_sems.at[1, b, j],
                device_id={"head": peer},
                device_id_type=MESH,
            )
            copy.start()
            b_copies.append(copy)
        b_full[b, mine] = b_send[b]

    for copy in got_residual:
        copy.wait()
    for copy in swap_copies[1:4]:
        copy.wait_recv()
    square_parts, l_copies = [], []
    for b in range(REQUESTS):
        for copy in b_copies[b * 15 : (b + 1) * 15]:
            copy.wait_recv()
        squares = jnp.zeros((HALF, 1), F32)
        scaled = []
        for side in range(2):
            attention = jnp.concatenate(
                [b_full[b, 2 * i + side].astype(F32) for i in range(8)], axis=0
            )
            hidden = residual[side, b * HALF : (b + 1) * HALF].astype(F32) + attention
            squares = squares + jnp.sum(hidden * hidden, -1, keepdims=True)
            scaled.append((hidden * gain_rows[side]).astype(BF16))
        square_parts.append(squares)
        if b == 1:
            squares = jnp.concatenate(square_parts * 2, axis=0)
            s_send[...] = jnp.broadcast_to(squares, (TOKENS, 128)).T[0:1]
            s_copies = []
            for j, peer in enumerate(seq_peers):
                copy = pltpu.make_async_remote_copy(
                    s_send,
                    s_recv.at[j],
                    s_sems.at[0, j],
                    s_sems.at[1, j],
                    device_id={"seq": peer},
                    device_id_type=MESH,
                )
                copy.start()
                s_copies.append(copy)
        chips = 4 if b == 0 else 2
        for slot in range(8):
            if b == 0:
                swap_copies[4 + slot].wait_recv()
        for group in range(0, 8, chips):
            columns = slice(group * 512, (group + chips) * 512)
            part = dot(scaled[0], vocab[0, :, columns]) + dot(scaled[1], vocab[1, :, columns])
            part = part.astype(BF16)
            for k in range(2 * chips):
                l_send[b, group + k // 2, k % 2] = part[:, k * 256 : (k + 1) * 256]
            for j in range(2 * group, min(2 * (group + chips), 15)):
                slot, dk = (7, 1) if j == 14 else (j // 2, j % 2)
                copy = pltpu.make_async_remote_copy(
                    l_send.at[b, slot, lax.rem(core + dk, 2)],
                    l_recv.at[b, j],
                    l_sems.at[0, b, j],
                    l_sems.at[1, b, j],
                    device_id={"seq": seq_peers[j]},
                    device_id_type=MESH,
                )
                copy.start()
                l_copies.append(copy)
    squares = [s_send[...], jnp.zeros((1, TOKENS), F32)]
    for j, (_, _, dk) in enumerate(SEQ_STEPS):
        s_copies[j].wait_recv()
        squares[dk] = squares[dk] + s_recv[j]
    scales = [
        jnp.broadcast_to(lax.rsqrt(total / model_width + EPSILON), (128, TOKENS)).T
        for total in squares
    ]
    for b in range(REQUESTS):
        sums = [l_send[b, 7, core].astype(F32), jnp.zeros((HALF, 256), F32)]
        for j, (_, _, dk) in enumerate(SEQ_STEPS):
            l_copies[b * 15 + j].wait_recv()
            sums[dk] = sums[dk] + l_recv[b, j].astype(F32)
        for dk in range(2):
            owner = lax.rem(core + dk, 2)
            rows = pl.ds(pl.multiple_of(b * DRAFT + owner * HALF, HALF), HALF)
            logits[rows, :] = (sums[dk] * scales[dk][b * HALF : (b + 1) * HALF, 0:1]).astype(BF16)
    for copy in o_copies + ml_copies + swap_copies + g_copies + a_copies + b_copies + s_copies + l_copies:
        copy.wait_send()


def per_device(
    latent_cache,
    draft_latent,
    query_nope,
    query_rope,
    parents,
    lengths,
    key_weight,
    value_weight,
    out_weight,
    residual,
    norm_gain,
    vocab_weight,
):
    local_width = residual.shape[2]
    model_width = local_width * lax.axis_size("seq")
    operands = [
        lengths,
        parents,
        jnp.swapaxes(latent_cache, 1, 2),
        draft_latent,
        query_nope.reshape(TOKENS * HEADS, 128),
        query_rope.reshape(TOKENS * HEADS, ROPE),
        key_weight,
        value_weight,
        out_weight.T,
        residual.reshape(TOKENS, local_width),
        norm_gain,
        vocab_weight,
    ]
    hbm = pl.BlockSpec(memory_space=pltpu.HBM)
    dma = pltpu.SemaphoreType.DMA
    logits = pl.pallas_call(
        functools.partial(kernel, model_width),
        out_shape=jax.ShapeDtypeStruct((TOKENS, 256), BF16),
        in_specs=[hbm] * 12,
        out_specs=pl.BlockSpec(memory_space=pltpu.VMEM),
        scratch_shapes=[
            pltpu.SMEM((REQUESTS,), jnp.int32),
            pltpu.VMEM((REQUESTS, DRAFT), jnp.int32),
            pltpu.VMEM((REQUESTS, WIDTH, KEYS), BF16),
            pltpu.VMEM((REQUESTS, 4, WIDTH), BF16),
            pltpu.VMEM((EXTRA, WIDTH), BF16),
            pltpu.VMEM((REQUESTS, DRAFT, EXTRA), F32),
            pltpu.VMEM((TOKENS * HEADS, 128), BF16),
            pltpu.VMEM((TOKENS * HEADS, ROPE), BF16),
            pltpu.VMEM((HEADS, 128, LATENT), BF16),
            pltpu.VMEM((HEADS, LATENT, 128), BF16),
            pltpu.VMEM((2, local_width, 1024), BF16),
            pltpu.VMEM((2, 2 * HALF, local_width), BF16),
            pltpu.VMEM((local_width,), BF16),
            pltpu.VMEM((2, 1, local_width), F32),
            pltpu.VMEM((2, local_width, 4096), BF16),
            pltpu.VMEM((TOKENS * HEADS, 128), F32),
            pltpu.VMEM((TOKENS * HEADS, ROPE), F32),
            pltpu.VMEM((REQUESTS, HEADS * DRAFT, WIDTH), BF16),
            pltpu.VMEM((REQUESTS, HEADS, DRAFT, 128), BF16),
            pltpu.VMEM((REQUESTS, 16, 32, 128), BF16),
            pltpu.VMEM((REQUESTS, HEADS, 1, 128), F32),
            pltpu.VMEM((REQUESTS, 16, 1, 128), F32),
            pltpu.VMEM((REQUESTS, 32, 128), BF16),
            pltpu.VMEM((REQUESTS, HALF, 1024), BF16),
            pltpu.VMEM((REQUESTS, 16, 4, local_width), BF16),
            pltpu.VMEM((REQUESTS, 15, 4, local_width), BF16),
            pltpu.VMEM((REQUESTS, 4, local_width), BF16),
            pltpu.VMEM((REQUESTS, 16, 4, local_width), BF16),
            pltpu.VMEM((1, TOKENS), F32),
            pltpu.VMEM((15, 1, TOKENS), F32),
            pltpu.VMEM((REQUESTS, 8, 2, HALF, 256), BF16),
            pltpu.VMEM((REQUESTS, 15, HALF, 256), BF16),
            dma((20,)),
            dma((8,)),
            dma((REQUESTS, 3)),
            dma((2, REQUESTS, 15)),
            dma((2, REQUESTS, 15)),
            dma((2, REQUESTS, 7)),
            dma((2, REQUESTS, 15)),
            dma((2, REQUESTS, 15)),
            dma((2, 15)),
            dma((2, 12)),
            dma((2, REQUESTS, 15)),
        ],
        compiler_params=pltpu.CompilerParams(
            collective_id=0, has_side_effects=True, vmem_limit_bytes=48 * 1024 * 1024
        ),
    )(
        *[pltpu.with_memory_space_constraint(a, pltpu.HBM) for a in operands],
    )
    return logits.reshape(REQUESTS, DRAFT, 256)


def solution(mesh):
    in_specs = (
        P(None, "seq", None),
        P(None, "seq", None),
        P(None, None, "head", None),
        P(None, None, "head", None),
        P(),
        P(),
        P("head", None, None),
        P("head", None, None),
        P("head", "seq"),
        P(None, None, "seq"),
        P("seq"),
        P("seq", "head"),
    )
    out_specs = P(None, None, ("head", "seq"))
    return jax.shard_map(
        per_device, mesh=mesh, in_specs=in_specs, out_specs=out_specs, check_vma=False
    )
```

```python
import functools
import math

import jax
import jax.numpy as jnp
from jax import lax
from jax.experimental import pallas as pl
from jax.experimental.pallas import tpu as pltpu
from jax.sharding import PartitionSpec as P

MESH = pl.DeviceIdType.MESH
NEGATIVE = -1e30
EPSILON = 1e-06
F32 = jnp.float32
BF16 = jnp.bfloat16

CHIP_STEPS = [(2, 1), (1, 1), (3, 1), (2, 0), (0, 1), (1, 0), (3, 0)]
SEQ_STEPS = [(dy, dx, dk) for dy, dx in CHIP_STEPS for dk in (0, 1)] + [(0, 0, 1)]
HEAD_STEPS = [(dx, dz) for dz in (4, 3, 5, 2, 6, 1, 7) for dx in (1, 0)] + [(1, 0)]
REQUESTS, DRAFT, HEADS, LATENT, ROPE, WIDTH = 2, 64, 8, 512, 64, 576
TOKENS = REQUESTS * DRAFT
KEYS, EXTRA = 2048, 128
KEY_PARTS = [slice(0, KEYS // 2), slice(KEYS // 2, KEYS)]
HALF = DRAFT // 2


def nt_dot(a, b):
    return lax.dot_general(a, b, (((1,), (1,)), ((), ())), preferred_element_type=F32)


def dot(a, b):
    return jnp.dot(a, b, preferred_element_type=F32)


def kernel(
    model_width,
    lengths_hbm,
    parents_hbm,
    cache_hbm,
    draft_hbm,
    nope_hbm,
    rope_hbm,
    key_hbm,
    value_hbm,
    out_hbm,
    residual_hbm,
    gain_hbm,
    vocab_hbm,
    logits,
    lengths,
    parents,
    kbuf,
    draft,
    dbuf,
    tree_bias,
    nope,
    rope,
    key_weight,
    value_weight,
    out_weight,
    residual,
    gain,
    gain_rows,
    vocab,
    nope32,
    rope32,
    qbuf,
    o_send,
    o_recv,
    ml_send,
    ml_recv,
    g_send,
    g_full,
    a_send,
    a_recv,
    b_send,
    b_full,
    s_send,
    s_recv,
    l_send,
    l_recv,
    load_sems,
    vocab_sems,
    local_sems,
    o_sems,
    ml_sems,
    g_sems,
    a_sems,
    b_sems,
    s_sems,
    swap_sems,
    l_sems,
):
    seat = lax.axis_index("seq")
    mine = lax.axis_index("head")
    y = lax.div(seat, 4)
    xh = lax.rem(lax.div(seat, 2), 2)
    core = lax.rem(seat, 2)
    chip = lax.div(seat, 2)

    def seat_at(dy, dx, dk):
        return lax.rem(y + dy, 4) * 4 + lax.rem(xh + dx, 2) * 2 + lax.rem(core + dk, 2)

    seq_peers = [seat_at(*step) for step in SEQ_STEPS]
    chip_peers = seq_peers[0:14:2]
    head_peers = [
        lax.rem(lax.div(mine, 8) + dx, 2) * 8 + lax.rem(lax.rem(mine, 8) + dz, 8)
        for dx, dz in HEAD_STEPS
    ]

    loads = []

    def load(src, dst):
        copy = pltpu.make_async_copy(src, dst, load_sems.at[len(loads)])
        loads.append(copy)
        copy.start()
        return copy

    got_parents = load(parents_hbm, parents)
    got_nope = load(nope_hbm, nope)
    got_key = load(key_hbm, key_weight)
    got_rope = load(rope_hbm, rope)
    got_draft = load(draft_hbm, draft)
    got_lengths = load(lengths_hbm, lengths)
    def load_cache(b):
        parts = [pl.ds(start, WIDTH // 4) for start in range(0, WIDTH, WIDTH // 4)]
        return [load(cache_hbm.at[b, part, :], kbuf.at[b, part, :]) for part in parts]

    got_cache = [load_cache(0)]

    barrier = pltpu.get_barrier_semaphore()
    for peer in seq_peers:
        pl.semaphore_signal(barrier, inc=1, device_id={"seq": peer}, device_id_type=MESH)
    for peer in head_peers:
        pl.semaphore_signal(barrier, inc=1, device_id={"head": peer}, device_id_type=MESH)

    for copy in (got_parents, got_draft, got_nope, got_rope, got_key):
        copy.wait()
    got_value = load(value_hbm, value_weight)
    row = lax.broadcasted_iota(jnp.int32, (DRAFT, DRAFT), 0)
    column = lax.broadcasted_iota(jnp.int32, (DRAFT, DRAFT), 1)
    reaches = [
        jnp.where((parents[b : b + 1, :] == row) | (row == column), 1.0, 0.0).astype(BF16)
        for b in range(REQUESTS)
    ]
    for _ in range(6):
        reaches = [jnp.where(dot(r, r) > 0.5, 1.0, 0.0).astype(BF16) for r in reaches]
    row = lax.broadcasted_iota(jnp.int32, (DRAFT, EXTRA), 0)
    column = lax.broadcasted_iota(jnp.int32, (DRAFT, EXTRA), 1)
    for b in range(REQUESTS):
        chosen = (column >= 4 * b) & (column < 4 * b + 4) & (row == seat * 4 + column - 4 * b)
        chosen = jnp.where(chosen, 1.0, 0.0).astype(BF16)
        reached = lax.dot_general(
            reaches[b], chosen, (((0,), (0,)), ((), ())), preferred_element_type=F32
        )
        tree_bias[b] = jnp.where(reached > 0.5, 0.0, NEGATIVE)
    dbuf[...] = jnp.zeros((EXTRA, WIDTH), BF16)
    dbuf[0:8, :] = jnp.concatenate([draft[b].astype(F32) for b in range(REQUESTS)], axis=0).astype(BF16)

    nope32[...] = nope[...].astype(F32)
    rope32[...] = rope[...].astype(F32)
    for h in range(HEADS):
        picked = nope32[pl.ds(h, TOKENS, stride=HEADS), :].astype(BF16)
        absorbed = dot(picked, key_weight[h]).astype(BF16)
        turned = rope32[pl.ds(h, TOKENS, stride=HEADS), :].astype(BF16)
        for b in range(REQUESTS):
            rows = pl.ds(h * DRAFT, DRAFT)
            qbuf[b, rows, 0:LATENT] = absorbed[b * DRAFT : (b + 1) * DRAFT]
            qbuf[b, rows, LATENT:WIDTH] = turned[b * DRAFT : (b + 1) * DRAFT]

    scale = math.log2(math.e) / math.sqrt(192.0)
    lane = lax.broadcasted_iota(jnp.int32, (DRAFT, 128), 1)
    position = seat * KEYS + lax.broadcasted_iota(jnp.int32, (1, KEYS), 1)
    partner = seq_peers[14]

    for copy in got_cache[0] + [got_lengths, got_value]:
        copy.wait()

    got_cache.append(load_cache(1))
    got_out = load(out_hbm, out_weight.at[core])
    got_residual = [
        load(
            residual_hbm.at[pl.ds(pl.multiple_of(b * DRAFT + core * HALF, HALF), HALF), :],
            residual.at[core, pl.ds(b * HALF, HALF), :],
        )
        for b in range(REQUESTS)
    ]
    got_gain = load(gain_hbm, gain)

    got_vocab = []
    for slot, (dy, dx) in enumerate(CHIP_STEPS + [(0, 0)]):
        owner = lax.div(seat_at(dy, dx, 0), 2)
        columns = pl.ds(pl.multiple_of(owner * 512, 512), 512)
        copy = pltpu.make_async_copy(
            vocab_hbm.at[:, columns], vocab.at[core, :, pl.ds(slot * 512, 512)], vocab_sems.at[slot]
        )
        copy.start()
        got_vocab.append(copy)

    def o_copy(b, j):
        peer = seq_peers[j]
        half = pl.ds(pl.multiple_of(lax.rem(peer, 2) * HALF, HALF), HALF)
        return pltpu.make_async_remote_copy(
            o_send.at[b, lax.div(peer, 2), half, :],
            o_recv.at[b, j],
            o_sems.at[0, b, j],
            o_sems.at[1, b, j],
            device_id={"seq": peer},
            device_id_type=MESH,
        )

    def ml_copy(b, j):
        peer = seq_peers[j]
        return pltpu.make_async_remote_copy(
            ml_send.at[b, lax.div(peer, 2)],
            ml_recv.at[b, j],
            ml_sems.at[0, b, j],
            ml_sems.at[1, b, j],
            device_id={"seq": peer},
            device_id_type=MESH,
        )

    def own_copy(b, k):
        half = pl.ds(pl.multiple_of(core * HALF, HALF), HALF)
        src, dst = (
            (o_send.at[b, chip, half, :], o_recv.at[b, 15]),
            (ml_send.at[b, chip], ml_recv.at[b, 15]),
        )[k]
        return pltpu.make_async_copy(src, dst, local_sems.at[b, k])

    swaps = [
        (out_weight.at[core], out_weight.at[core]),
        (gain_rows.at[core], gain_rows.at[core]),
    ]
    for request in range(REQUESTS):
        other_rows = pl.multiple_of(request * DRAFT + (1 - core) * HALF, HALF)
        swaps.append(
            (
                residual_hbm.at[pl.ds(other_rows, HALF), :],
                residual.at[core, pl.ds(request * HALF, HALF), :],
            )
        )
    for slot in range(8):
        place = vocab.at[core, :, pl.ds(slot * 512, 512)]
        swaps.append((place, place))
    swap_copies = [
        pltpu.make_async_remote_copy(
            src,
            dst,
            swap_sems.at[0, k],
            swap_sems.at[1, k],
            device_id={"seq": partner},
            device_id_type=MESH,
        )
        for k, (src, dst) in enumerate(swaps)
    ]

    @pl.loop(0, REQUESTS)
    def _(b):
        @pl.when(b == 1)
        def _():
            for copy in got_cache[1]:
                copy.wait()

        tree = jnp.concatenate([tree_bias[b]] * HEADS, axis=0)
        drafted = nt_dot(qbuf[b], dbuf[...]) + tree
        top = jnp.max(drafted, -1, keepdims=True)
        scores = []
        for columns in KEY_PARTS:
            live_bias = jnp.where(position[:, columns] < lengths[b], 0.0, NEGATIVE)
            scores.append(dot(qbuf[b], kbuf[b, :, columns]) + live_bias)
            top = jnp.maximum(top, jnp.max(scores[-1], -1, keepdims=True))
        drafted = jnp.exp2((drafted - top) * scale)
        total = jnp.sum(drafted, -1, keepdims=True)
        mixed = dot(drafted.astype(BF16), dbuf[:, 0:LATENT])
        for columns, cached in zip(KEY_PARTS, scores):
            cached = jnp.exp2((cached - top) * scale)
            total = total + jnp.sum(cached, -1, keepdims=True)
            mixed = mixed + nt_dot(cached.astype(BF16), kbuf[b, 0:LATENT, columns])
        mixed = mixed.astype(BF16)
        tops = jnp.zeros((DRAFT, 128), F32)
        totals = jnp.zeros((DRAFT, 128), F32)
        for h in range(HEADS):
            sub = slice(h * DRAFT, (h + 1) * DRAFT)
            o_send[b, h] = dot(mixed[sub], value_weight[h]).astype(BF16)
            tops = jnp.where(lane == h, top[sub] * scale, tops)
            totals = jnp.where(lane == h, total[sub], totals)
        turned = jnp.concatenate([tops, totals], axis=0).T
        for h in range(HEADS):
            ml_send[b, h] = turned[h : h + 1]

        @pl.when(b == 0)
        def _():
            pl.semaphore_wait(barrier, 30)

        for j in range(15):
            o_copy(b, j).start()
            ml_copy(b, j).start()
        for k in range(2):
            own_copy(b, k).start()

        @pl.when(b == 0)
        def _():
            got_out.wait()
            got_gain.wait()
            gain_rows[core] = gain[...].astype(F32)[None, :]
            for copy in got_vocab:
                copy.wait()
            for copy in swap_copies:
                copy.start()

    o_copies = [o_copy(b, j) for b in range(REQUESTS) for j in range(15)]
    ml_copies = [ml_copy(b, j) for b in range(REQUESTS) for j in range(15)]
    own_copies = [own_copy(b, k) for b in range(REQUESTS) for k in range(2)]

    g_copies = []
    for b in range(REQUESTS):
        for copy in ml_copies[b * 15 : (b + 1) * 15]:
            copy.wait_recv()
        for copy in own_copies[b * 2 : (b + 1) * 2]:
            copy.wait()
        gathered = jnp.concatenate(
            [ml_recv[b, j] for j in range(16)] + [jnp.full((112, 128), NEGATIVE, F32)], axis=0
        ).T
        tops, totals = gathered[:DRAFT], gathered[DRAFT:]
        shares = jnp.exp2(tops - jnp.max(tops, -1, keepdims=True))
        shares = shares / jnp.sum(shares * totals, -1, keepdims=True)
        shares = jnp.where(core == 0, shares[:32], shares[32:])
        for copy in o_copies[b * 15 : (b + 1) * 15]:
            copy.wait_recv()
        summed = jnp.zeros((32, 128), F32)
        for j in range(16):
            summed = summed + shares[:, j : j + 1] * o_recv[b, j].astype(F32)
        g_send[b] = summed.astype(BF16)
        place = g_full.at[b, :, pl.ds(pl.multiple_of(chip * 128, 128), 128)]
        for j, peer in enumerate(chip_peers):
            copy = pltpu.make_async_remote_copy(
                g_send.at[b],
                place,
                g_sems.at[0, b, j],
                g_sems.at[1, b, j],
                device_id={"seq": peer},
                device_id_type=MESH,
            )
            copy.start()
            g_copies.append(copy)
        copy = pltpu.make_async_copy(g_send.at[b], place, local_sems.at[b, 2])
        copy.start()
        own_copies.append(copy)

    a_copies, b_copies = [], []
    for b in range(REQUESTS):
        own_copies[4 + b].wait()
        if b == 0:
            swap_copies[0].wait_recv()
        for copy in g_copies[b * 7 : (b + 1) * 7]:
            copy.wait_recv()
        for side in range(2):
            attention = nt_dot(g_full[b], out_weight[side])
            for i in range(8):
                a_send[b, 2 * i + side] = attention[i * 4 : (i + 1) * 4].astype(BF16)
        for j, peer in enumerate(head_peers):
            copy = pltpu.make_async_remote_copy(
                a_send.at[b, peer],
                a_recv.at[b, j],
                a_sems.at[0, b, j],
                a_sems.at[1, b, j],
                device_id={"head": peer},
                device_id_type=MESH,
            )
            copy.start()
            a_copies.append(copy)
    for b in range(REQUESTS):
        summed = a_send[b, mine].astype(F32)
        for j in range(15):
            a_copies[b * 15 + j].wait_recv()
            summed = summed + a_recv[b, j].astype(F32)
        b_send[b] = summed.astype(BF16)
        for j, peer in enumerate(head_peers):
            copy = pltpu.make_async_remote_copy(
                b_send.at[b],
                b_full.at[b, mine],
                b_sems.at[0, b, j],
                b_sems.at[1, b, j],
                device_id={"head": peer},
                device_id_type=MESH,
            )
            copy.start()
            b_copies.append(copy)
        b_full[b, mine] = b_send[b]

    for copy in got_residual:
        copy.wait()
    for copy in swap_copies[1:4]:
        copy.wait_recv()
    square_parts, l_copies = [], []
    for b in range(REQUESTS):
        for copy in b_copies[b * 15 : (b + 1) * 15]:
            copy.wait_recv()
        squares = jnp.zeros((HALF, 1), F32)
        scaled = []
        for side in range(2):
            attention = jnp.concatenate(
                [b_full[b, 2 * i + side].astype(F32) for i in range(8)], axis=0
            )
            hidden = residual[side, b * HALF : (b + 1) * HALF].astype(F32) + attention
            squares = squares + jnp.sum(hidden * hidden, -1, keepdims=True)
            scaled.append((hidden * gain_rows[side]).astype(BF16))
        square_parts.append(squares)
        chips = 4 if b == 0 else 2
        for slot in range(8):
            if b == 0:
                swap_copies[4 + slot].wait_recv()
        for group in range(0, 8, chips):
            columns = slice(group * 512, (group + chips) * 512)
            part = dot(scaled[0], vocab[0, :, columns]) + dot(scaled[1], vocab[1, :, columns])
            part = part.astype(BF16)
            for k in range(2 * chips):
                l_send[b, group + k // 2, k % 2] = part[:, k * 256 : (k + 1) * 256]
            for j in range(2 * group, min(2 * (group + chips), 15)):
                slot, dk = (7, 1) if j == 14 else (j // 2, j % 2)
                copy = pltpu.make_async_remote_copy(
                    l_send.at[b, slot, lax.rem(core + dk, 2)],
                    l_recv.at[b, j],
                    l_sems.at[0, b, j],
                    l_sems.at[1, b, j],
                    device_id={"seq": seq_peers[j]},
                    device_id_type=MESH,
                )
                copy.start()
                l_copies.append(copy)
            if b == 1 and group == 0:
                squares = jnp.concatenate(square_parts * 2, axis=0)
                s_send[...] = jnp.broadcast_to(squares, (TOKENS, 128)).T[0:1]
                s_copies = []
                for j, peer in enumerate(seq_peers):
                    copy = pltpu.make_async_remote_copy(
                        s_send,
                        s_recv.at[j],
                        s_sems.at[0, j],
                        s_sems.at[1, j],
                        device_id={"seq": peer},
                        device_id_type=MESH,
                    )
                    copy.start()
                    s_copies.append(copy)
    squares = [s_send[...], jnp.zeros((1, TOKENS), F32)]
    for j, (_, _, dk) in enumerate(SEQ_STEPS):
        s_copies[j].wait_recv()
        squares[dk] = squares[dk] + s_recv[j]
    scales = [
        jnp.broadcast_to(lax.rsqrt(total / model_width + EPSILON), (128, TOKENS)).T
        for total in squares
    ]
    for b in range(REQUESTS):
        sums = [l_send[b, 7, core].astype(F32), jnp.zeros((HALF, 256), F32)]
        for j, (_, _, dk) in enumerate(SEQ_STEPS):
            l_copies[b * 15 + j].wait_recv()
            sums[dk] = sums[dk] + l_recv[b, j].astype(F32)
        for dk in range(2):
            owner = lax.rem(core + dk, 2)
            rows = pl.ds(pl.multiple_of(b * DRAFT + owner * HALF, HALF), HALF)
            logits[rows, :] = (sums[dk] * scales[dk][b * HALF : (b + 1) * HALF, 0:1]).astype(BF16)
    for copy in o_copies + ml_copies + swap_copies + g_copies + a_copies + b_copies + s_copies + l_copies:
        copy.wait_send()


def per_device(
    latent_cache,
    draft_latent,
    query_nope,
    query_rope,
    parents,
    lengths,
    key_weight,
    value_weight,
    out_weight,
    residual,
    norm_gain,
    vocab_weight,
):
    local_width = residual.shape[2]
    model_width = local_width * lax.axis_size("seq")
    operands = [
        lengths,
        parents,
        jnp.swapaxes(latent_cache, 1, 2),
        draft_latent,
        query_nope.reshape(TOKENS * HEADS, 128),
        query_rope.reshape(TOKENS * HEADS, ROPE),
        key_weight,
        value_weight,
        out_weight.T,
        residual.reshape(TOKENS, local_width),
        norm_gain,
        vocab_weight,
    ]
    hbm = pl.BlockSpec(memory_space=pltpu.HBM)
    dma = pltpu.SemaphoreType.DMA
    logits = pl.pallas_call(
        functools.partial(kernel, model_width),
        out_shape=jax.ShapeDtypeStruct((TOKENS, 256), BF16),
        in_specs=[hbm] * 12,
        out_specs=pl.BlockSpec(memory_space=pltpu.VMEM),
        scratch_shapes=[
            pltpu.SMEM((REQUESTS,), jnp.int32),
            pltpu.VMEM((REQUESTS, DRAFT), jnp.int32),
            pltpu.VMEM((REQUESTS, WIDTH, KEYS), BF16),
            pltpu.VMEM((REQUESTS, 4, WIDTH), BF16),
            pltpu.VMEM((EXTRA, WIDTH), BF16),
            pltpu.VMEM((REQUESTS, DRAFT, EXTRA), F32),
            pltpu.VMEM((TOKENS * HEADS, 128), BF16),
            pltpu.VMEM((TOKENS * HEADS, ROPE), BF16),
            pltpu.VMEM((HEADS, 128, LATENT), BF16),
            pltpu.VMEM((HEADS, LATENT, 128), BF16),
            pltpu.VMEM((2, local_width, 1024), BF16),
            pltpu.VMEM((2, 2 * HALF, local_width), BF16),
            pltpu.VMEM((local_width,), BF16),
            pltpu.VMEM((2, 1, local_width), F32),
            pltpu.VMEM((2, local_width, 4096), BF16),
            pltpu.VMEM((TOKENS * HEADS, 128), F32),
            pltpu.VMEM((TOKENS * HEADS, ROPE), F32),
            pltpu.VMEM((REQUESTS, HEADS * DRAFT, WIDTH), BF16),
            pltpu.VMEM((REQUESTS, HEADS, DRAFT, 128), BF16),
            pltpu.VMEM((REQUESTS, 16, 32, 128), BF16),
            pltpu.VMEM((REQUESTS, HEADS, 1, 128), F32),
            pltpu.VMEM((REQUESTS, 16, 1, 128), F32),
            pltpu.VMEM((REQUESTS, 32, 128), BF16),
            pltpu.VMEM((REQUESTS, HALF, 1024), BF16),
            pltpu.VMEM((REQUESTS, 16, 4, local_width), BF16),
            pltpu.VMEM((REQUESTS, 15, 4, local_width), BF16),
            pltpu.VMEM((REQUESTS, 4, local_width), BF16),
            pltpu.VMEM((REQUESTS, 16, 4, local_width), BF16),
            pltpu.VMEM((1, TOKENS), F32),
            pltpu.VMEM((15, 1, TOKENS), F32),
            pltpu.VMEM((REQUESTS, 8, 2, HALF, 256), BF16),
            pltpu.VMEM((REQUESTS, 15, HALF, 256), BF16),
            dma((20,)),
            dma((8,)),
            dma((REQUESTS, 3)),
            dma((2, REQUESTS, 15)),
            dma((2, REQUESTS, 15)),
            dma((2, REQUESTS, 7)),
            dma((2, REQUESTS, 15)),
            dma((2, REQUESTS, 15)),
            dma((2, 15)),
            dma((2, 12)),
            dma((2, REQUESTS, 15)),
        ],
        compiler_params=pltpu.CompilerParams(
            collective_id=0, has_side_effects=True, vmem_limit_bytes=48 * 1024 * 1024
        ),
    )(
        *[pltpu.with_memory_space_constraint(a, pltpu.HBM) for a in operands],
    )
    return logits.reshape(REQUESTS, DRAFT, 256)


def solution(mesh):
    in_specs = (
        P(None, "seq", None),
        P(None, "seq", None),
        P(None, None, "head", None),
        P(None, None, "head", None),
        P(),
        P(),
        P("head", None, None),
        P("head", None, None),
        P("head", "seq"),
        P(None, None, "seq"),
        P("seq"),
        P("seq", "head"),
    )
    out_specs = P(None, None, ("head", "seq"))
    return jax.shard_map(
        per_device, mesh=mesh, in_specs=in_specs, out_specs=out_specs, check_vma=False
    )
```

```python
import functools
import math

import jax
import jax.numpy as jnp
from jax import lax
from jax.experimental import pallas as pl
from jax.experimental.pallas import tpu as pltpu
from jax.sharding import PartitionSpec as P

MESH = pl.DeviceIdType.MESH
NEGATIVE = -1e30
EPSILON = 1e-06
F32 = jnp.float32
BF16 = jnp.bfloat16

CHIP_STEPS = [(2, 1), (1, 1), (3, 1), (2, 0), (0, 1), (1, 0), (3, 0)]
SEQ_STEPS = [(dy, dx, dk) for dy, dx in CHIP_STEPS for dk in (0, 1)] + [(0, 0, 1)]
REQUESTS, DRAFT, HEADS, LATENT, ROPE, WIDTH = 2, 64, 8, 512, 64, 576
TOKENS = REQUESTS * DRAFT
KEYS, EXTRA = 2048, 128
KEY_PARTS = [slice(0, KEYS // 2), slice(KEYS // 2, KEYS)]
HALF = DRAFT // 2


def nt_dot(a, b):
    return lax.dot_general(a, b, (((1,), (1,)), ((), ())), preferred_element_type=F32)


def dot(a, b):
    return jnp.dot(a, b, preferred_element_type=F32)


def kernel(
    model_width,
    lengths_hbm,
    parents_hbm,
    cache_hbm,
    draft_hbm,
    nope_hbm,
    rope_hbm,
    key_hbm,
    value_hbm,
    out_hbm,
    residual_hbm,
    gain_hbm,
    vocab_hbm,
    logits,
    lengths,
    parents,
    kbuf,
    draft,
    dbuf,
    tree_bias,
    nope,
    rope,
    key_weight,
    value_weight,
    out_weight,
    residual,
    gain,
    gain_rows,
    vocab,
    nope32,
    rope32,
    qbuf,
    o_send,
    o_recv,
    ml_send,
    ml_recv,
    g_send,
    g_full,
    a_send,
    a_recv,
    b_send,
    b_full,
    s_send,
    s_recv,
    l_send,
    l_recv,
    load_sems,
    vocab_sems,
    local_sems,
    o_sems,
    ml_sems,
    g_sems,
    a_sems,
    b_sems,
    s_sems,
    swap_sems,
    l_sems,
):
    seat = lax.axis_index("seq")
    mine = lax.axis_index("head")
    y = lax.div(seat, 4)
    xh = lax.rem(lax.div(seat, 2), 2)
    core = lax.rem(seat, 2)
    chip = lax.div(seat, 2)

    def seat_at(dy, dx, dk):
        return lax.rem(y + dy, 4) * 4 + lax.rem(xh + dx, 2) * 2 + lax.rem(core + dk, 2)

    seq_peers = [seat_at(*step) for step in SEQ_STEPS]
    chip_peers = seq_peers[0:14:2]
    head_peers = [lax.rem(mine + j, 16) for j in range(1, 16)]

    loads = []

    def load(src, dst):
        copy = pltpu.make_async_copy(src, dst, load_sems.at[len(loads)])
        loads.append(copy)
        copy.start()
        return copy

    got_parents = load(parents_hbm, parents)
    got_nope = load(nope_hbm, nope)
    got_key = load(key_hbm, key_weight)
    got_rope = load(rope_hbm, rope)
    got_draft = load(draft_hbm, draft)
    got_lengths = load(lengths_hbm, lengths)
    def load_cache(b):
        parts = [pl.ds(start, WIDTH // 4) for start in range(0, WIDTH, WIDTH // 4)]
        return [load(cache_hbm.at[b, part, :], kbuf.at[b, part, :]) for part in parts]

    got_cache = [load_cache(0)]

    barrier = pltpu.get_barrier_semaphore()
    for peer in seq_peers:
        pl.semaphore_signal(barrier, inc=1, device_id={"seq": peer}, device_id_type=MESH)
    for peer in head_peers:
        pl.semaphore_signal(barrier, inc=1, device_id={"head": peer}, device_id_type=MESH)

    for copy in (got_parents, got_draft, got_nope, got_rope, got_key):
        copy.wait()
    got_value = load(value_hbm, value_weight)
    row = lax.broadcasted_iota(jnp.int32, (DRAFT, DRAFT), 0)
    column = lax.broadcasted_iota(jnp.int32, (DRAFT, DRAFT), 1)
    reaches = [
        jnp.where((parents[b : b + 1, :] == row) | (row == column), 1.0, 0.0).astype(BF16)
        for b in range(REQUESTS)
    ]
    for _ in range(6):
        reaches = [jnp.where(dot(r, r) > 0.5, 1.0, 0.0).astype(BF16) for r in reaches]
    row = lax.broadcasted_iota(jnp.int32, (DRAFT, EXTRA), 0)
    column = lax.broadcasted_iota(jnp.int32, (DRAFT, EXTRA), 1)
    for b in range(REQUESTS):
        chosen = (column >= 4 * b) & (column < 4 * b + 4) & (row == seat * 4 + column - 4 * b)
        chosen = jnp.where(chosen, 1.0, 0.0).astype(BF16)
        reached = lax.dot_general(
            reaches[b], chosen, (((0,), (0,)), ((), ())), preferred_element_type=F32
        )
        tree_bias[b] = jnp.where(reached > 0.5, 0.0, NEGATIVE)
    dbuf[...] = jnp.zeros((EXTRA, WIDTH), BF16)
    dbuf[0:8, :] = jnp.concatenate([draft[b].astype(F32) for b in range(REQUESTS)], axis=0).astype(BF16)

    nope32[...] = nope[...].astype(F32)
    rope32[...] = rope[...].astype(F32)
    for h in range(HEADS):
        picked = nope32[pl.ds(h, TOKENS, stride=HEADS), :].astype(BF16)
        absorbed = dot(picked, key_weight[h]).astype(BF16)
        turned = rope32[pl.ds(h, TOKENS, stride=HEADS), :].astype(BF16)
        for b in range(REQUESTS):
            rows = pl.ds(h * DRAFT, DRAFT)
            qbuf[b, rows, 0:LATENT] = absorbed[b * DRAFT : (b + 1) * DRAFT]
            qbuf[b, rows, LATENT:WIDTH] = turned[b * DRAFT : (b + 1) * DRAFT]

    scale = math.log2(math.e) / math.sqrt(192.0)
    lane = lax.broadcasted_iota(jnp.int32, (DRAFT, 128), 1)
    position = seat * KEYS + lax.broadcasted_iota(jnp.int32, (1, KEYS), 1)
    partner = seq_peers[14]

    for copy in got_cache[0] + [got_lengths, got_value]:
        copy.wait()

    got_cache.append(load_cache(1))
    got_out = load(out_hbm, out_weight.at[core])
    got_residual = [
        load(
            residual_hbm.at[pl.ds(pl.multiple_of(b * DRAFT + core * HALF, HALF), HALF), :],
            residual.at[core, pl.ds(b * HALF, HALF), :],
        )
        for b in range(REQUESTS)
    ]
    got_gain = load(gain_hbm, gain)

    got_vocab = []
    for slot, (dy, dx) in enumerate(CHIP_STEPS + [(0, 0)]):
        owner = lax.div(seat_at(dy, dx, 0), 2)
        columns = pl.ds(pl.multiple_of(owner * 512, 512), 512)
        copy = pltpu.make_async_copy(
            vocab_hbm.at[:, columns], vocab.at[core, :, pl.ds(slot * 512, 512)], vocab_sems.at[slot]
        )
        copy.start()
        got_vocab.append(copy)

    def o_copy(b, j):
        peer = seq_peers[j]
        half = pl.ds(pl.multiple_of(lax.rem(peer, 2) * HALF, HALF), HALF)
        return pltpu.make_async_remote_copy(
            o_send.at[b, lax.div(peer, 2), half, :],
            o_recv.at[b, j],
            o_sems.at[0, b, j],
            o_sems.at[1, b, j],
            device_id={"seq": peer},
            device_id_type=MESH,
        )

    def ml_copy(b, j):
        peer = seq_peers[j]
        return pltpu.make_async_remote_copy(
            ml_send.at[b, lax.div(peer, 2)],
            ml_recv.at[b, j],
            ml_sems.at[0, b, j],
            ml_sems.at[1, b, j],
            device_id={"seq": peer},
            device_id_type=MESH,
        )

    def own_copy(b, k):
        half = pl.ds(pl.multiple_of(core * HALF, HALF), HALF)
        src, dst = (
            (o_send.at[b, chip, half, :], o_recv.at[b, 15]),
            (ml_send.at[b, chip], ml_recv.at[b, 15]),
        )[k]
        return pltpu.make_async_copy(src, dst, local_sems.at[b, k])

    swaps = [
        (out_weight.at[core], out_weight.at[core]),
        (gain_rows.at[core], gain_rows.at[core]),
    ]
    for request in range(REQUESTS):
        other_rows = pl.multiple_of(request * DRAFT + (1 - core) * HALF, HALF)
        swaps.append(
            (
                residual_hbm.at[pl.ds(other_rows, HALF), :],
                residual.at[core, pl.ds(request * HALF, HALF), :],
            )
        )
    for slot in range(8):
        place = vocab.at[core, :, pl.ds(slot * 512, 512)]
        swaps.append((place, place))
    swap_copies = [
        pltpu.make_async_remote_copy(
            src,
            dst,
            swap_sems.at[0, k],
            swap_sems.at[1, k],
            device_id={"seq": partner},
            device_id_type=MESH,
        )
        for k, (src, dst) in enumerate(swaps)
    ]

    @pl.loop(0, REQUESTS)
    def _(b):
        @pl.when(b == 1)
        def _():
            for copy in got_cache[1]:
                copy.wait()

        tree = jnp.concatenate([tree_bias[b]] * HEADS, axis=0)
        drafted = nt_dot(qbuf[b], dbuf[...]) + tree
        top = jnp.max(drafted, -1, keepdims=True)
        scores = []
        for columns in KEY_PARTS:
            live_bias = jnp.where(position[:, columns] < lengths[b], 0.0, NEGATIVE)
            scores.append(dot(qbuf[b], kbuf[b, :, columns]) + live_bias)
            top = jnp.maximum(top, jnp.max(scores[-1], -1, keepdims=True))
        drafted = jnp.exp2((drafted - top) * scale)
        total = jnp.sum(drafted, -1, keepdims=True)
        mixed = dot(drafted.astype(BF16), dbuf[:, 0:LATENT])
        for columns, cached in zip(KEY_PARTS, scores):
            cached = jnp.exp2((cached - top) * scale)
            total = total + jnp.sum(cached, -1, keepdims=True)
            mixed = mixed + nt_dot(cached.astype(BF16), kbuf[b, 0:LATENT, columns])
        mixed = mixed.astype(BF16)
        tops = jnp.zeros((DRAFT, 128), F32)
        totals = jnp.zeros((DRAFT, 128), F32)
        for h in range(HEADS):
            sub = slice(h * DRAFT, (h + 1) * DRAFT)
            o_send[b, h] = dot(mixed[sub], value_weight[h]).astype(BF16)
            tops = jnp.where(lane == h, top[sub] * scale, tops)
            totals = jnp.where(lane == h, total[sub], totals)
        turned = jnp.concatenate([tops, totals], axis=0).T
        for h in range(HEADS):
            ml_send[b, h] = turned[h : h + 1]

        @pl.when(b == 0)
        def _():
            pl.semaphore_wait(barrier, 30)

        for j in range(15):
            o_copy(b, j).start()
            ml_copy(b, j).start()
        for k in range(2):
            own_copy(b, k).start()

        @pl.when(b == 0)
        def _():
            got_out.wait()
            got_gain.wait()
            gain_rows[core] = gain[...].astype(F32)[None, :]
            for copy in got_vocab:
                copy.wait()
            for copy in swap_copies:
                copy.start()

    o_copies = [o_copy(b, j) for b in range(REQUESTS) for j in range(15)]
    ml_copies = [ml_copy(b, j) for b in range(REQUESTS) for j in range(15)]
    own_copies = [own_copy(b, k) for b in range(REQUESTS) for k in range(2)]

    g_copies = []
    for b in range(REQUESTS):
        for copy in ml_copies[b * 15 : (b + 1) * 15]:
            copy.wait_recv()
        for copy in own_copies[b * 2 : (b + 1) * 2]:
            copy.wait()
        gathered = jnp.concatenate(
            [ml_recv[b, j] for j in range(16)] + [jnp.full((112, 128), NEGATIVE, F32)], axis=0
        ).T
        tops, totals = gathered[:DRAFT], gathered[DRAFT:]
        shares = jnp.exp2(tops - jnp.max(tops, -1, keepdims=True))
        shares = shares / jnp.sum(shares * totals, -1, keepdims=True)
        shares = jnp.where(core == 0, shares[:32], shares[32:])
        for copy in o_copies[b * 15 : (b + 1) * 15]:
            copy.wait_recv()
        summed = jnp.zeros((32, 128), F32)
        for j in range(16):
            summed = summed + shares[:, j : j + 1] * o_recv[b, j].astype(F32)
        g_send[b] = summed.astype(BF16)
        place = g_full.at[b, :, pl.ds(pl.multiple_of(chip * 128, 128), 128)]
        for j, peer in enumerate(chip_peers):
            copy = pltpu.make_async_remote_copy(
                g_send.at[b],
                place,
                g_sems.at[0, b, j],
                g_sems.at[1, b, j],
                device_id={"seq": peer},
                device_id_type=MESH,
            )
            copy.start()
            g_copies.append(copy)
        copy = pltpu.make_async_copy(g_send.at[b], place, local_sems.at[b, 2])
        copy.start()
        own_copies.append(copy)

    a_copies, b_copies = [], []
    for b in range(REQUESTS):
        own_copies[4 + b].wait()
        if b == 0:
            swap_copies[0].wait_recv()
        for copy in g_copies[b * 7 : (b + 1) * 7]:
            copy.wait_recv()
        for side in range(2):
            attention = nt_dot(g_full[b], out_weight[side])
            for i in range(8):
                a_send[b, 2 * i + side] = attention[i * 4 : (i + 1) * 4].astype(BF16)
        for j, peer in enumerate(head_peers):
            copy = pltpu.make_async_remote_copy(
                a_send.at[b, peer],
                a_recv.at[b, j],
                a_sems.at[0, b, j],
                a_sems.at[1, b, j],
                device_id={"head": peer},
                device_id_type=MESH,
            )
            copy.start()
            a_copies.append(copy)
    for b in range(REQUESTS):
        summed = a_send[b, mine].astype(F32)
        for j in range(15):
            a_copies[b * 15 + j].wait_recv()
            summed = summed + a_recv[b, j].astype(F32)
        b_send[b] = summed.astype(BF16)
        for j, peer in enumerate(head_peers):
            copy = pltpu.make_async_remote_copy(
                b_send.at[b],
                b_full.at[b, mine],
                b_sems.at[0, b, j],
                b_sems.at[1, b, j],
                device_id={"head": peer},
                device_id_type=MESH,
            )
            copy.start()
            b_copies.append(copy)
        b_full[b, mine] = b_send[b]

    for copy in got_residual:
        copy.wait()
    for copy in swap_copies[1:4]:
        copy.wait_recv()
    square_parts, l_copies = [], []
    for b in range(REQUESTS):
        for copy in b_copies[b * 15 : (b + 1) * 15]:
            copy.wait_recv()
        squares = jnp.zeros((HALF, 1), F32)
        scaled = []
        for side in range(2):
            attention = jnp.concatenate(
                [b_full[b, 2 * i + side].astype(F32) for i in range(8)], axis=0
            )
            hidden = residual[side, b * HALF : (b + 1) * HALF].astype(F32) + attention
            squares = squares + jnp.sum(hidden * hidden, -1, keepdims=True)
            scaled.append((hidden * gain_rows[side]).astype(BF16))
        square_parts.append(squares)
        if b == 1:
            squares = jnp.concatenate(square_parts * 2, axis=0)
            s_send[...] = jnp.broadcast_to(squares, (TOKENS, 128)).T[0:1]
            s_copies = []
            for j, peer in enumerate(seq_peers):
                copy = pltpu.make_async_remote_copy(
                    s_send,
                    s_recv.at[j],
                    s_sems.at[0, j],
                    s_sems.at[1, j],
                    device_id={"seq": peer},
                    device_id_type=MESH,
                )
                copy.start()
                s_copies.append(copy)
        chips = 4
        for slot in range(8):
            if b == 0:
                swap_copies[4 + slot].wait_recv()
        for group in range(0, 8, chips):
            columns = slice(group * 512, (group + chips) * 512)
            part = dot(scaled[0], vocab[0, :, columns]) + dot(scaled[1], vocab[1, :, columns])
            part = part.astype(BF16)
            for k in range(2 * chips):
                l_send[b, group + k // 2, k % 2] = part[:, k * 256 : (k + 1) * 256]
            for j in range(2 * group, min(2 * (group + chips), 15)):
                slot, dk = (7, 1) if j == 14 else (j // 2, j % 2)
                copy = pltpu.make_async_remote_copy(
                    l_send.at[b, slot, lax.rem(core + dk, 2)],
                    l_recv.at[b, j],
                    l_sems.at[0, b, j],
                    l_sems.at[1, b, j],
                    device_id={"seq": seq_peers[j]},
                    device_id_type=MESH,
                )
                copy.start()
                l_copies.append(copy)
    squares = [s_send[...], jnp.zeros((1, TOKENS), F32)]
    for j, (_, _, dk) in enumerate(SEQ_STEPS):
        s_copies[j].wait_recv()
        squares[dk] = squares[dk] + s_recv[j]
    scales = [
        jnp.broadcast_to(lax.rsqrt(total / model_width + EPSILON), (128, TOKENS)).T
        for total in squares
    ]
    for b in range(REQUESTS):
        sums = [l_send[b, 7, core].astype(F32), jnp.zeros((HALF, 256), F32)]
        for j, (_, _, dk) in enumerate(SEQ_STEPS):
            l_copies[b * 15 + j].wait_recv()
            sums[dk] = sums[dk] + l_recv[b, j].astype(F32)
        for dk in range(2):
            owner = lax.rem(core + dk, 2)
            rows = pl.ds(pl.multiple_of(b * DRAFT + owner * HALF, HALF), HALF)
            logits[rows, :] = (sums[dk] * scales[dk][b * HALF : (b + 1) * HALF, 0:1]).astype(BF16)
    for copy in o_copies + ml_copies + swap_copies + g_copies + a_copies + b_copies + s_copies + l_copies:
        copy.wait_send()


def per_device(
    latent_cache,
    draft_latent,
    query_nope,
    query_rope,
    parents,
    lengths,
    key_weight,
    value_weight,
    out_weight,
    residual,
    norm_gain,
    vocab_weight,
):
    local_width = residual.shape[2]
    model_width = local_width * lax.axis_size("seq")
    operands = [
        lengths,
        parents,
        jnp.swapaxes(latent_cache, 1, 2),
        draft_latent,
        query_nope.reshape(TOKENS * HEADS, 128),
        query_rope.reshape(TOKENS * HEADS, ROPE),
        key_weight,
        value_weight,
        out_weight.T,
        residual.reshape(TOKENS, local_width),
        norm_gain,
        vocab_weight,
    ]
    hbm = pl.BlockSpec(memory_space=pltpu.HBM)
    dma = pltpu.SemaphoreType.DMA
    logits = pl.pallas_call(
        functools.partial(kernel, model_width),
        out_shape=jax.ShapeDtypeStruct((TOKENS, 256), BF16),
        in_specs=[hbm] * 12,
        out_specs=pl.BlockSpec(memory_space=pltpu.VMEM),
        scratch_shapes=[
            pltpu.SMEM((REQUESTS,), jnp.int32),
            pltpu.VMEM((REQUESTS, DRAFT), jnp.int32),
            pltpu.VMEM((REQUESTS, WIDTH, KEYS), BF16),
            pltpu.VMEM((REQUESTS, 4, WIDTH), BF16),
            pltpu.VMEM((EXTRA, WIDTH), BF16),
            pltpu.VMEM((REQUESTS, DRAFT, EXTRA), F32),
            pltpu.VMEM((TOKENS * HEADS, 128), BF16),
            pltpu.VMEM((TOKENS * HEADS, ROPE), BF16),
            pltpu.VMEM((HEADS, 128, LATENT), BF16),
            pltpu.VMEM((HEADS, LATENT, 128), BF16),
            pltpu.VMEM((2, local_width, 1024), BF16),
            pltpu.VMEM((2, 2 * HALF, local_width), BF16),
            pltpu.VMEM((local_width,), BF16),
            pltpu.VMEM((2, 1, local_width), F32),
            pltpu.VMEM((2, local_width, 4096), BF16),
            pltpu.VMEM((TOKENS * HEADS, 128), F32),
            pltpu.VMEM((TOKENS * HEADS, ROPE), F32),
            pltpu.VMEM((REQUESTS, HEADS * DRAFT, WIDTH), BF16),
            pltpu.VMEM((REQUESTS, HEADS, DRAFT, 128), BF16),
            pltpu.VMEM((REQUESTS, 16, 32, 128), BF16),
            pltpu.VMEM((REQUESTS, HEADS, 1, 128), F32),
            pltpu.VMEM((REQUESTS, 16, 1, 128), F32),
            pltpu.VMEM((REQUESTS, 32, 128), BF16),
            pltpu.VMEM((REQUESTS, HALF, 1024), BF16),
            pltpu.VMEM((REQUESTS, 16, 4, local_width), BF16),
            pltpu.VMEM((REQUESTS, 15, 4, local_width), BF16),
            pltpu.VMEM((REQUESTS, 4, local_width), BF16),
            pltpu.VMEM((REQUESTS, 16, 4, local_width), BF16),
            pltpu.VMEM((1, TOKENS), F32),
            pltpu.VMEM((15, 1, TOKENS), F32),
            pltpu.VMEM((REQUESTS, 8, 2, HALF, 256), BF16),
            pltpu.VMEM((REQUESTS, 15, HALF, 256), BF16),
            dma((20,)),
            dma((8,)),
            dma((REQUESTS, 3)),
            dma((2, REQUESTS, 15)),
            dma((2, REQUESTS, 15)),
            dma((2, REQUESTS, 7)),
            dma((2, REQUESTS, 15)),
            dma((2, REQUESTS, 15)),
            dma((2, 15)),
            dma((2, 12)),
            dma((2, REQUESTS, 15)),
        ],
        compiler_params=pltpu.CompilerParams(
            collective_id=0, has_side_effects=True, vmem_limit_bytes=48 * 1024 * 1024
        ),
    )(
        *[pltpu.with_memory_space_constraint(a, pltpu.HBM) for a in operands],
    )
    return logits.reshape(REQUESTS, DRAFT, 256)


def solution(mesh):
    in_specs = (
        P(None, "seq", None),
        P(None, "seq", None),
        P(None, None, "head", None),
        P(None, None, "head", None),
        P(),
        P(),
        P("head", None, None),
        P("head", None, None),
        P("head", "seq"),
        P(None, None, "seq"),
        P("seq"),
        P("seq", "head"),
    )
    out_specs = P(None, None, ("head", "seq"))
    return jax.shard_map(
        per_device, mesh=mesh, in_specs=in_specs, out_specs=out_specs, check_vma=False
    )
```
